128 devices in a mesh: gx: 16 (over z, y), gy: 8 (over x, core).
Axes of the slice: x: 4, y: 4, z: 4, core: 2. Of those that a mesh axis runs over, the one named last changes fastest.
Arguments:
- velocity: float32 [3, 16, 2048, 2048], P(None, None, 'gx', 'gy'), may hold values from -6 to 6
- metric_x: float32 [2048], replicated, may hold values from 0.5 to 2
- metric_y: float32 [2048], replicated, may hold values from 0.5 to 2
- marker_force: float32 [3, 262144], P(None, ('gx', 'gy')), may hold values from -24 to 24
- marker_frac: float32 [3, 262144], P(None, ('gx', 'gy')), may hold values from 0 to 1
- marker_cell_x: int32 [262144], P(('gx', 'gy')), may hold values from 0 to 127
- marker_cell_y: int32 [262144], P(('gx', 'gy')), may hold values from 0 to 255
- marker_cell_z: int32 [262144], P(('gx', 'gy')), may hold values from 0 to 15
- send_counts: int32 [128, 128], P(('gx', 'gy')), may hold values from 0 to 32, as said below
Outputs:
- ddx: float32 [3, 16, 2048, 2048], P(None, None, 'gx', 'gy')
- ddy: float32 [3, 16, 2048, 2048], P(None, None, 'gx', 'gy')
The draws below stay inside these ranges and needn't reach their ends.
Inputs may be any that keep to these rules, and one draw needn't show every extreme that they name: `send_counts`: row s lists, block by block in gx+gy order, how many of source device s's markers each grid block owns; the markers of a device come in that block order; each row sums to 2048; in every draw some block owns 32 markers of every source device.
All inputs are finite; a program needn't handle non-finite values.
Results may differ from the reference program's by a relative error of at most 0.00035.
Values sent between devices are 32-bit elements; how exact they have to be, the bound alone decides.
A program may use at most 640 MiB of HBM per device.

```python
import math
import jax
import jax.numpy as jnp

NX = 2048
NY = 2048
Z = 16
CAP = 32
CX = 128
CY = 256
M_DEV = 2048
MARKERS = 262144
N_GX = 16
N_GY = 8


def draw_send_counts(key, part):
    devices = N_GX * N_GY
    pairs = devices // 2
    half = CAP // 2
    keys = jax.random.split(key, 5)
    heavy = jax.random.randint(keys[0], (1, pairs), 0, 4) == 0
    leaning = 2 * jax.random.randint(keys[1], (1, pairs), 0, 2) - 1
    lean = leaning * jax.random.randint(keys[2], (devices, pairs), half // 2, half + 1)
    loose = jax.random.randint(keys[3], (devices, pairs), -half, half + 1)
    tilt = jnp.where(heavy, lean, loose)
    filled = jax.random.randint(keys[4], (), 0, pairs)
    tilt = jnp.where(jnp.arange(pairs)[None, :] == filled, half, tilt)
    counts = jnp.stack((half + tilt, half - tilt), axis=2).reshape(devices, devices)
    return counts.astype(jnp.int32)


def place_ends(values, rng, low, top_value):
    longest = values.shape.index(max(values.shape))
    spots = []
    for shift in (0, 1):
        where = [jax.random.randint(jax.random.fold_in(rng, axis), (), 0, length) for axis, length in enumerate(values.shape)]
        where[longest] = (where[longest] + shift) % values.shape[longest]
        spots.append(tuple(where))
    return values.at[spots[0]].set(low).at[spots[1]].set(top_value)


def block_scale(stream_key, dims, pieces, least, high):
    loudness, own = 1.0, jax.random.fold_in(stream_key, 6)
    for position, blocks in pieces:
        heights = jnp.exp(jax.random.uniform(jax.random.fold_in(own, position), (blocks,), jnp.float32, least / len(pieces), high / len(pieces)))
        loudness = loudness * jnp.repeat(heights, dims[position] // blocks).reshape([-1 if axis == position else 1 for axis in range(len(dims))])
    return loudness


def noise(own_key, extent, deviation, limit, cuts=(), kind=jnp.bfloat16):
    factor_of = block_scale(own_key, extent, cuts, -0.22, 0.18) if cuts else 1.0
    values = jax.random.normal(own_key, extent, jnp.float32) * deviation * factor_of
    return jnp.minimum(jnp.maximum(values, -limit), limit).astype(kind)


def setup_inputs(seed: int = 0) -> dict:
    arg_keys = jax.random.split(jax.random.key(seed), 10)
    return {
        "velocity": noise(arg_keys[0], (3, Z, NX, NY), 1.0, 6.0, ((2, 16), (3, 8)), jnp.float32),
        "metric_x": jnp.clip(jnp.exp(jax.random.uniform(arg_keys[1], (NX,), jnp.float32, math.log(0.5), math.log(2.0))), 0.5, 2.0),
        "metric_y": jnp.clip(jnp.exp(jax.random.uniform(arg_keys[2], (NY,), jnp.float32, math.log(0.5), math.log(2.0))), 0.5, 2.0),
        "marker_force": noise(arg_keys[3], (3, MARKERS), 4.0, 24.0, ((1, 128),), jnp.float32),
        "marker_frac": jnp.clip(1.0 * jax.random.uniform(arg_keys[4], (3, MARKERS), jnp.float32) ** block_scale(arg_keys[4], (3, MARKERS), ((1, 128),), -0.2, 0.2), 0.0, 1.0),
        "marker_cell_x": place_ends(jax.random.randint(arg_keys[5], (MARKERS,), 0, CX), jax.random.fold_in(arg_keys[5], 1), 0, CX - 1).astype(jnp.int32),
        "marker_cell_y": place_ends(jax.random.randint(arg_keys[6], (MARKERS,), 0, CY), jax.random.fold_in(arg_keys[6], 1), 0, CY - 1).astype(jnp.int32),
        "marker_cell_z": place_ends(jax.random.randint(arg_keys[7], (MARKERS,), 0, Z), jax.random.fold_in(arg_keys[7], 1), 0, Z - 1).astype(jnp.int32),
        "send_counts": draw_send_counts(jax.random.fold_in(arg_keys[9], 71), 0),
    }


section_weight = 0.5

def kernel_weights(frac):
    root = jnp.sqrt(1.0 + 4.0 * frac - 4.0 * frac * frac)
    return ((3.0 - 2.0 * frac - root) / 8.0, (3.0 - 2.0 * frac + root) / 8.0, (1.0 + 2.0 * frac + root) / 8.0, (1.0 + 2.0 * frac - root) / 8.0)

def compact_along(field, axis, length, metric):
    wave = 2.0 * math.pi * jnp.arange(length // 2 + 1, dtype=jnp.float32) / length
    factor = (14.0 / 9.0 * jnp.sin(wave) + 1.0 / 18.0 * jnp.sin(2.0 * wave)) / (1.0 + 2.0 / 3.0 * jnp.cos(wave))
    layout = [1] * field.ndim
    layout[axis] = length // 2 + 1
    spectrum = jnp.fft.rfft(field, axis=axis)
    result = jnp.fft.irfft(spectrum * (1j * factor.reshape(layout)), n=length, axis=axis).astype(jnp.float32)
    stretch = [1] * field.ndim
    stretch[axis] = length
    return result * metric.reshape(stretch)

def reference(velocity, metric_x, metric_y, marker_force, marker_frac, marker_cell_x, marker_cell_y, marker_cell_z, send_counts):
    totals = jnp.cumsum(send_counts, axis=1).astype(jnp.int32)
    local = jnp.arange(M_DEV, dtype=jnp.int32)
    owner = jax.vmap(lambda row: jnp.searchsorted(row, local, side='right'))(totals).astype(jnp.int32).reshape(-1)
    cell_x = (owner // N_GY * CX + marker_cell_x).astype(jnp.int32)
    cell_y = (owner % N_GY * CY + marker_cell_y).astype(jnp.int32)
    cell_z = marker_cell_z.astype(jnp.int32)
    weight_x = kernel_weights(marker_frac[0])
    weight_y = kernel_weights(marker_frac[1])
    weight_z = kernel_weights(marker_frac[2])
    density = jnp.zeros((3, Z, NX, NY), jnp.float32)
    for step_x in range(4):
        index_x = (cell_x - 1 + step_x) % NX
        for step_y in range(4):
            index_y = (cell_y - 1 + step_y) % NY
            for step_z in range(4):
                index_z = (cell_z - 1 + step_z) % Z
                weight = weight_x[step_x] * weight_y[step_y] * weight_z[step_z]
                density = density.at[:, index_z, index_x, index_y].add(marker_force * weight[None, :])
    density = density * metric_x[None, None, :, None] * metric_y[None, None, None, :]
    forced = velocity + section_weight * density
    ddx = compact_along(forced, 2, NX, metric_x)
    ddy = compact_along(forced, 3, NY, metric_y)
    return (ddx, ddy)
```

```python
import functools
import math

import jax
import jax.numpy as jnp
import numpy as np
from jax import lax
from jax.experimental import pallas as pl
from jax.experimental.pallas import tpu as pltpu
from jax.sharding import PartitionSpec as P

SLOTS = 32
HALF = 0.5
GROUP = 42
BASES = 39
OFF = 8
XEXT = 144
ZEXT = 19
TILES = 7
COPIES = 2
ROOT = (math.sqrt(5.0) - 3.0) / 2.0
MESH = pl.DeviceIdType.MESH
VMEM = pltpu.VMEM
F32 = jnp.float32
BF16 = jnp.bfloat16


SCALE = 1.0 / (1.0 + 2.0 * ROOT / 3.0)
LEAD = SCALE * (7.0 / 9.0 * (1.0 / ROOT - ROOT) + 1.0 / 36.0 * (1.0 / ROOT**2 - ROOT**2))
NEAR = SCALE / 36.0 * (ROOT - 1.0 / ROOT)


def line_matrix(n):
    gap = np.arange(n)[None, :] - np.arange(n)[:, None]
    out = np.sign(gap) * LEAD * ROOT ** np.abs(gap).astype(np.float64)
    return out + np.where(np.abs(gap) == 1, np.sign(gap) * NEAR, 0.0)


def halo_columns(n):
    out = np.zeros((n, 4))
    steps = np.arange(n)
    out[:, 0] = -LEAD * ROOT ** (steps + 1.0)
    out[0, 1] = -NEAR
    out[:, 2] = LEAD * ROOT ** (n - steps * 1.0)
    out[n - 1, 3] = NEAR
    return out


def halves(values):
    values = np.asarray(values, np.float32)
    high = values.astype(BF16)
    low = (values - high.astype(np.float32)).astype(BF16)
    return high, low


def split(x):
    high = x.astype(BF16)
    return high, (x - high.astype(F32)).astype(BF16)


def dot(a, b):
    return jnp.dot(a, b, preferred_element_type=F32)


def edge_weights(n, total):
    out = np.zeros((8, total))
    steps = np.arange(n)
    out[0, :n] = ROOT ** (n - 1.0 - steps)
    out[1, n - 1] = 1.0
    out[2, n] = 1.0
    out[3, n + 1] = 1.0
    out[4, :n] = ROOT ** (steps * 1.0)
    out[5, 0] = 1.0
    out[6, n + 2] = 1.0
    return out


def pack_kernel(counts_ref, table_ref, out_ref, wide):
    size = table_ref.shape[1]
    wide[:, 0:size] = table_ref[...]
    wide[:, size:] = jnp.zeros((8, wide.shape[1] - size), F32)
    lane = lax.broadcasted_iota(jnp.int32, (8, 128), 1)
    sub = lax.broadcasted_iota(jnp.int32, (8, 128), 0)
    part = sub & 3

    def one(d, start):
        count = counts_ref[0, d]
        first = pl.multiple_of((start >> 7) << 7, 128)
        shift = start & 127
        back = (128 - shift) & 127
        a = pltpu.roll(wide[:, pl.ds(first, 128)], back, 1)
        b = pltpu.roll(wide[:, pl.ds(first + 128, 128)], back, 1)
        w = jnp.where(lane + shift < 128, a, b)
        w = jnp.where(lane < count, w, 0.0)
        m = w
        for j in range(1, 4):
            m = jnp.where(part == j, pltpu.roll(w, SLOTS * j, 1), m)
        top = jnp.sum(jnp.where(sub < 4, m, 0.0), axis=0, keepdims=True)
        low = jnp.sum(jnp.where(sub < 4, 0.0, m), axis=0, keepdims=True)
        return start + count, top, low

    def eight(g, start):
        tops, lows = [], []
        for k in range(8):
            start, top, low = one(g * 8 + k, start)
            tops.append(top)
            lows.append(low)
        at = pl.multiple_of(g * 8, 8)
        out_ref[pl.ds(at, 8), 0:128] = jnp.concatenate(tops, axis=0)
        out_ref[pl.ds(at, 8), 128:256] = jnp.concatenate(lows, axis=0)
        return start

    lax.fori_loop(0, out_ref.shape[0] // 8, eight, jnp.int32(0))


def pack(counts, table):
    blocks = counts.shape[1]
    return pl.pallas_call(
        pack_kernel,
        out_shape=jax.ShapeDtypeStruct((blocks, 256), F32),
        in_specs=[pl.BlockSpec(memory_space=pltpu.SMEM), pl.BlockSpec(memory_space=VMEM)],
        out_specs=pl.BlockSpec(memory_space=VMEM),
        scratch_shapes=[VMEM((8, table.shape[1] + 256), F32)],
        name="pack",
    )(counts, table)


def spread_kernel(
    inbox_ref, mx_ref, my_ref, sel0_ref, sel1_ref, selr_ref, pick_ref, tail_ref, wfar_ref, wnear_ref, v_hbm,
    e_hbm, rl_ref, cn_ref, ud_ref,
    *scratch,
):
    grids = scratch[:COPIES]
    vbuf, m8, wz_v, base_v, wz_s, base_s, fcy, mxcol, rlp, udp, v_sem, e_sems, s_sems = scratch[COPIES:]
    sources = inbox_ref.shape[0]
    total = sources * SLOTS
    chunks = total // 128
    vin = pltpu.make_async_copy(v_hbm, vbuf, v_sem)
    vin.start()
    lane = lax.broadcasted_iota(jnp.int32, (8, 128), 1)
    sub = lax.broadcasted_iota(jnp.int32, (8, 128), 0)

    def regroup(pair, carry):
        rows = inbox_ref[pl.ds(pl.multiple_of(pair * 8, 8), 8), :]
        four(pair * 2, rows[0:4])
        four(pair * 2 + 1, rows[4:8])
        return carry

    def four(g, rows):
        out = None
        for k in range(4):
            row = rows[k : k + 1]
            x = jnp.where(
                sub < 4, jnp.broadcast_to(row[:, 0:128], (8, 128)), jnp.broadcast_to(row[:, 128:256], (8, 128))
            )
            y = x
            for j in range(4):
                turn = (SLOTS * (k - j)) % 128
                z = pltpu.roll(x, turn, 1) if turn else x
                y = jnp.where((sub & 3) == j, z, y)
            out = y if out is None else jnp.where((lane >> 5) == k, y, out)
        at = pl.multiple_of(g * 128, 128)
        m8[:, pl.ds(at, 128)] = out
        root = jnp.sqrt(jnp.maximum(1.0 + 4.0 * out - 4.0 * out * out, 0.0))
        frac = out
        ws = (
            (3.0 - 2.0 * frac - root) / 8.0,
            (3.0 - 2.0 * frac + root) / 8.0,
            (1.0 + 2.0 * frac + root) / 8.0,
            (1.0 + 2.0 * frac - root) / 8.0,
        )
        wz_v[:, pl.ds(at, 128)] = jnp.concatenate([w[5:6] for w in ws] + [jnp.zeros((4, 128), F32)], axis=0)
        code = out[6:7].astype(jnp.int32)
        cell_z = code & 15
        cell_y = (code >> 4) & 255
        cell_x = code >> 12
        tile = (cell_y * 1681) >> 16
        base = (tile * ZEXT + cell_z) * XEXT + cell_x + (OFF - 1)
        base_v[:, pl.ds(at, 128)] = jnp.broadcast_to(base, (8, 128))

    lax.fori_loop(0, chunks // 2, regroup, 0)
    c1 = pltpu.make_async_copy(wz_v, wz_s, s_sems.at[0])
    c2 = pltpu.make_async_copy(base_v, base_s, s_sems.at[1])
    c1.start()
    c2.start()

    rows = grids[0].shape[0]
    step = 152

    def clear(i, carry):
        for grid in grids:
            grid[pl.ds(pl.multiple_of(i * step, 8), step), :] = jnp.zeros((step, 128), F32)
        return carry

    lax.fori_loop(0, rows // step, clear, 0)
    c1.wait()
    c2.wait()

    lane2 = lax.broadcasted_iota(jnp.int32, (128, 128), 1)
    comp = jnp.where(lane2 >= 2 * GROUP, 2, jnp.where(lane2 >= GROUP, 1, 0))
    rel = jnp.where(lane2 >= 3 * GROUP, -100, lane2 - GROUP * comp).astype(F32)

    def chunk(c, carry):
        at = pl.multiple_of(c * 128, 128)
        m = m8[:, pl.ds(at, 128)]
        root = jnp.sqrt(jnp.maximum(1.0 + 4.0 * m - 4.0 * m * m, 0.0))
        ws = (
            (3.0 - 2.0 * m - root) / 8.0,
            (3.0 - 2.0 * m + root) / 8.0,
            (1.0 + 2.0 * m + root) / 8.0,
            (1.0 + 2.0 * m - root) / 8.0,
        )
        code = m[6:7].astype(jnp.int32)
        cell_y = (code >> 4) & 255
        tile = (cell_y * 1681) >> 16
        inner = (cell_y - BASES * tile).astype(F32)
        block = jnp.concatenate([m[0:3], inner] + [w[4:5] for w in ws] + [jnp.zeros((120, 128), F32)], axis=0)
        cols = jnp.transpose(block)
        col = lambda i: jnp.broadcast_to(cols[:, i : i + 1], (128, 128))
        d = rel - col(3)
        w = jnp.where(d == 0.0, col(4), 0.0)
        w = jnp.where(d == 1.0, col(5), w)
        w = jnp.where(d == 2.0, col(6), w)
        w = jnp.where(d == 3.0, col(7), w)
        f = jnp.where(comp == 0, col(0), jnp.where(comp == 1, col(1), col(2)))
        fcy[...] = w * f
        wx = jnp.concatenate([w[3:4] for w in ws] + [jnp.zeros((4, 128), F32)], axis=0)

        def eight(g, wx):
            for k0 in range(0, 8, COPIES):
                loads = []
                for k in range(k0, k0 + COPIES):
                    idx = c * 128 + g * 8 + k
                    b = base_s[0, idx]
                    p = wx[:, k : k + 1] * fcy[pl.ds(g * 8 + k, 1), :]
                    grid = grids[k % COPIES]
                    loads.append(
                        [
                            (grid, b + dz * XEXT, grid[pl.ds(b + dz * XEXT, 8), :] + wz_s[dz, idx] * p)
                            for dz in range(4)
                        ]
                    )
                for group in loads:
                    for grid, at, value in group:
                        grid[pl.ds(at, 8), :] = value
            return pltpu.roll(wx, 120, 1)

        lax.fori_loop(0, 16, eight, wx)
        return carry

    lax.fori_loop(0, chunks, chunk, 0)

    for t in range(TILES):
        for src, dst in ((0, 16), (17, 1), (18, 2)):
            i, j = (t * ZEXT + src) * XEXT, (t * ZEXT + dst) * XEXT
            moved = grids[0][i : i + XEXT, :]
            for grid in grids[1:]:
                moved = moved + grid[i : i + XEXT, :]
            grids[0][j : j + XEXT, :] += moved

    mrow = mx_ref[0:1, :]
    mxcol[0:128, :] = jnp.transpose(jnp.broadcast_to(mrow[:, 0:128], (128, 128)))
    mxcol[128:144, :] = jnp.transpose(jnp.broadcast_to(mrow[:, 128:256], (128, 128)))[0:16]
    vin.wait()

    def plane(z, carry):
        highs, lows = [], []
        for t in range(TILES):
            at = pl.multiple_of((t * ZEXT + z + 1) * XEXT, 8)
            x = grids[0][pl.ds(at, XEXT), :]
            for grid in grids[1:]:
                x = x + grid[pl.ds(at, XEXT), :]
            high, low = split(x)
            highs.append(high)
            lows.append(low)
        outs = []
        for tiles, sel in (((0, 1, 2, 3), sel0_ref), ((3, 4, 5, 6), sel1_ref), ((0, 6), selr_ref)):
            high = jnp.concatenate([highs[t] for t in tiles], axis=1)
            low = jnp.concatenate([lows[t] for t in tiles], axis=1)
            outs.append(dot(high, sel[...]) + dot(low, sel[...]))
        mcol = mxcol[...]
        far, near = wfar_ref[...], wnear_ref[...]
        for c in range(3):
            p = c * 16 + z
            ext = []
            for h in range(3):
                e = outs[h][:, c * 128 : (c + 1) * 128] * mcol * my_ref[0:1, h * 128 : (h + 1) * 128]
                if h < 2:
                    inner = e[OFF : OFF + 128] + vbuf[c, z, :, h * 128 : (h + 1) * 128]
                    vbuf[c, z, :, h * 128 : (h + 1) * 128] = inner
                    e = jnp.concatenate([e[0:OFF], inner, e[OFF + 128 :]], axis=0)
                ext.append(e)
                rowset = [
                    jnp.sum(e * far, axis=0, keepdims=True),
                    e[OFF + 127 : OFF + 130],
                    jnp.sum(e * near, axis=0, keepdims=True),
                    e[OFF : OFF + 1],
                    e[OFF - 1 : OFF],
                    jnp.zeros((1, 128), F32),
                ]
                rlp[h, pl.ds(pl.multiple_of(p * 8, 8), 8), :] = jnp.concatenate(rowset, axis=0)
            high, low = split(jnp.concatenate([e[OFF : OFF + 128] for e in ext], axis=1))
            nt = (((1,), (1,)), ((), ()))
            one = lax.dot_general(pick_ref[...], high, nt, preferred_element_type=F32)
            two = lax.dot_general(pick_ref[...], low, nt, preferred_element_type=F32)
            udp[pl.ds(pl.multiple_of(p * 8, 8), 8), :] = one[0:8] + one[8:16] + two[0:8]
        pltpu.make_async_copy(vbuf.at[:, z], e_hbm.at[:, z], e_sems.at[z]).start()
        return carry

    lax.fori_loop(0, 16, plane, 0)

    corner = jnp.zeros((48, 128), F32)
    for t in range(7):
        row = jnp.concatenate([rlp[h, pl.ds(t, 48, stride=8), :] for h in range(3)], axis=1)
        rl_ref[t] = row[:, 0:256]
        ends = jnp.dot(row, tail_ref[...], preferred_element_type=F32, precision=lax.Precision.HIGHEST)
        corner = corner + (pltpu.roll(ends, 8 * t, 1) if t else ends)
        ud_ref[t] = udp[pl.ds(t, 48, stride=8), :]
    rl_ref[7] = jnp.zeros((48, 256), F32)
    ud_ref[7] = jnp.zeros((48, 128), F32)
    cn_ref[...] = corner
    for z in range(16):
        pltpu.make_async_copy(vbuf.at[:, z], e_hbm.at[:, z], e_sems.at[z]).wait()


def selectors():
    pick = {}
    for name, tiles, first in (("a", (0, 1, 2, 3), 0), ("b", (3, 4, 5, 6), 128)):
        out = np.zeros((4 * 128, 3 * 128), np.float32)
        for i, t in enumerate(tiles):
            for c in range(3):
                for j in range(GROUP):
                    y = BASES * t - 1 + j - first
                    if 0 <= y < 128:
                        out[i * 128 + c * GROUP + j, c * 128 + y] = 1.0
        pick[name] = out.astype(BF16)
    out = np.zeros((2 * 128, 3 * 128), np.float32)
    for i, t in enumerate((0, 6)):
        for c in range(3):
            for j in range(GROUP):
                y = BASES * t - 1 + j
                spot = {256: 0, 257: 1, -1: 2}.get(y)
                if spot is not None:
                    out[i * 128 + c * GROUP + j, c * 128 + spot] = 1.0
    return pick["a"], pick["b"], out.astype(BF16)


def spread(inbox, mx, my, v):
    sel0, sel1, selr = selectors()
    ends = edge_weights(256, 384)
    high, low = halves(ends)
    pick = np.concatenate([high, low], axis=0)
    tail = np.zeros((384, 128), np.float32)
    tail[:, 0:8] = ends.T
    weights = edge_weights(128, 144)
    far = np.zeros((XEXT, 128), np.float32)
    near = np.zeros((XEXT, 128), np.float32)
    far[OFF : OFF + 128] = weights[0, 0:128, None]
    near[OFF : OFF + 128] = weights[4, 0:128, None]
    rows = TILES * ZEXT * XEXT
    total = inbox.shape[0] * SLOTS
    vm = pl.BlockSpec(memory_space=VMEM)
    return pl.pallas_call(
        spread_kernel,
        out_shape=(
            jax.ShapeDtypeStruct(v.shape, F32),
            jax.ShapeDtypeStruct((8, 48, 256), F32),
            jax.ShapeDtypeStruct((48, 128), F32),
            jax.ShapeDtypeStruct((8, 48, 128), F32),
        ),
        in_specs=[vm] * 10 + [pl.BlockSpec(memory_space=pl.ANY)],
        out_specs=(pl.BlockSpec(memory_space=pl.ANY), vm, vm, vm),
        scratch_shapes=[VMEM((rows, 128), F32)] * COPIES
        + [
            VMEM(v.shape, F32),
            VMEM((8, total), F32),
            VMEM((8, total), F32),
            VMEM((8, total), jnp.int32),
            pltpu.SMEM((8, total), F32),
            pltpu.SMEM((8, total), jnp.int32),
            VMEM((128, 128), F32),
            VMEM((XEXT, 128), F32),
            VMEM((3, 48 * 8, 128), F32),
            VMEM((48 * 8, 128), F32),
            pltpu.SemaphoreType.DMA,
            pltpu.SemaphoreType.DMA((16,)),
            pltpu.SemaphoreType.DMA((2,)),
        ],
        compiler_params=pltpu.CompilerParams(vmem_limit_bytes=56 << 20),
        name="spread",
    )(inbox, mx, my, sel0, sel1, selr, pick, tail, far, near, v)


def exchange_kernel(
    rl_ref, cn_ref, ud_ref, xh_ref, yh_ref, ra, ca, rb, cb, umsg, hmsg, pu, ph, qd, qh, send_sems, recv_sems
):
    gx, gy = lax.axis_index("gx"), lax.axis_index("gy")
    nx, ny = lax.axis_size("gx"), lax.axis_size("gy")
    right = (lax.rem(gx + 1, nx), gy)
    left = (lax.rem(gx + nx - 1, nx), gy)
    up = (gx, lax.rem(gy + 1, ny))
    down = (gx, lax.rem(gy + ny - 1, ny))
    barrier = pltpu.get_barrier_semaphore()
    for device in (right, left, up, down):
        pl.semaphore_signal(barrier, inc=1, device_id=device, device_id_type=MESH)
    pl.semaphore_wait(barrier, 4)

    def send(i, src, dst, device):
        copy = pltpu.make_async_remote_copy(
            src_ref=src, dst_ref=dst, send_sem=send_sems.at[i], recv_sem=recv_sems.at[i],
            device_id=device, device_id_type=MESH,
        )
        copy.start()
        return copy

    first = [
        send(0, cn_ref, ca, right),
        send(1, cn_ref, cb, left),
        send(2, rl_ref.at[0:4], ra, right),
        send(3, rl_ref.at[4:7], rb, left),
    ]
    planes = cn_ref.shape[0]
    lane = lax.broadcasted_iota(jnp.int32, (planes, 128), 1)
    first[0].wait()
    first[1].wait()
    own, a, b = cn_ref[...], ca[...], cb[...]
    turn = lambda x, by: pltpu.roll(x, by % 128, 1)
    hold = jnp.where(lane < 8, a + turn(own, -48), a + turn(own, -40))
    hold = jnp.where(
        lane < 16, hold, turn(b, -16) + jnp.where(lane < 24, own + ROOT * turn(own, -8), turn(own, 8))
    )
    hmsg[...] = jnp.where(lane < 32, hold, 0.0)
    for s in range(7):
        umsg[s] = (
            ud_ref[s]
            + jnp.where(lane == 0, a[:, 16 + s : 17 + s], 0.0)
            + jnp.where(lane == 1, a[:, 24 + s : 25 + s], 0.0)
            + jnp.where(lane == 127, b[:, 48 + s : 49 + s], 0.0)
        )
    second = [
        send(4, hmsg, ph, up),
        send(5, hmsg, qh, down),
        send(6, umsg.at[0:4], pu, up),
        send(7, umsg.at[4:7], qd, down),
    ]
    first[2].wait()
    first[3].wait()
    second[0].wait()
    second[1].wait()
    lane = lax.broadcasted_iota(jnp.int32, (planes, 256), 1)
    p, q = ph[...], qh[...]

    def rims(h):
        return (
            jnp.where(lane == 0, p[:, 8 * h + 2 : 8 * h + 3], 0.0)
            + jnp.where(lane == 1, p[:, 8 * h + 3 : 8 * h + 4], 0.0)
            + jnp.where(lane == 255, q[:, 8 * h + 6 : 8 * h + 7], 0.0)
        )

    def put(t, value):
        for h in range(2):
            xh_ref[h, pl.ds(t, planes, stride=8), :] = value[:, h * 128 : (h + 1) * 128]

    put(0, ra[0] + rl_ref[6] + rims(0))
    put(1, ra[1] + rl_ref[6] + rims(1))
    put(2, rb[0] + rl_ref[2] + ROOT * rl_ref[3] + rims(2))
    put(3, rb[1] + rl_ref[2] + rims(3))
    put(4, ra[2])
    put(5, ra[3])
    put(6, rb[2])
    put(7, jnp.zeros((planes, 256), F32))
    second[2].wait()
    second[3].wait()
    yh_ref[pl.ds(0, planes, stride=8), :] = pu[0] + umsg[6]
    yh_ref[pl.ds(1, planes, stride=8), :] = pu[1] + umsg[6]
    yh_ref[pl.ds(2, planes, stride=8), :] = qd[0] + umsg[2] + ROOT * umsg[3]
    yh_ref[pl.ds(3, planes, stride=8), :] = qd[1] + umsg[2]
    yh_ref[pl.ds(4, planes, stride=8), :] = pu[2]
    yh_ref[pl.ds(5, planes, stride=8), :] = pu[3]
    yh_ref[pl.ds(6, planes, stride=8), :] = qd[2]
    yh_ref[pl.ds(7, planes, stride=8), :] = jnp.zeros((planes, 128), F32)


def exchange(rl, cn, ud):
    n = cn.shape[0]
    vm = pl.BlockSpec(memory_space=VMEM)
    return pl.pallas_call(
        exchange_kernel,
        out_shape=(jax.ShapeDtypeStruct((2, 8 * n, 128), F32), jax.ShapeDtypeStruct((8 * n, 128), F32)),
        in_specs=[vm, vm, vm],
        out_specs=(vm, vm),
        scratch_shapes=[
            VMEM((4, n, 256), F32),
            VMEM((n, 128), F32),
            VMEM((3, n, 256), F32),
            VMEM((n, 128), F32),
            VMEM((7, n, 128), F32),
            VMEM((n, 128), F32),
            VMEM((4, n, 128), F32),
            VMEM((n, 128), F32),
            VMEM((3, n, 128), F32),
            VMEM((n, 128), F32),
            pltpu.SemaphoreType.DMA((8,)),
            pltpu.SemaphoreType.DMA((8,)),
        ],
        compiler_params=pltpu.CompilerParams(collective_id=0, has_side_effects=True),
        name="exchange",
    )(rl, cn, ud)


def derive_kernel(e_ref, xh_ref, yh_ref, mx_ref, my_ref, kx_ref, ky_ref, kl_ref, rim_ref, dx_ref, dy_ref, mxcol):
    step = pl.program_id(0)

    @pl.when(step == 0)
    def _():
        mxcol[...] = jnp.transpose(jnp.broadcast_to(mx_ref[0:1, :], (128, 128)))

    each = e_ref.shape[0]
    for i in range(each):
        xall = jnp.concatenate([xh_ref[0, i * 8 : i * 8 + 8, :], xh_ref[1, i * 8 : i * 8 + 8, :]], axis=1)
        yrow = yh_ref[i * 8 : i * 8 + 8, :]
        high = yrow.astype(BF16).astype(F32)
        lows = yrow - high
        stack = jnp.concatenate([high, lows, high, jnp.zeros((8, 128), F32)], axis=0).astype(BF16)
        extra = lax.dot_general(stack, rim_ref[...], (((0,), (0,)), ((), ())), preferred_element_type=F32)
        zero = jnp.zeros((1, 256), F32)
        top = jnp.concatenate([xall[4:6]] + [zero] * 6, axis=0)
        low = jnp.concatenate([zero] * 7 + [xall[6:7]], axis=0)
        e = e_ref[i]
        f = jnp.concatenate([e[0:8] + top, e[8:120], e[120:128] + low], axis=0) + extra[:, 256:512]
        halo = jnp.concatenate([xall[0:4]] + [zero] * 12, axis=0)
        fh, fl = split(f)
        hh, hl = split(halo)
        xh = jnp.concatenate([fh, hh], axis=0)
        xl = jnp.concatenate([fl, hl], axis=0)
        one = dot(kx_ref[...], xh)
        dx = one[0:128] + one[128:256] + dot(kx_ref[0:128], xl)
        col = mxcol[...]
        dx_ref[i, :, 0:128] = dx[:, 0:128] * col
        dx_ref[i, :, 128:256] = dx[:, 128:256] * col
        two = dot(jnp.concatenate([fh, fl], axis=0), ky_ref[...])
        dy = two[0:128] + two[128:256] + dot(fh, kl_ref[...]) + extra[:, 0:256]
        dy_ref[i] = dy * my_ref[0:1, :]


def derive(e, xh, yh, mx, my):
    n, rows, cols = e.shape
    each = 4
    kx = np.zeros((rows, 144))
    kx[:, 0:rows] = line_matrix(rows)
    kx[:, rows : rows + 4] = halo_columns(rows)
    kx = np.concatenate(halves(kx), axis=0)
    kh, kl = halves(line_matrix(cols).T)
    rim = np.zeros((8, 512))
    rim[0:4, 0:256] = halo_columns(cols).T
    rim[4, 256] = 1.0
    rim[5, 257] = 1.0
    rim[6, 511] = 1.0
    rh, rlow = halves(rim)
    rim = np.concatenate([rh, rh, rlow, np.zeros((8, 512), BF16)], axis=0)
    whole = lambda x: pl.BlockSpec(x.shape, lambda i: (0,) * x.ndim)
    block = pl.BlockSpec((each, rows, cols), lambda i: (i, 0, 0))
    consts = (kx, kh, kl, rim)
    return pl.pallas_call(
        derive_kernel,
        grid=(n // each,),
        out_shape=(jax.ShapeDtypeStruct(e.shape, F32),) * 2,
        in_specs=[block, pl.BlockSpec((2, each * 8, 128), lambda i: (0, i, 0)), pl.BlockSpec((each * 8, 128), lambda i: (i, 0))]
        + [whole(x) for x in (mx, my) + consts],
        out_specs=(block, block),
        scratch_shapes=[VMEM((128, 128), F32)],
        compiler_params=pltpu.CompilerParams(vmem_limit_bytes=48 << 20),
        name="derive",
    )(e, xh, yh, mx, my, *consts)


def metrics(metric_x, metric_y, gx, gy, rows, cols):
    nx, ny = metric_x.shape[0], metric_y.shape[0]
    long = jnp.concatenate([metric_x[nx - OFF :], metric_x, metric_x[: 256 - OFF]])
    mx = lax.dynamic_slice(long, (gx * rows,), (256,))
    here = lax.dynamic_slice(metric_x, (gx * rows,), (rows,))
    inner = lax.dynamic_slice(metric_y, (gy * cols,), (cols,))
    long = jnp.concatenate([metric_y[ny - 1 :], metric_y, metric_y[:2]])
    before = lax.dynamic_slice(long, (gy * cols,), (1,))
    after = lax.dynamic_slice(long, (gy * cols + cols + 1,), (2,))
    my = HALF * jnp.concatenate([inner, after, before, jnp.zeros((125,), F32)])
    wide = lambda x: jnp.broadcast_to(x[None, :], (8, x.shape[0]))
    return wide(mx), wide(my), wide(here), wide(inner)


def local(
    velocity, metric_x, metric_y, marker_force, marker_frac, marker_cell_x, marker_cell_y, marker_cell_z, send_counts
):
    comps, planes, rows, cols = velocity.shape
    gx, gy = lax.axis_index("gx"), lax.axis_index("gy")
    code = (marker_cell_x * cols + marker_cell_y) * planes + marker_cell_z
    code = code.astype(F32)[None, :]
    table = jnp.concatenate([marker_force, marker_frac, code, jnp.zeros_like(code)], axis=0)
    outbox = pack(send_counts, table)
    inbox = lax.all_to_all(outbox, ("gx", "gy"), split_axis=0, concat_axis=0, tiled=True)
    mx, my, here, inner = metrics(metric_x, metric_y, gx, gy, rows, cols)
    e, rl, cn, ud = spread(inbox, mx, my, velocity)
    xh, yh = exchange(rl, cn, ud)
    dx, dy = derive(e.reshape(comps * planes, rows, cols), xh, yh, here, inner)
    return dx.reshape(velocity.shape), dy.reshape(velocity.shape)


def solution(mesh):
    both = ("gx", "gy")
    placed = (
        P(None, None, "gx", "gy"), P(), P(), P(None, both), P(None, both), P(both), P(both), P(both), P(both, None),
    )
    return jax.shard_map(
        local,
        mesh=mesh,
        in_specs=placed,
        out_specs=(P(None, None, "gx", "gy"), P(None, None, "gx", "gy")),
        check_vma=False,
    )
```

```python
import functools
import math

import jax
import jax.numpy as jnp
import numpy as np
from jax import lax
from jax.experimental import pallas as pl
from jax.experimental.pallas import tpu as pltpu
from jax.sharding import PartitionSpec as P

SLOTS = 32
HALF = 0.5
GROUP = 42
BASES = 39
OFF = 8
XEXT = 144
PAIRS = 10
EACH = 8
TILES = 7
COPIES = 2
ROOT = (math.sqrt(5.0) - 3.0) / 2.0
MESH = pl.DeviceIdType.MESH
VMEM = pltpu.VMEM
F32 = jnp.float32
BF16 = jnp.bfloat16


SCALE = 1.0 / (1.0 + 2.0 * ROOT / 3.0)
LEAD = SCALE * (7.0 / 9.0 * (1.0 / ROOT - ROOT) + 1.0 / 36.0 * (1.0 / ROOT**2 - ROOT**2))
NEAR = SCALE / 36.0 * (ROOT - 1.0 / ROOT)


def line_matrix(n):
    gap = np.arange(n)[None, :] - np.arange(n)[:, None]
    out = np.sign(gap) * LEAD * ROOT ** np.abs(gap).astype(np.float64)
    return out + np.where(np.abs(gap) == 1, np.sign(gap) * NEAR, 0.0)


def halo_columns(n):
    out = np.zeros((n, 4))
    steps = np.arange(n)
    out[:, 0] = -LEAD * ROOT ** (steps + 1.0)
    out[0, 1] = -NEAR
    out[:, 2] = LEAD * ROOT ** (n - steps * 1.0)
    out[n - 1, 3] = NEAR
    return out


def halves(values):
    values = np.asarray(values, np.float32)
    high = values.astype(BF16)
    low = (values - high.astype(np.float32)).astype(BF16)
    return high, low


def split(x):
    high = x.astype(BF16)
    return high, (x - high.astype(F32)).astype(BF16)


def dot(a, b):
    return jnp.dot(a, b, preferred_element_type=F32)


def edge_weights(n, total):
    out = np.zeros((8, total))
    steps = np.arange(n)
    out[0, :n] = ROOT ** (n - 1.0 - steps)
    out[1, n - 1] = 1.0
    out[2, n] = 1.0
    out[3, n + 1] = 1.0
    out[4, :n] = ROOT ** (steps * 1.0)
    out[5, 0] = 1.0
    out[6, n + 2] = 1.0
    return out


def pack_kernel(counts_ref, force_ref, frac_ref, cx_ref, cy_ref, cz_ref, out_ref, wide):
    size = force_ref.shape[1]
    wide[0:3, 0:size] = force_ref[...]
    wide[3:6, 0:size] = frac_ref[...]
    code = ((cx_ref[...] * 256 + cy_ref[...]) * 16 + cz_ref[...]).astype(F32)
    for i in range(size // 128):
        wide[6:7, i * 128 : (i + 1) * 128] = code[i : i + 1]
    wide[7:8, 0:size] = jnp.zeros((1, size), F32)
    wide[:, size:] = jnp.zeros((8, wide.shape[1] - size), F32)
    lane = lax.broadcasted_iota(jnp.int32, (8, 128), 1)
    sub = lax.broadcasted_iota(jnp.int32, (8, 128), 0)
    part = sub & 3

    def one(d, start):
        count = counts_ref[0, d]
        first = pl.multiple_of((start >> 7) << 7, 128)
        shift = start & 127
        back = (128 - shift) & 127
        a = pltpu.roll(wide[:, pl.ds(first, 128)], back, 1)
        b = pltpu.roll(wide[:, pl.ds(first + 128, 128)], back, 1)
        w = jnp.where(lane + shift < 128, a, b)
        w = jnp.where(lane < count, w, 0.0)
        m = w
        for j in range(1, 4):
            m = jnp.where(part == j, pltpu.roll(w, SLOTS * j, 1), m)
        top = jnp.sum(jnp.where(sub < 4, m, 0.0), axis=0, keepdims=True)
        low = jnp.sum(jnp.where(sub < 4, 0.0, m), axis=0, keepdims=True)
        return start + count, jnp.concatenate([top, low], axis=1)

    def eight(g, start):
        for k in range(8):
            start, out_ref[k, g] = one(g * 8 + k, start)
        return start

    lax.fori_loop(0, out_ref.shape[1], eight, jnp.int32(0))


def pack(counts, *fields):
    vm = pl.BlockSpec(memory_space=VMEM)
    return pl.pallas_call(
        pack_kernel,
        out_shape=jax.ShapeDtypeStruct((8, counts.shape[1] // 8, 1, 256), F32),
        in_specs=[pl.BlockSpec(memory_space=pltpu.SMEM)] + [vm] * 5,
        out_specs=vm,
        scratch_shapes=[VMEM((8, fields[0].shape[1] + 256), F32)],
        name="pack",
    )(counts, *fields)


def shuffle_kernel(out_ref, in_ref, mid, own_sems, send_y, recv_y, send_x, recv_x):
    gx, gy = lax.axis_index("gx"), lax.axis_index("gy")
    nx, ny = lax.axis_size("gx"), lax.axis_size("gy")
    own = pltpu.make_async_copy(out_ref.at[gy], mid.at[gy], own_sems.at[0])
    own.start()
    barrier = pltpu.get_barrier_semaphore()
    for k in range(1, ny):
        pl.semaphore_signal(barrier, inc=1, device_id=(gx, lax.rem(gy + k, ny)), device_id_type=MESH)
    for k in range(1, nx):
        pl.semaphore_signal(barrier, inc=1, device_id=(lax.rem(gx + k, nx), gy), device_id_type=MESH)
    pl.semaphore_wait(barrier, nx + ny - 2)
    copies = []
    for k in range(1, ny):
        peer = lax.rem(gy + k, ny)
        copy = pltpu.make_async_remote_copy(
            src_ref=out_ref.at[peer], dst_ref=mid.at[gy], send_sem=send_y.at[k], recv_sem=recv_y.at[k],
            device_id=(gx, peer), device_id_type=MESH,
        )
        copy.start()
        copies.append(copy)
    own.wait()
    for copy in copies:
        copy.wait()
    own = pltpu.make_async_copy(mid.at[:, gx], in_ref.at[gx], own_sems.at[1])
    own.start()
    copies = []
    for k in range(1, nx):
        peer = lax.rem(gx + k, nx)
        copy = pltpu.make_async_remote_copy(
            src_ref=mid.at[:, peer], dst_ref=in_ref.at[gx], send_sem=send_x.at[k], recv_sem=recv_x.at[k],
            device_id=(peer, gy), device_id_type=MESH,
        )
        copy.start()
        copies.append(copy)
    own.wait()
    for copy in copies:
        copy.wait()


def shuffle(outbox):
    ny, nx = outbox.shape[0:2]
    anywhere = pl.BlockSpec(memory_space=pl.ANY)
    dma = pltpu.SemaphoreType.DMA
    return pl.pallas_call(
        shuffle_kernel,
        out_shape=jax.ShapeDtypeStruct((nx, ny, 1, 256), F32),
        in_specs=[anywhere],
        out_specs=anywhere,
        scratch_shapes=[VMEM((ny, nx, 1, 256), F32), dma((2,)), dma((ny,)), dma((ny,)), dma((nx,)), dma((nx,))],
        compiler_params=pltpu.CompilerParams(collective_id=1, has_side_effects=True),
        name="shuffle",
    )(outbox)


def row_as_column(row):
    return jnp.transpose(jnp.broadcast_to(row, (128, 128)))


def stencil_weights(t):
    root = jnp.sqrt(jnp.maximum(1.0 + 4.0 * t - 4.0 * t * t, 0.0))
    return (
        (3.0 - 2.0 * t - root) / 8.0,
        (3.0 - 2.0 * t + root) / 8.0,
        (1.0 + 2.0 * t + root) / 8.0,
        (1.0 + 2.0 * t - root) / 8.0,
    )


def spread_kernel(
    inbox_ref, mx_ref, my_ref, pick_ref, tail_ref, wfar_ref, wnear_ref, v_hbm,
    e_hbm, rl_ref, cn_ref, ud_ref,
    *scratch,
):
    grids = scratch[:COPIES]
    vbuf, m8, base_v, base_s, fcy, mxcol, ext, rlp, udp, v_sem, e_sems, s_sem = scratch[COPIES:]
    gx, gy = lax.axis_index("gx"), lax.axis_index("gy")
    chunks = inbox_ref.shape[0] * SLOTS // 128
    vin = pltpu.make_async_copy(v_hbm, vbuf, v_sem)
    vin.start()
    lane = lax.broadcasted_iota(jnp.int32, (8, 128), 1)
    sub = lax.broadcasted_iota(jnp.int32, (8, 128), 0)

    def regroup(g, carry):
        out = None
        for k in range(4):
            row = inbox_ref[g * 4 + k]
            x = jnp.where(
                sub < 4, jnp.broadcast_to(row[:, 0:128], (8, 128)), jnp.broadcast_to(row[:, 128:256], (8, 128))
            )
            y = x
            for j in range(4):
                turn = (SLOTS * (k - j)) % 128
                z = pltpu.roll(x, turn, 1) if turn else x
                y = jnp.where((sub & 3) == j, z, y)
            out = y if out is None else jnp.where((lane >> 5) == k, y, out)
        at = pl.multiple_of(g * 128, 128)
        m8[:, pl.ds(at, 128)] = out
        code = out[6:7].astype(jnp.int32)
        tile = (((code >> 4) & 255) * 1681) >> 16
        base_v[:, pl.ds(at, 128)] = (tile * PAIRS + ((code & 15) >> 1)) * (2 * XEXT) + 2 * ((code >> 12) + OFF - 1)
        return carry

    lax.fori_loop(0, chunks, regroup, 0)
    bcopy = pltpu.make_async_copy(base_v, base_s, s_sem)
    bcopy.start()
    rows = grids[0].shape[0]
    step = 160

    def clear(i, carry):
        for grid in grids:
            grid[pl.ds(pl.multiple_of(i * step, 8), step), :] = jnp.zeros((step, 128), F32)
        return carry

    lax.fori_loop(0, rows // step, clear, 0)
    bcopy.wait()

    sub2 = lax.broadcasted_iota(jnp.int32, (128, 128), 0)
    comp = jnp.where(sub2 >= 2 * GROUP, 2, jnp.where(sub2 >= GROUP, 1, 0))
    rel = jnp.where(sub2 >= 3 * GROUP, -100, sub2 - GROUP * comp)

    def chunk(c, carry):
        m = m8[:, pl.ds(pl.multiple_of(c * 128, 128), 128)]
        ws = stencil_weights(m)
        code = m[6:7].astype(jnp.int32)
        cell_y = (code >> 4) & 255
        inner = cell_y - BASES * ((cell_y * 1681) >> 16)
        d = rel - inner
        w = jnp.where(d == 0, ws[0][4:5], 0.0)
        w = jnp.where(d == 1, ws[1][4:5], w)
        w = jnp.where(d == 2, ws[2][4:5], w)
        w = jnp.where(d == 3, ws[3][4:5], w)
        f = jnp.where(comp == 0, m[0:1], jnp.where(comp == 1, m[1:2], m[2:3]))
        fcy[...] = jnp.transpose(w * f)
        odd = (code & 1) == 1
        wx = [w[3:4] for w in ws]
        wz = [w[5:6] for w in ws]
        none = jnp.zeros((1, 128), F32)
        sides = (
            (jnp.where(odd, none, wz[0]), jnp.where(odd, wz[0], wz[1])),
            (jnp.where(odd, wz[1], wz[2]), jnp.where(odd, wz[2], wz[3])),
            (jnp.where(odd, wz[3], none), none),
        )
        wx8 = jnp.concatenate([wx[i // 2] for i in range(8)], axis=0)
        tall = [wx8 * jnp.concatenate(list(side) * 4, axis=0) for side in sides]
        fr = fcy[...]
        bs = [base_s[0, c * 128 + k] for k in range(128)]
        for k0 in range(0, 128, COPIES):
            group = []
            for k in range(k0, k0 + COPIES):
                grid = grids[k % COPIES]
                for q in range(3):
                    at = bs[k] + q * (2 * XEXT)
                    group.append((grid, at, grid[pl.ds(at, 8), :] + tall[q][:, k : k + 1] * fr[k : k + 1, :]))
            for grid, at, value in group:
                grid[pl.ds(at, 8), :] = value
        return carry

    lax.fori_loop(0, chunks, chunk, 0)

    def first_row(t, e):
        return (t * PAIRS + (e >> 1)) * (2 * XEXT) + (e & 1)

    for t in range(TILES):
        for src, dst in ((0, 16), (17, 1), (18, 2)):
            moved = None
            for grid in grids:
                x = grid[pl.ds(first_row(t, src), XEXT, stride=2), :]
                moved = x if moved is None else moved + x
            here = pl.ds(first_row(t, dst), XEXT, stride=2)
            grids[0][here, :] = grids[0][here, :] + moved

    nx, ny = mx_ref.shape[0], my_ref.shape[0]
    mxcol[0:OFF, :] = row_as_column(mx_ref[pl.ds(lax.rem(gx + nx - 1, nx), 1), :])[128 - OFF : 128]
    mxcol[OFF : OFF + 128, :] = row_as_column(mx_ref[pl.ds(gx, 1), :])
    mxcol[OFF + 128 : XEXT, :] = row_as_column(mx_ref[pl.ds(lax.rem(gx + 1, nx), 1), :])[0 : XEXT - OFF - 128]
    after = my_ref[pl.ds(lax.rem(2 * gy + 2, ny), 1), :]
    before = pltpu.roll(jnp.broadcast_to(my_ref[pl.ds(lax.rem(2 * gy + ny - 1, ny), 1), :], (8, 128)), 3, 1)[0:1]
    lane1 = lax.broadcasted_iota(jnp.int32, (1, 128), 1)
    rim = jnp.where(lane1 < 2, after, jnp.where(lane1 == 2, before, 0.0))
    mys = [HALF * my_ref[pl.ds(2 * gy, 1), :], HALF * my_ref[pl.ds(2 * gy + 1, 1), :], HALF * rim]
    vin.wait()

    part = 48
    lanes = lax.broadcasted_iota(jnp.int32, (part, 128), 1)

    def moves(c, h):
        out = []
        if h == 2:
            out.append((6, (-(GROUP * c + 256 - (6 * BASES - 1))) % 128, 0, 2))
            out.append((0, (2 - GROUP * c) % 128, 2, 3))
            return out
        for t in range(TILES):
            low, high = BASES * t - 1 - 128 * h, BASES * t - 1 + GROUP - 128 * h
            if high > 0 and low < 128:
                out.append((t, (low - GROUP * c) % 128, max(low, 0), min(high, 128)))
        return out

    def plane(z, carry):
        far = [[jnp.zeros((8, 128), F32)] * 3 for _ in range(3)]
        near = [[jnp.zeros((8, 128), F32)] * 3 for _ in range(3)]
        for r0 in range(0, XEXT, part):
            tiles = []
            for t in range(TILES):
                x = None
                for grid in grids:
                    y = grid[pl.ds(first_row(t, z + 1) + 2 * r0, part, stride=2), :]
                    x = y if x is None else x + y
                tiles.append(x)
            mcol = mxcol[r0 : r0 + part, :]
            wf, wn = wfar_ref[r0 : r0 + part, :], wnear_ref[r0 : r0 + part, :]
            r1 = r0 + part
            i0, i1 = max(r0, OFF), min(r1, OFF + 128)
            for c in range(3):
                for h in range(3):
                    e = None
                    for t, turn, low, high in moves(c, h):
                        x = pltpu.roll(tiles[t], turn, 1) if turn else tiles[t]
                        if low > 0 or high < 128:
                            x = jnp.where((lanes >= low) & (lanes < high), x, 0.0)
                        e = x if e is None else e + x
                    e = e * mcol * mys[h]
                    if h < 2:
                        cols = slice(h * 128, (h + 1) * 128)
                        inner = e[i0 - r0 : i1 - r0] + vbuf[c, z, i0 - OFF : i1 - OFF, cols]
                        vbuf[c, z, i0 - OFF : i1 - OFF, cols] = inner
                        pieces = [e[0 : i0 - r0]] if i0 > r0 else []
                        pieces.append(inner)
                        if i1 < r1:
                            pieces.append(e[i1 - r0 :])
                        e = jnp.concatenate(pieces, axis=0) if len(pieces) > 1 else inner
                    ext[c, h, r0:r1, :] = e
                    far[c][h] = far[c][h] + jnp.sum((e * wf).reshape(part // 8, 8, 128), axis=0)
                    near[c][h] = near[c][h] + jnp.sum((e * wn).reshape(part // 8, 8, 128), axis=0)
        for c in range(3):
            p = c * 16 + z
            at = pl.multiple_of(p * 8, 8)
            for h in range(3):
                rowset = [
                    jnp.sum(far[c][h], axis=0, keepdims=True),
                    ext[c, h, OFF + 127 : OFF + 130, :],
                    jnp.sum(near[c][h], axis=0, keepdims=True),
                    ext[c, h, OFF : OFF + 1, :],
                    ext[c, h, OFF - 1 : OFF, :],
                    jnp.zeros((1, 128), F32),
                ]
                rlp[h, pl.ds(at, 8), :] = jnp.concatenate(rowset, axis=0)
            high, low = split(jnp.concatenate([ext[c, h, OFF : OFF + 128, :] for h in range(3)], axis=1))
            nt = (((1,), (1,)), ((), ()))
            one = lax.dot_general(pick_ref[...], high, nt, preferred_element_type=F32)
            two = lax.dot_general(pick_ref[...], low, nt, preferred_element_type=F32)
            udp[pl.ds(at, 8), :] = one[0:8] + one[8:16] + two[0:8]
        pltpu.make_async_copy(vbuf.at[:, z], e_hbm.at[:, z], e_sems.at[z]).start()
        return carry

    lax.fori_loop(0, 16, plane, 0)

    corner = jnp.zeros((48, 128), F32)
    for t in range(7):
        row = jnp.concatenate([rlp[h, pl.ds(t, 48, stride=8), :] for h in range(3)], axis=1)
        rl_ref[t] = row[:, 0:256]
        ends = jnp.dot(row, tail_ref[...], preferred_element_type=F32, precision=lax.Precision.HIGHEST)
        corner = corner + (pltpu.roll(ends, 8 * t, 1) if t else ends)
        ud_ref[t] = udp[pl.ds(t, 48, stride=8), :]
    rl_ref[7] = jnp.zeros((48, 256), F32)
    ud_ref[7] = jnp.zeros((48, 128), F32)
    cn_ref[...] = corner
    for z in range(16):
        pltpu.make_async_copy(vbuf.at[:, z], e_hbm.at[:, z], e_sems.at[z]).wait()


def spread(inbox, mx, my, v):
    ends = edge_weights(256, 384)
    high, low = halves(ends)
    pick = np.concatenate([high, low], axis=0)
    tail = np.zeros((384, 128), np.float32)
    tail[:, 0:8] = ends.T
    weights = edge_weights(128, 144)
    far = np.zeros((XEXT, 128), np.float32)
    near = np.zeros((XEXT, 128), np.float32)
    far[OFF : OFF + 128] = weights[0, 0:128, None]
    near[OFF : OFF + 128] = weights[4, 0:128, None]
    rows = TILES * PAIRS * 2 * XEXT
    total = inbox.shape[0] * SLOTS
    vm = pl.BlockSpec(memory_space=VMEM)
    return pl.pallas_call(
        spread_kernel,
        out_shape=(
            jax.ShapeDtypeStruct(v.shape, F32),
            jax.ShapeDtypeStruct((8, 48, 256), F32),
            jax.ShapeDtypeStruct((48, 128), F32),
            jax.ShapeDtypeStruct((8, 48, 128), F32),
        ),
        in_specs=[vm] * 7 + [pl.BlockSpec(memory_space=pl.ANY)],
        out_specs=(pl.BlockSpec(memory_space=pl.ANY), vm, vm, vm),
        scratch_shapes=[VMEM((rows, 128), F32)] * COPIES
        + [
            VMEM(v.shape, F32),
            VMEM((8, total), F32),
            VMEM((1, total), jnp.int32),
            pltpu.SMEM((1, total), jnp.int32),
            VMEM((128, 128), F32),
            VMEM((XEXT, 128), F32),
            VMEM((3, 3, XEXT, 128), F32),
            VMEM((3, 48 * 8, 128), F32),
            VMEM((48 * 8, 128), F32),
            pltpu.SemaphoreType.DMA,
            pltpu.SemaphoreType.DMA((16,)),
            pltpu.SemaphoreType.DMA,
        ],
        compiler_params=pltpu.CompilerParams(vmem_limit_bytes=60 << 20),
        name="spread",
    )(inbox, mx, my, pick, tail, far, near, v)


def exchange_kernel(
    rl_hbm, cn_hbm, ud_hbm, xh_ref, yh_ref, rl_ref, cn_ref, ud_ref,
    ra, ca, rb, cb, umsg, hmsg, pu, ph, qd, qh, own_sems, send_sems, recv_sems,
):
    pairs = ((cn_hbm, cn_ref), (ud_hbm, ud_ref), (rl_hbm, rl_ref))
    loads = [pltpu.make_async_copy(src, dst, own_sems.at[i]) for i, (src, dst) in enumerate(pairs)]
    for load in loads:
        load.start()
    gx, gy = lax.axis_index("gx"), lax.axis_index("gy")
    nx, ny = lax.axis_size("gx"), lax.axis_size("gy")
    right = (lax.rem(gx + 1, nx), gy)
    left = (lax.rem(gx + nx - 1, nx), gy)
    up = (gx, lax.rem(gy + 1, ny))
    down = (gx, lax.rem(gy + ny - 1, ny))
    barrier = pltpu.get_barrier_semaphore()
    for device in (right, left, up, down):
        pl.semaphore_signal(barrier, inc=1, device_id=device, device_id_type=MESH)
    pl.semaphore_wait(barrier, 4)

    def send(i, src, dst, device):
        copy = pltpu.make_async_remote_copy(
            src_ref=src, dst_ref=dst, send_sem=send_sems.at[i], recv_sem=recv_sems.at[i],
            device_id=device, device_id_type=MESH,
        )
        copy.start()
        return copy

    first = [
        send(0, cn_hbm, ca, right),
        send(1, cn_hbm, cb, left),
        send(2, rl_hbm.at[0:4], ra, right),
        send(3, rl_hbm.at[4:7], rb, left),
    ]
    planes = cn_ref.shape[0]
    lane = lax.broadcasted_iota(jnp.int32, (planes, 128), 1)
    for load in loads:
        load.wait()
    first[0].wait()
    first[1].wait()
    own, a, b = cn_ref[...], ca[...], cb[...]
    turn = lambda x, by: pltpu.roll(x, by % 128, 1)
    hold = jnp.where(lane < 8, a + turn(own, -48), a + turn(own, -40))
    hold = jnp.where(
        lane < 16, hold, turn(b, -16) + jnp.where(lane < 24, own + ROOT * turn(own, -8), turn(own, 8))
    )
    hmsg[...] = jnp.where(lane < 32, hold, 0.0)
    for s in range(7):
        umsg[s] = (
            ud_ref[s]
            + jnp.where(lane == 0, a[:, 16 + s : 17 + s], 0.0)
            + jnp.where(lane == 1, a[:, 24 + s : 25 + s], 0.0)
            + jnp.where(lane == 127, b[:, 48 + s : 49 + s], 0.0)
        )
    second = [
        send(4, hmsg, ph, up),
        send(5, hmsg, qh, down),
        send(6, umsg.at[0:4], pu, up),
        send(7, umsg.at[4:7], qd, down),
    ]
    first[2].wait()
    first[3].wait()
    second[0].wait()
    second[1].wait()
    lane = lax.broadcasted_iota(jnp.int32, (planes, 256), 1)
    p, q = ph[...], qh[...]

    def rims(h):
        return (
            jnp.where(lane == 0, p[:, 8 * h + 2 : 8 * h + 3], 0.0)
            + jnp.where(lane == 1, p[:, 8 * h + 3 : 8 * h + 4], 0.0)
            + jnp.where(lane == 255, q[:, 8 * h + 6 : 8 * h + 7], 0.0)
        )

    def put(t, value):
        for h in range(2):
            xh_ref[h, pl.ds(t, planes, stride=8), :] = value[:, h * 128 : (h + 1) * 128]

    put(0, ra[0] + rl_ref[6] + rims(0))
    put(1, ra[1] + rl_ref[6] + rims(1))
    put(2, rb[0] + rl_ref[2] + ROOT * rl_ref[3] + rims(2))
    put(3, rb[1] + rl_ref[2] + rims(3))
    put(4, ra[2])
    put(5, ra[3])
    put(6, rb[2])
    put(7, jnp.zeros((planes, 256), F32))
    second[2].wait()
    second[3].wait()
    yh_ref[pl.ds(0, planes, stride=8), :] = pu[0] + umsg[6]
    yh_ref[pl.ds(1, planes, stride=8), :] = pu[1] + umsg[6]
    yh_ref[pl.ds(2, planes, stride=8), :] = qd[0] + umsg[2] + ROOT * umsg[3]
    yh_ref[pl.ds(3, planes, stride=8), :] = qd[1] + umsg[2]
    yh_ref[pl.ds(4, planes, stride=8), :] = pu[2]
    yh_ref[pl.ds(5, planes, stride=8), :] = pu[3]
    yh_ref[pl.ds(6, planes, stride=8), :] = qd[2]
    yh_ref[pl.ds(7, planes, stride=8), :] = jnp.zeros((planes, 128), F32)


def exchange(rl, cn, ud):
    n = cn.shape[0]
    vm = pl.BlockSpec(memory_space=VMEM)
    return pl.pallas_call(
        exchange_kernel,
        out_shape=(jax.ShapeDtypeStruct((2, 8 * n, 128), F32), jax.ShapeDtypeStruct((8 * n, 128), F32)),
        in_specs=[pl.BlockSpec(memory_space=pl.ANY)] * 3,
        out_specs=(vm, vm),
        scratch_shapes=[
            VMEM((8, n, 256), F32),
            VMEM((n, 128), F32),
            VMEM((8, n, 128), F32),
            VMEM((4, n, 256), F32),
            VMEM((n, 128), F32),
            VMEM((3, n, 256), F32),
            VMEM((n, 128), F32),
            VMEM((7, n, 128), F32),
            VMEM((n, 128), F32),
            VMEM((4, n, 128), F32),
            VMEM((n, 128), F32),
            VMEM((3, n, 128), F32),
            VMEM((n, 128), F32),
            pltpu.SemaphoreType.DMA((3,)),
            pltpu.SemaphoreType.DMA((8,)),
            pltpu.SemaphoreType.DMA((8,)),
        ],
        compiler_params=pltpu.CompilerParams(collective_id=0, has_side_effects=True),
        name="exchange",
    )(rl, cn, ud)


def derive_kernel(e_ref, xh_ref, yh_ref, mx_ref, my_ref, kx_ref, ky_ref, kl_ref, rim_ref, dx_ref, dy_ref, mxcol, myrow):
    @pl.when(pl.program_id(0) == 0)
    def _():
        gx, gy = lax.axis_index("gx"), lax.axis_index("gy")
        mxcol[...] = row_as_column(mx_ref[pl.ds(gx, 1), :])
        myrow[:, 0:128] = jnp.broadcast_to(my_ref[pl.ds(2 * gy, 1), :], (8, 128))
        myrow[:, 128:256] = jnp.broadcast_to(my_ref[pl.ds(2 * gy + 1, 1), :], (8, 128))

    each = e_ref.shape[0]
    zero = jnp.zeros((1, 256), F32)
    col = mxcol[...]
    yall = jnp.concatenate([yh_ref[i * 8 : i * 8 + 8, :] for i in range(each)], axis=1)
    high = yall.astype(BF16).astype(F32)
    stack = jnp.concatenate([high, yall - high, high, jnp.zeros_like(high)], axis=0).astype(BF16)
    extra = lax.dot_general(stack, rim_ref[...], (((0,), (0,)), ((), ())), preferred_element_type=F32)
    highs, lows = [], []
    for i in range(each):
        xall = jnp.concatenate([xh_ref[0, i * 8 : i * 8 + 8, :], xh_ref[1, i * 8 : i * 8 + 8, :]], axis=1)
        top = jnp.concatenate([xall[4:6]] + [zero] * 6, axis=0)
        low = jnp.concatenate([zero] * 7 + [xall[6:7]], axis=0)
        e = e_ref[i]
        f = jnp.concatenate([e[0:8] + top, e[8:120], e[120:128] + low], axis=0)
        f = f + extra[i * 128 : (i + 1) * 128, 256:512]
        halo = jnp.concatenate([xall[0:4]] + [zero] * 12, axis=0)
        fh, fl = split(f)
        hh, hl = split(halo)
        highs.append(fh)
        lows.append(fl)
        one = dot(kx_ref[...], jnp.concatenate([fh, hh], axis=0))
        dx = one[0:128] + one[128:256] + dot(kx_ref[0:128], jnp.concatenate([fl, hl], axis=0))
        dx_ref[i, :, 0:128] = dx[:, 0:128] * col
        dx_ref[i, :, 128:256] = dx[:, 128:256] * col
    two = dot(jnp.concatenate(highs + lows, axis=0), ky_ref[...])
    n = each * 128
    dy = two[0:n] + two[n : 2 * n] + dot(jnp.concatenate(highs, axis=0), kl_ref[...]) + extra[:, 0:256]
    dy_ref[...] = (dy * myrow[0:1, :]).reshape(dy_ref.shape)


def derive(e, xh, yh, mx, my):
    n, rows, cols = e.shape
    each = EACH
    kx = np.zeros((rows, 144))
    kx[:, 0:rows] = line_matrix(rows)
    kx[:, rows : rows + 4] = halo_columns(rows)
    kx = np.concatenate(halves(kx), axis=0)
    kh, kl = halves(line_matrix(cols).T)
    rim = np.zeros((8, 512))
    rim[0:4, 0:256] = halo_columns(cols).T
    rim[4, 256] = 1.0
    rim[5, 257] = 1.0
    rim[6, 511] = 1.0
    rh, rlow = halves(rim)
    rim = np.concatenate([rh, rh, rlow, np.zeros((8, 512), BF16)], axis=0)
    whole = lambda x: pl.BlockSpec(x.shape, lambda i: (0,) * x.ndim)
    block = pl.BlockSpec((each, rows, cols), lambda i: (i, 0, 0))
    consts = (kx, kh, kl, rim)
    xspec = pl.BlockSpec((2, each * 8, 128), lambda i: (0, i, 0))
    yspec = pl.BlockSpec((each * 8, 128), lambda i: (i, 0))
    return pl.pallas_call(
        derive_kernel,
        grid=(n // each,),
        out_shape=(jax.ShapeDtypeStruct(e.shape, F32),) * 2,
        in_specs=[block, xspec, yspec] + [whole(x) for x in (mx, my) + consts],
        out_specs=(block, block),
        scratch_shapes=[VMEM((128, 128), F32), VMEM((8, 256), F32)],
        compiler_params=pltpu.CompilerParams(vmem_limit_bytes=62 << 20),
        name="derive",
    )(e, xh, yh, mx, my, *consts)


def local(
    velocity, metric_x, metric_y, marker_force, marker_frac, marker_cell_x, marker_cell_y, marker_cell_z, send_counts
):
    comps, planes, rows, cols = velocity.shape
    fold = lambda x: x.reshape(-1, 128)
    cells = [fold(x) for x in (marker_cell_x, marker_cell_y, marker_cell_z)]
    outbox = pack(send_counts, marker_force, marker_frac, *cells)
    inbox = shuffle(outbox).reshape(-1, 1, 256)
    mx, my = fold(metric_x), fold(metric_y)
    e, rl, cn, ud = spread(inbox, mx, my, velocity)
    xh, yh = exchange(rl, cn, ud)
    dx, dy = derive(e.reshape(comps * planes, rows, cols), xh, yh, mx, my)
    return dx.reshape(velocity.shape), dy.reshape(velocity.shape)


def solution(mesh):
    both = ("gx", "gy")
    placed = (
        P(None, None, "gx", "gy"), P(), P(), P(None, both), P(None, both), P(both), P(both), P(both), P(both, None),
    )
    return jax.shard_map(
        local,
        mesh=mesh,
        in_specs=placed,
        out_specs=(P(None, None, "gx", "gy"), P(None, None, "gx", "gy")),
        check_vma=False,
    )
```

```python
import functools
import math

import jax
import jax.numpy as jnp
import numpy as np
from jax import lax
from jax.experimental import pallas as pl
from jax.experimental.pallas import tpu as pltpu
from jax.sharding import PartitionSpec as P

SLOTS = 32
HALF = 0.5
GROUP = 42
BASES = 39
OFF = 8
XEXT = 144
PAIRS = 9
SPAN = 2 * XEXT
EACH = 8
TILES = 7
COPIES = 2
ROOT = (math.sqrt(5.0) - 3.0) / 2.0
MESH = pl.DeviceIdType.MESH
VMEM = pltpu.VMEM
F32 = jnp.float32
BF16 = jnp.bfloat16


SCALE = 1.0 / (1.0 + 2.0 * ROOT / 3.0)
LEAD = SCALE * (7.0 / 9.0 * (1.0 / ROOT - ROOT) + 1.0 / 36.0 * (1.0 / ROOT**2 - ROOT**2))
NEAR = SCALE / 36.0 * (ROOT - 1.0 / ROOT)


def line_matrix(n):
    gap = np.arange(n)[None, :] - np.arange(n)[:, None]
    out = np.sign(gap) * LEAD * ROOT ** np.abs(gap).astype(np.float64)
    return out + np.where(np.abs(gap) == 1, np.sign(gap) * NEAR, 0.0)


def halo_columns(n):
    out = np.zeros((n, 4))
    steps = np.arange(n)
    out[:, 0] = -LEAD * ROOT ** (steps + 1.0)
    out[0, 1] = -NEAR
    out[:, 2] = LEAD * ROOT ** (n - steps * 1.0)
    out[n - 1, 3] = NEAR
    return out


def halves(values):
    values = np.asarray(values, np.float32)
    high = values.astype(BF16)
    low = (values - high.astype(np.float32)).astype(BF16)
    return high, low


def split(x):
    high = x.astype(BF16)
    return high, (x - high.astype(F32)).astype(BF16)


def dot(a, b):
    return jnp.dot(a, b, preferred_element_type=F32)


def cost(size):
    return pl.CostEstimate(flops=0, bytes_accessed=size, transcendentals=0)


def pack_kernel(counts_ref, force_ref, frac_ref, cx_ref, cy_ref, cz_ref, out_ref, wide):
    size = force_ref.shape[1]
    wide[0:3, 0:size] = force_ref[...]
    wide[3:6, 0:size] = frac_ref[...]
    code = ((cx_ref[...] * 256 + cy_ref[...]) * 16 + cz_ref[...]).astype(F32)
    for i in range(size // 128):
        wide[6:7, i * 128 : (i + 1) * 128] = code[i : i + 1]
    wide[7:8, 0:size] = jnp.zeros((1, size), F32)
    wide[:, size:] = jnp.zeros((8, wide.shape[1] - size), F32)
    lane = lax.broadcasted_iota(jnp.int32, (8, 128), 1)
    sub = lax.broadcasted_iota(jnp.int32, (8, 128), 0)
    part = sub & 3

    def one(d, start):
        count = counts_ref[0, d]
        first = pl.multiple_of((start >> 7) << 7, 128)
        shift = start & 127
        back = (128 - shift) & 127
        a = pltpu.roll(wide[:, pl.ds(first, 128)], back, 1)
        b = pltpu.roll(wide[:, pl.ds(first + 128, 128)], back, 1)
        w = jnp.where(lane + shift < 128, a, b)
        w = jnp.where(lane < count, w, 0.0)
        m = w
        for j in range(1, 4):
            m = jnp.where(part == j, pltpu.roll(w, SLOTS * j, 1), m)
        top = jnp.sum(jnp.where(sub < 4, m, 0.0), axis=0, keepdims=True)
        low = jnp.sum(jnp.where(sub < 4, 0.0, m), axis=0, keepdims=True)
        return start + count, jnp.concatenate([top, low], axis=1)

    def eight(g, start):
        for k in range(8):
            start, out_ref[k, g] = one(g * 8 + k, start)
        return start

    lax.fori_loop(0, out_ref.shape[1], eight, jnp.int32(0))


def pack(counts, *fields):
    vm = pl.BlockSpec(memory_space=VMEM)
    return pl.pallas_call(
        pack_kernel,
        out_shape=jax.ShapeDtypeStruct((8, counts.shape[1] // 8, 1, 256), F32),
        in_specs=[pl.BlockSpec(memory_space=pltpu.SMEM)] + [vm] * 5,
        out_specs=vm,
        scratch_shapes=[VMEM((8, fields[0].shape[1] + 256), F32)],
        cost_estimate=cost(12 << 20),
        name="pack",
    )(counts, *fields)


def shuffle_kernel(out_ref, in_ref, mid, own_sems, send_y, recv_y, send_x, recv_x):
    gx, gy = lax.axis_index("gx"), lax.axis_index("gy")
    nx, ny = lax.axis_size("gx"), lax.axis_size("gy")
    own = pltpu.make_async_copy(out_ref.at[gy], mid.at[gy], own_sems.at[0])
    own.start()
    barrier = pltpu.get_barrier_semaphore()
    for k in range(1, ny):
        pl.semaphore_signal(barrier, inc=1, device_id=(gx, lax.rem(gy + k, ny)), device_id_type=MESH)
    for k in range(1, nx):
        pl.semaphore_signal(barrier, inc=1, device_id=(lax.rem(gx + k, nx), gy), device_id_type=MESH)
    pl.semaphore_wait(barrier, nx + ny - 2)
    copies = []
    for k in range(1, ny):
        peer = lax.rem(gy + k, ny)
        copy = pltpu.make_async_remote_copy(
            src_ref=out_ref.at[peer], dst_ref=mid.at[gy], send_sem=send_y.at[k], recv_sem=recv_y.at[k],
            device_id=(gx, peer), device_id_type=MESH,
        )
        copy.start()
        copies.append(copy)
    own.wait()
    for copy in copies:
        copy.wait()
    own = pltpu.make_async_copy(mid.at[:, gx], in_ref.at[gx], own_sems.at[1])
    own.start()
    copies = []
    for k in range(1, nx):
        peer = lax.rem(gx + k, nx)
        copy = pltpu.make_async_remote_copy(
            src_ref=mid.at[:, peer], dst_ref=in_ref.at[gx], send_sem=send_x.at[k], recv_sem=recv_x.at[k],
            device_id=(peer, gy), device_id_type=MESH,
        )
        copy.start()
        copies.append(copy)
    own.wait()
    for copy in copies:
        copy.wait()


def shuffle(outbox):
    ny, nx = outbox.shape[0:2]
    anywhere = pl.BlockSpec(memory_space=pl.ANY)
    dma = pltpu.SemaphoreType.DMA
    return pl.pallas_call(
        shuffle_kernel,
        out_shape=jax.ShapeDtypeStruct((nx, ny, 1, 256), F32),
        in_specs=[anywhere],
        out_specs=anywhere,
        scratch_shapes=[VMEM((ny, nx, 1, 256), F32), dma((2,)), dma((ny,)), dma((ny,)), dma((nx,)), dma((nx,))],
        compiler_params=pltpu.CompilerParams(collective_id=1, has_side_effects=True),
        cost_estimate=cost(36 << 20),
        name="shuffle",
    )(outbox)


def row_as_column(row):
    return jnp.transpose(jnp.broadcast_to(row, (128, 128)))


def stencil_weights(t):
    root = jnp.sqrt(jnp.maximum(1.0 + 4.0 * t - 4.0 * t * t, 0.0))
    return (
        (3.0 - 2.0 * t - root) / 8.0,
        (3.0 - 2.0 * t + root) / 8.0,
        (1.0 + 2.0 * t + root) / 8.0,
        (1.0 + 2.0 * t - root) / 8.0,
    )


def powers(steps):
    size = jnp.exp(steps.astype(F32) * math.log(-ROOT))
    return jnp.where((steps & 1) == 1, -size, size)


def edge_table(n, kinds, spots):
    inside = (spots >= 0) & (spots < n)
    steps = jnp.where(kinds == 0, n - 1 - spots, spots)
    sums = jnp.where(inside & ((kinds == 0) | (kinds == 4)), powers(jnp.where(inside, steps, 0)), 0.0)
    only = jnp.where(kinds < 4, n - 2 + kinds, jnp.where(kinds == 5, 0, n + 2))
    single = (kinds != 0) & (kinds != 4) & (kinds < 7) & (spots == only)
    return jnp.where(single, 1.0, sums)


def spread_kernel(
    inbox_ref, mx_ref, my_ref, v_hbm,
    e_hbm, rl_ref, cn_ref, ud_ref,
    *scratch,
):
    grids = scratch[:COPIES]
    vbuf, m8, base_v, base_s, fcy, mxcol, wfar_ref, wnear_ref, pick_ref, ext, rlp, udp, v_sem, e_sems, s_sem = scratch[COPIES:]
    gx, gy = lax.axis_index("gx"), lax.axis_index("gy")
    chunks = inbox_ref.shape[0] * SLOTS // 128
    vin = pltpu.make_async_copy(v_hbm, vbuf, v_sem)
    vin.start()
    lane = lax.broadcasted_iota(jnp.int32, (8, 128), 1)
    sub = lax.broadcasted_iota(jnp.int32, (8, 128), 0)

    def regroup(g):
        out = None
        for k in range(4):
            row = inbox_ref[g * 4 + k]
            x = jnp.where(
                sub < 4, jnp.broadcast_to(row[:, 0:128], (8, 128)), jnp.broadcast_to(row[:, 128:256], (8, 128))
            )
            y = x
            for j in range(4):
                turn = (SLOTS * (k - j)) % 128
                z = pltpu.roll(x, turn, 1) if turn else x
                y = jnp.where((sub & 3) == j, z, y)
            out = y if out is None else jnp.where((lane >> 5) == k, y, out)
        at = g * 128 if isinstance(g, int) else pl.multiple_of(g * 128, 128)
        m8[:, pl.ds(at, 128)] = out
        code = out[6:7].astype(jnp.int32)
        tile = (((code >> 4) & 255) * 1681) >> 16
        pair = (2 * tile + (code & 1)) * PAIRS + ((code & 15) >> 1)
        base_v[:, pl.ds(at, 128)] = pair * SPAN + 2 * ((code >> 12) + OFF - 1)

    rows = grids[0].shape[0]
    share = 8 * (-(-rows // (8 * chunks)))
    full = rows // share

    def regroup_and_clear(g, carry):
        for grid in grids:
            grid[pl.ds(pl.multiple_of(g * share, 8), share), :] = jnp.zeros((share, 128), F32)
        regroup(g)
        return carry

    lax.fori_loop(0, full, regroup_and_clear, 0)
    for grid in grids:
        if full * share < rows:
            grid[full * share : rows, :] = jnp.zeros((rows - full * share, 128), F32)
    for g in range(full, chunks):
        regroup(g)
    bcopy = pltpu.make_async_copy(base_v, base_s, s_sem)
    bcopy.start()
    bcopy.wait()

    sub2 = lax.broadcasted_iota(jnp.int32, (128, 128), 0)
    comp = jnp.where(sub2 >= 2 * GROUP, 2, jnp.where(sub2 >= GROUP, 1, 0))
    rel = jnp.where(sub2 >= 3 * GROUP, -100, sub2 - GROUP * comp)

    def chunk(c, carry):
        m = m8[:, pl.ds(pl.multiple_of(c * 128, 128), 128)]
        ws = stencil_weights(m)
        code = m[6:7].astype(jnp.int32)
        cell_y = (code >> 4) & 255
        inner = cell_y - BASES * ((cell_y * 1681) >> 16)
        d = rel - inner
        w = jnp.where(d == 0, ws[0][4:5], 0.0)
        w = jnp.where(d == 1, ws[1][4:5], w)
        w = jnp.where(d == 2, ws[2][4:5], w)
        w = jnp.where(d == 3, ws[3][4:5], w)
        f = jnp.where(comp == 0, m[0:1], jnp.where(comp == 1, m[1:2], m[2:3]))
        fcy[...] = jnp.transpose(w * f)
        wx = [w[3:4] for w in ws]
        wz = [w[5:6] for w in ws]
        sides = ((wz[0], wz[1]), (wz[2], wz[3]))
        wx8 = jnp.concatenate([wx[i // 2] for i in range(8)], axis=0)
        tall = [wx8 * jnp.concatenate(list(side) * 4, axis=0) for side in sides]
        fr = fcy[...]
        bs = [base_s[0, c * 128 + k] for k in range(128)]
        for k0 in range(0, 128, COPIES):
            group = []
            for k in range(k0, k0 + COPIES):
                grid = grids[k % COPIES]
                for q in range(2):
                    at = bs[k] + q * SPAN
                    group.append((grid, at, grid[pl.ds(at, 8), :] + tall[q][:, k : k + 1] * fr[k : k + 1, :]))
            for grid, at, value in group:
                grid[pl.ds(at, 8), :] = value
        return carry

    lax.fori_loop(0, chunks, chunk, 0)

    def spots(t, e, odds=(0, 1)):
        return [(2 * t + odd) * PAIRS * SPAN + ((e - odd) >> 1) * SPAN + ((e - odd) & 1) for odd in odds]

    for t in range(TILES):
        for src, odds, dst in ((0, (0,), 16), (17, (0, 1), 1), (18, (1,), 2)):
            moved = None
            for grid in grids:
                for at in spots(t, src, odds):
                    x = grid[pl.ds(at, XEXT, stride=2), :]
                    moved = x if moved is None else moved + x
            here = pl.ds(spots(t, dst)[0], XEXT, stride=2)
            grids[0][here, :] = grids[0][here, :] + moved

    nx, ny = mx_ref.shape[0], my_ref.shape[0]
    mxcol[0:OFF, :] = row_as_column(mx_ref[pl.ds(lax.rem(gx + nx - 1, nx), 1), :])[128 - OFF : 128]
    mxcol[OFF : OFF + 128, :] = row_as_column(mx_ref[pl.ds(gx, 1), :])
    mxcol[OFF + 128 : XEXT, :] = row_as_column(mx_ref[pl.ds(lax.rem(gx + 1, nx), 1), :])[0 : XEXT - OFF - 128]
    after = my_ref[pl.ds(lax.rem(2 * gy + 2, ny), 1), :]
    before = pltpu.roll(jnp.broadcast_to(my_ref[pl.ds(lax.rem(2 * gy + ny - 1, ny), 1), :], (8, 128)), 3, 1)[0:1]
    lane1 = lax.broadcasted_iota(jnp.int32, (1, 128), 1)
    rim = jnp.where(lane1 < 2, after, jnp.where(lane1 == 2, before, 0.0))
    mys = [HALF * my_ref[pl.ds(2 * gy, 1), :], HALF * my_ref[pl.ds(2 * gy + 1, 1), :], HALF * rim]
    at = lax.broadcasted_iota(jnp.int32, (XEXT, 128), 0) - OFF
    wfar_ref[...] = edge_table(128, 0, at)
    wnear_ref[...] = edge_table(128, 4, at)
    kinds = lax.broadcasted_iota(jnp.int32, (8, 384), 0)
    high, low = split(edge_table(256, kinds, lax.broadcasted_iota(jnp.int32, (8, 384), 1)))
    pick_ref[...] = jnp.concatenate([high.astype(F32), low.astype(F32)], axis=0).astype(BF16)
    vin.wait()

    part = 48
    lanes = lax.broadcasted_iota(jnp.int32, (part, 128), 1)

    def moves(c, h):
        out = []
        if h == 2:
            out.append((6, (-(GROUP * c + 256 - (6 * BASES - 1))) % 128, 0, 2))
            out.append((0, (2 - GROUP * c) % 128, 2, 3))
            return out
        for t in range(TILES):
            low, high = BASES * t - 1 - 128 * h, BASES * t - 1 + GROUP - 128 * h
            if high > 0 and low < 128:
                out.append((t, (low - GROUP * c) % 128, max(low, 0), min(high, 128)))
        return out

    def plane(z, carry):
        far = [[jnp.zeros((8, 128), F32)] * 3 for _ in range(3)]
        near = [[jnp.zeros((8, 128), F32)] * 3 for _ in range(3)]
        for r0 in range(0, XEXT, part):
            tiles = []
            for t in range(TILES):
                x = None
                for grid in grids:
                    for at in spots(t, z + 1):
                        y = grid[pl.ds(at + 2 * r0, part, stride=2), :]
                        x = y if x is None else x + y
                tiles.append(x)
            mcol = mxcol[r0 : r0 + part, :]
            wf, wn = wfar_ref[r0 : r0 + part, :], wnear_ref[r0 : r0 + part, :]
            r1 = r0 + part
            i0, i1 = max(r0, OFF), min(r1, OFF + 128)
            for c in range(3):
                for h in range(3):
                    e = None
                    for t, turn, low, high in moves(c, h):
                        x = pltpu.roll(tiles[t], turn, 1) if turn else tiles[t]
                        if low > 0 or high < 128:
                            x = jnp.where((lanes >= low) & (lanes < high), x, 0.0)
                        e = x if e is None else e + x
                    e = e * mcol * mys[h]
                    if h < 2:
                        cols = slice(h * 128, (h + 1) * 128)
                        inner = e[i0 - r0 : i1 - r0] + vbuf[c, z, i0 - OFF : i1 - OFF, cols]
                        vbuf[c, z, i0 - OFF : i1 - OFF, cols] = inner
                        pieces = [e[0 : i0 - r0]] if i0 > r0 else []
                        pieces.append(inner)
                        if i1 < r1:
                            pieces.append(e[i1 - r0 :])
                        e = jnp.concatenate(pieces, axis=0) if len(pieces) > 1 else inner
                    ext[c, h, r0:r1, :] = e
                    far[c][h] = far[c][h] + jnp.sum((e * wf).reshape(part // 8, 8, 128), axis=0)
                    near[c][h] = near[c][h] + jnp.sum((e * wn).reshape(part // 8, 8, 128), axis=0)
        for c in range(3):
            p = c * 16 + z
            at = pl.multiple_of(p * 8, 8)
            for h in range(3):
                rowset = [
                    jnp.sum(far[c][h], axis=0, keepdims=True),
                    ext[c, h, OFF + 127 : OFF + 130, :],
                    jnp.sum(near[c][h], axis=0, keepdims=True),
                    ext[c, h, OFF : OFF + 1, :],
                    ext[c, h, OFF - 1 : OFF, :],
                    jnp.zeros((1, 128), F32),
                ]
                rlp[h, pl.ds(at, 8), :] = jnp.concatenate(rowset, axis=0)
            high, low = split(jnp.concatenate([ext[c, h, OFF : OFF + 128, :] for h in range(3)], axis=1))
            nt = (((1,), (1,)), ((), ()))
            one = lax.dot_general(pick_ref[...], high, nt, preferred_element_type=F32)
            two = lax.dot_general(pick_ref[...], low, nt, preferred_element_type=F32)
            udp[pl.ds(at, 8), :] = one[0:8] + one[8:16] + two[0:8]
        pltpu.make_async_copy(vbuf.at[:, z], e_hbm.at[:, z], e_sems.at[z]).start()
        return carry

    lax.fori_loop(0, 16, plane, 0)

    corner = jnp.zeros((48, 128), F32)
    kinds = jnp.minimum(lax.broadcasted_iota(jnp.int32, (384, 128), 1), 7)
    tail = edge_table(256, kinds, lax.broadcasted_iota(jnp.int32, (384, 128), 0))
    for t in range(7):
        row = jnp.concatenate([rlp[h, pl.ds(t, 48, stride=8), :] for h in range(3)], axis=1)
        rl_ref[t] = row[:, 0:256]
        ends = jnp.dot(row, tail, preferred_element_type=F32, precision=lax.Precision.HIGHEST)
        corner = corner + (pltpu.roll(ends, 8 * t, 1) if t else ends)
        ud_ref[t] = udp[pl.ds(t, 48, stride=8), :]
    rl_ref[7] = jnp.zeros((48, 256), F32)
    ud_ref[7] = jnp.zeros((48, 128), F32)
    cn_ref[...] = corner
    for z in range(16):
        pltpu.make_async_copy(vbuf.at[:, z], e_hbm.at[:, z], e_sems.at[z]).wait()


def spread(inbox, mx, my, v):
    rows = TILES * 2 * PAIRS * SPAN
    total = inbox.shape[0] * SLOTS
    vm = pl.BlockSpec(memory_space=VMEM)
    return pl.pallas_call(
        spread_kernel,
        out_shape=(
            jax.ShapeDtypeStruct(v.shape, F32),
            jax.ShapeDtypeStruct((8, 48, 256), F32),
            jax.ShapeDtypeStruct((48, 128), F32),
            jax.ShapeDtypeStruct((8, 48, 128), F32),
        ),
        in_specs=[vm] * 3 + [pl.BlockSpec(memory_space=pl.ANY)],
        out_specs=(pl.BlockSpec(memory_space=pl.ANY), vm, vm, vm),
        scratch_shapes=[VMEM((rows, 128), F32)] * COPIES
        + [
            VMEM(v.shape, F32),
            VMEM((8, total), F32),
            VMEM((1, total), jnp.int32),
            pltpu.SMEM((1, total), jnp.int32),
            VMEM((128, 128), F32),
            VMEM((XEXT, 128), F32),
            VMEM((XEXT, 128), F32),
            VMEM((XEXT, 128), F32),
            VMEM((16, 384), BF16),
            VMEM((3, 3, XEXT, 128), F32),
            VMEM((3, 48 * 8, 128), F32),
            VMEM((48 * 8, 128), F32),
            pltpu.SemaphoreType.DMA,
            pltpu.SemaphoreType.DMA((16,)),
            pltpu.SemaphoreType.DMA,
        ],
        compiler_params=pltpu.CompilerParams(vmem_limit_bytes=45 << 20),
        cost_estimate=cost(100 << 20),
        name="spread",
    )(inbox, mx, my, v)


def exchange_kernel(
    rl_hbm, cn_hbm, ud_hbm, xh_ref, yh_ref, rl_ref, cn_ref, ud_ref,
    ra, ca, rb, cb, umsg, hmsg, pu, ph, qd, qh, own_sems, send_sems, recv_sems,
):
    pairs = ((cn_hbm, cn_ref), (ud_hbm, ud_ref), (rl_hbm, rl_ref))
    loads = [pltpu.make_async_copy(src, dst, own_sems.at[i]) for i, (src, dst) in enumerate(pairs)]
    for load in loads:
        load.start()
    gx, gy = lax.axis_index("gx"), lax.axis_index("gy")
    nx, ny = lax.axis_size("gx"), lax.axis_size("gy")
    right = (lax.rem(gx + 1, nx), gy)
    left = (lax.rem(gx + nx - 1, nx), gy)
    up = (gx, lax.rem(gy + 1, ny))
    down = (gx, lax.rem(gy + ny - 1, ny))
    barrier = pltpu.get_barrier_semaphore()
    for device in (right, left, up, down):
        pl.semaphore_signal(barrier, inc=1, device_id=device, device_id_type=MESH)
    pl.semaphore_wait(barrier, 4)

    def send(i, src, dst, device):
        copy = pltpu.make_async_remote_copy(
            src_ref=src, dst_ref=dst, send_sem=send_sems.at[i], recv_sem=recv_sems.at[i],
            device_id=device, device_id_type=MESH,
        )
        copy.start()
        return copy

    first = [
        send(0, cn_hbm, ca, right),
        send(1, cn_hbm, cb, left),
        send(2, rl_hbm.at[0:4], ra, right),
        send(3, rl_hbm.at[4:7], rb, left),
    ]
    planes = cn_ref.shape[0]
    lane = lax.broadcasted_iota(jnp.int32, (planes, 128), 1)
    for load in loads:
        load.wait()
    first[0].wait()
    first[1].wait()
    own, a, b = cn_ref[...], ca[...], cb[...]
    turn = lambda x, by: pltpu.roll(x, by % 128, 1)
    hold = jnp.where(lane < 8, a + turn(own, -48), a + turn(own, -40))
    hold = jnp.where(
        lane < 16, hold, turn(b, -16) + jnp.where(lane < 24, own + ROOT * turn(own, -8), turn(own, 8))
    )
    hmsg[...] = jnp.where(lane < 32, hold, 0.0)
    for s in range(7):
        umsg[s] = (
            ud_ref[s]
            + jnp.where(lane == 0, a[:, 16 + s : 17 + s], 0.0)
            + jnp.where(lane == 1, a[:, 24 + s : 25 + s], 0.0)
            + jnp.where(lane == 127, b[:, 48 + s : 49 + s], 0.0)
        )
    second = [
        send(4, hmsg, ph, up),
        send(5, hmsg, qh, down),
        send(6, umsg.at[0:4], pu, up),
        send(7, umsg.at[4:7], qd, down),
    ]
    first[2].wait()
    first[3].wait()
    second[0].wait()
    second[1].wait()
    lane = lax.broadcasted_iota(jnp.int32, (planes, 256), 1)
    p, q = ph[...], qh[...]

    def rims(h):
        return (
            jnp.where(lane == 0, p[:, 8 * h + 2 : 8 * h + 3], 0.0)
            + jnp.where(lane == 1, p[:, 8 * h + 3 : 8 * h + 4], 0.0)
            + jnp.where(lane == 255, q[:, 8 * h + 6 : 8 * h + 7], 0.0)
        )

    def put(t, value):
        for h in range(2):
            xh_ref[h, pl.ds(t, planes, stride=8), :] = value[:, h * 128 : (h + 1) * 128]

    put(0, ra[0] + rl_ref[6] + rims(0))
    put(1, ra[1] + rl_ref[6] + rims(1))
    put(2, rb[0] + rl_ref[2] + ROOT * rl_ref[3] + rims(2))
    put(3, rb[1] + rl_ref[2] + rims(3))
    put(4, ra[2])
    put(5, ra[3])
    put(6, rb[2])
    put(7, jnp.zeros((planes, 256), F32))
    second[2].wait()
    second[3].wait()
    yh_ref[pl.ds(0, planes, stride=8), :] = pu[0] + umsg[6]
    yh_ref[pl.ds(1, planes, stride=8), :] = pu[1] + umsg[6]
    yh_ref[pl.ds(2, planes, stride=8), :] = qd[0] + umsg[2] + ROOT * umsg[3]
    yh_ref[pl.ds(3, planes, stride=8), :] = qd[1] + umsg[2]
    yh_ref[pl.ds(4, planes, stride=8), :] = pu[2]
    yh_ref[pl.ds(5, planes, stride=8), :] = pu[3]
    yh_ref[pl.ds(6, planes, stride=8), :] = qd[2]
    yh_ref[pl.ds(7, planes, stride=8), :] = jnp.zeros((planes, 128), F32)


def exchange(rl, cn, ud):
    n = cn.shape[0]
    vm = pl.BlockSpec(memory_space=VMEM)
    return pl.pallas_call(
        exchange_kernel,
        out_shape=(jax.ShapeDtypeStruct((2, 8 * n, 128), F32), jax.ShapeDtypeStruct((8 * n, 128), F32)),
        in_specs=[pl.BlockSpec(memory_space=pl.ANY)] * 3,
        out_specs=(vm, vm),
        scratch_shapes=[
            VMEM((8, n, 256), F32),
            VMEM((n, 128), F32),
            VMEM((8, n, 128), F32),
            VMEM((4, n, 256), F32),
            VMEM((n, 128), F32),
            VMEM((3, n, 256), F32),
            VMEM((n, 128), F32),
            VMEM((7, n, 128), F32),
            VMEM((n, 128), F32),
            VMEM((4, n, 128), F32),
            VMEM((n, 128), F32),
            VMEM((3, n, 128), F32),
            VMEM((n, 128), F32),
            pltpu.SemaphoreType.DMA((3,)),
            pltpu.SemaphoreType.DMA((8,)),
            pltpu.SemaphoreType.DMA((8,)),
        ],
        compiler_params=pltpu.CompilerParams(vmem_limit_bytes=8 << 20, collective_id=0, has_side_effects=True),
        cost_estimate=cost(30 << 20),
        name="exchange",
    )(rl, cn, ud)


def derive_kernel(e_ref, xh_ref, yh_ref, mx_ref, my_ref, kx_ref, ky_ref, kl_ref, rim_ref, dx_ref, dy_ref, mxcol, myrow):
    @pl.when(pl.program_id(0) == 0)
    def _():
        gx, gy = lax.axis_index("gx"), lax.axis_index("gy")
        mxcol[...] = row_as_column(mx_ref[pl.ds(gx, 1), :])
        myrow[:, 0:128] = jnp.broadcast_to(my_ref[pl.ds(2 * gy, 1), :], (8, 128))
        myrow[:, 128:256] = jnp.broadcast_to(my_ref[pl.ds(2 * gy + 1, 1), :], (8, 128))

    each = e_ref.shape[0]
    zero = jnp.zeros((1, 256), F32)
    col = mxcol[...]
    yall = jnp.concatenate([yh_ref[i * 8 : i * 8 + 8, :] for i in range(each)], axis=1)
    high = yall.astype(BF16).astype(F32)
    stack = jnp.concatenate([high, yall - high, high, jnp.zeros_like(high)], axis=0).astype(BF16)
    extra = lax.dot_general(stack, rim_ref[...], (((0,), (0,)), ((), ())), preferred_element_type=F32)
    highs, lows = [], []
    for i in range(each):
        xall = jnp.concatenate([xh_ref[0, i * 8 : i * 8 + 8, :], xh_ref[1, i * 8 : i * 8 + 8, :]], axis=1)
        top = jnp.concatenate([xall[4:6]] + [zero] * 6, axis=0)
        low = jnp.concatenate([zero] * 7 + [xall[6:7]], axis=0)
        e = e_ref[i]
        f = jnp.concatenate([e[0:8] + top, e[8:120], e[120:128] + low], axis=0)
        f = f + extra[i * 128 : (i + 1) * 128, 256:512]
        halo = jnp.concatenate([xall[0:4]] + [zero] * 12, axis=0)
        fh, fl = split(f)
        hh, hl = split(halo)
        highs.append(fh)
        lows.append(fl)
        one = dot(kx_ref[...], jnp.concatenate([fh, hh], axis=0))
        dx = one[0:128] + one[128:256] + dot(kx_ref[0:128], jnp.concatenate([fl, hl], axis=0))
        dx_ref[i, :, 0:128] = dx[:, 0:128] * col
        dx_ref[i, :, 128:256] = dx[:, 128:256] * col
    two = dot(jnp.concatenate(highs + lows, axis=0), ky_ref[...])
    n = each * 128
    dy = two[0:n] + two[n : 2 * n] + dot(jnp.concatenate(highs, axis=0), kl_ref[...]) + extra[:, 0:256]
    dy_ref[...] = (dy * myrow[0:1, :]).reshape(dy_ref.shape)


def derive(e, xh, yh, mx, my):
    n, rows, cols = e.shape
    each = EACH
    kx = np.zeros((rows, 144))
    kx[:, 0:rows] = line_matrix(rows)
    kx[:, rows : rows + 4] = halo_columns(rows)
    kx = np.concatenate(halves(kx), axis=0)
    kh, kl = halves(line_matrix(cols).T)
    rim = np.zeros((8, 512))
    rim[0:4, 0:256] = halo_columns(cols).T
    rim[4, 256] = 1.0
    rim[5, 257] = 1.0
    rim[6, 511] = 1.0
    rh, rlow = halves(rim)
    rim = np.concatenate([rh, rh, rlow, np.zeros((8, 512), BF16)], axis=0)
    whole = lambda x: pl.BlockSpec(x.shape, lambda i: (0,) * x.ndim)
    block = pl.BlockSpec((each, rows, cols), lambda i: (i, 0, 0))
    consts = (kx, kh, kl, rim)
    xspec = pl.BlockSpec((2, each * 8, 128), lambda i: (0, i, 0))
    yspec = pl.BlockSpec((each * 8, 128), lambda i: (i, 0))
    return pl.pallas_call(
        derive_kernel,
        grid=(n // each,),
        out_shape=(jax.ShapeDtypeStruct(e.shape, F32),) * 2,
        in_specs=[block, xspec, yspec] + [whole(x) for x in (mx, my) + consts],
        out_specs=(block, block),
        scratch_shapes=[VMEM((128, 128), F32), VMEM((8, 256), F32)],
        compiler_params=pltpu.CompilerParams(vmem_limit_bytes=24 << 20),
        cost_estimate=cost(30 << 20),
        name="derive",
    )(e, xh, yh, mx, my, *consts)


def local(
    velocity, metric_x, metric_y, marker_force, marker_frac, marker_cell_x, marker_cell_y, marker_cell_z, send_counts
):
    comps, planes, rows, cols = velocity.shape
    fold = lambda x: x.reshape(-1, 128)
    cells = [fold(x) for x in (marker_cell_x, marker_cell_y, marker_cell_z)]
    outbox = pack(send_counts, marker_force, marker_frac, *cells)
    inbox = shuffle(outbox).reshape(-1, 1, 256)
    mx, my = fold(metric_x), fold(metric_y)
    e, rl, cn, ud = spread(inbox, mx, my, velocity)
    xh, yh = exchange(rl, cn, ud)
    dx, dy = derive(e.reshape(comps * planes, rows, cols), xh, yh, mx, my)
    return dx.reshape(velocity.shape), dy.reshape(velocity.shape)


def solution(mesh):
    both = ("gx", "gy")
    placed = (
        P(None, None, "gx", "gy"), P(), P(), P(None, both), P(None, both), P(both), P(both), P(both), P(both, None),
    )
    return jax.shard_map(
        local,
        mesh=mesh,
        in_specs=placed,
        out_specs=(P(None, None, "gx", "gy"), P(None, None, "gx", "gy")),
        check_vma=False,
    )
```

```python
import functools
import math

import jax
import jax.numpy as jnp
import numpy as np
from jax import lax
from jax.experimental import pallas as pl
from jax.experimental.pallas import tpu as pltpu
from jax.sharding import PartitionSpec as P

SLOTS = 32
HALF = 0.5
GROUP = 42
BASES = 39
OFF = 8
XEXT = 144
PAIRS = 9
SPAN = 2 * XEXT
EACH = 12
UNROLL = 4
TOGETHER = 4
TILES = 7
COPIES = 2
ROOT = (math.sqrt(5.0) - 3.0) / 2.0
MESH = pl.DeviceIdType.MESH
VMEM = pltpu.VMEM
F32 = jnp.float32
BF16 = jnp.bfloat16


SCALE = 1.0 / (1.0 + 2.0 * ROOT / 3.0)
LEAD = SCALE * (7.0 / 9.0 * (1.0 / ROOT - ROOT) + 1.0 / 36.0 * (1.0 / ROOT**2 - ROOT**2))
NEAR = SCALE / 36.0 * (ROOT - 1.0 / ROOT)


def line_matrix(n):
    gap = np.arange(n)[None, :] - np.arange(n)[:, None]
    out = np.sign(gap) * LEAD * ROOT ** np.abs(gap).astype(np.float64)
    return out + np.where(np.abs(gap) == 1, np.sign(gap) * NEAR, 0.0)


def halo_columns(n):
    out = np.zeros((n, 4))
    steps = np.arange(n)
    out[:, 0] = -LEAD * ROOT ** (steps + 1.0)
    out[0, 1] = -NEAR
    out[:, 2] = LEAD * ROOT ** (n - steps * 1.0)
    out[n - 1, 3] = NEAR
    return out


def halves(values):
    values = np.asarray(values, np.float32)
    high = values.astype(BF16)
    low = (values - high.astype(np.float32)).astype(BF16)
    return high, low


def split(x):
    high = x.astype(BF16)
    return high, (x - high.astype(F32)).astype(BF16)


def dot(a, b):
    return jnp.dot(a, b, preferred_element_type=F32)


def cost(size):
    return pl.CostEstimate(flops=0, bytes_accessed=size, transcendentals=0)


def pack_kernel(counts_ref, force_ref, frac_ref, cx_ref, cy_ref, cz_ref, out_ref, wide):
    size = force_ref.shape[1]
    wide[0:3, 0:size] = force_ref[...]
    wide[3:6, 0:size] = frac_ref[...]
    code = ((cx_ref[...] * 256 + cy_ref[...]) * 16 + cz_ref[...]).astype(F32)
    for i in range(size // 128):
        wide[6:7, i * 128 : (i + 1) * 128] = code[i : i + 1]
    wide[7:8, 0:size] = jnp.zeros((1, size), F32)
    wide[:, size:] = jnp.zeros((8, wide.shape[1] - size), F32)
    lane = lax.broadcasted_iota(jnp.int32, (8, 128), 1)
    sub = lax.broadcasted_iota(jnp.int32, (8, 128), 0)
    part = sub & 3
    unused = jnp.where((sub == 6) & (lane < SLOTS), lane * (4 << 12), 0).astype(F32)

    def one(d, start):
        count = counts_ref[0, d]
        first = pl.multiple_of((start >> 7) << 7, 128)
        shift = start & 127
        back = (128 - shift) & 127
        a = pltpu.roll(wide[:, pl.ds(first, 128)], back, 1)
        b = pltpu.roll(wide[:, pl.ds(first + 128, 128)], back, 1)
        w = jnp.where(lane + shift < 128, a, b)
        w = jnp.where(lane < count, w, unused)
        m = w
        for j in range(1, 4):
            m = jnp.where(part == j, pltpu.roll(w, SLOTS * j, 1), m)
        top = jnp.sum(jnp.where(sub < 4, m, 0.0), axis=0, keepdims=True)
        low = jnp.sum(jnp.where(sub < 4, 0.0, m), axis=0, keepdims=True)
        return start + count, jnp.concatenate([top, low], axis=1)

    def several(g, start):
        for j in range(UNROLL):
            for k in range(8):
                start, out_ref[k, g * UNROLL + j] = one((g * UNROLL + j) * 8 + k, start)
        return start

    lax.fori_loop(0, out_ref.shape[1] // UNROLL, several, jnp.int32(0))


def pack(counts, *fields):
    vm = pl.BlockSpec(memory_space=VMEM)
    return pl.pallas_call(
        pack_kernel,
        out_shape=jax.ShapeDtypeStruct((8, counts.shape[1] // 8, 1, 256), F32),
        in_specs=[pl.BlockSpec(memory_space=pltpu.SMEM)] + [vm] * 5,
        out_specs=vm,
        scratch_shapes=[VMEM((8, fields[0].shape[1] + 256), F32)],
        cost_estimate=cost(12 << 20),
        name="pack",
    )(counts, *fields)


def shuffle_kernel(out_ref, in_ref, mid, own_sems, send_y, recv_y, send_x, recv_x):
    gx, gy = lax.axis_index("gx"), lax.axis_index("gy")
    nx, ny = lax.axis_size("gx"), lax.axis_size("gy")
    own = pltpu.make_async_copy(out_ref.at[gy], mid.at[gy], own_sems.at[0])
    own.start()
    barrier = pltpu.get_barrier_semaphore()
    for k in range(1, ny):
        pl.semaphore_signal(barrier, inc=1, device_id=(gx, lax.rem(gy + k, ny)), device_id_type=MESH)
    for k in range(1, nx):
        pl.semaphore_signal(barrier, inc=1, device_id=(lax.rem(gx + k, nx), gy), device_id_type=MESH)
    pl.semaphore_wait(barrier, nx + ny - 2)
    copies = []
    for k in range(1, ny):
        peer = lax.rem(gy + k, ny)
        copy = pltpu.make_async_remote_copy(
            src_ref=out_ref.at[peer], dst_ref=mid.at[gy], send_sem=send_y.at[k], recv_sem=recv_y.at[k],
            device_id=(gx, peer), device_id_type=MESH,
        )
        copy.start()
        copies.append(copy)
    own.wait()
    for copy in copies:
        copy.wait()
    own = pltpu.make_async_copy(mid.at[:, gx], in_ref.at[gx], own_sems.at[1])
    own.start()
    copies = []
    for k in range(1, nx):
        peer = lax.rem(gx + k, nx)
        copy = pltpu.make_async_remote_copy(
            src_ref=mid.at[:, peer], dst_ref=in_ref.at[gx], send_sem=send_x.at[k], recv_sem=recv_x.at[k],
            device_id=(peer, gy), device_id_type=MESH,
        )
        copy.start()
        copies.append(copy)
    own.wait()
    for copy in copies:
        copy.wait()


def shuffle(outbox):
    ny, nx = outbox.shape[0:2]
    anywhere = pl.BlockSpec(memory_space=pl.ANY)
    dma = pltpu.SemaphoreType.DMA
    return pl.pallas_call(
        shuffle_kernel,
        out_shape=jax.ShapeDtypeStruct((nx, ny, 1, 256), F32),
        in_specs=[anywhere],
        out_specs=anywhere,
        scratch_shapes=[VMEM((ny, nx, 1, 256), F32), dma((2,)), dma((ny,)), dma((ny,)), dma((nx,)), dma((nx,))],
        compiler_params=pltpu.CompilerParams(collective_id=1, has_side_effects=True),
        cost_estimate=cost(36 << 20),
        name="shuffle",
    )(outbox)


def row_as_column(row):
    return jnp.transpose(jnp.broadcast_to(row, (128, 128)))


def stencil_weights(t):
    root = jnp.sqrt(jnp.maximum(1.0 + 4.0 * t - 4.0 * t * t, 0.0))
    return (
        (3.0 - 2.0 * t - root) / 8.0,
        (3.0 - 2.0 * t + root) / 8.0,
        (1.0 + 2.0 * t + root) / 8.0,
        (1.0 + 2.0 * t - root) / 8.0,
    )


def powers(steps):
    size = jnp.exp(steps.astype(F32) * math.log(-ROOT))
    return jnp.where((steps & 1) == 1, -size, size)


def edge_table(n, kinds, spots):
    inside = (spots >= 0) & (spots < n)
    steps = jnp.where(kinds == 0, n - 1 - spots, spots)
    sums = jnp.where(inside & ((kinds == 0) | (kinds == 4)), powers(jnp.where(inside, steps, 0)), 0.0)
    only = jnp.where(kinds < 4, n - 2 + kinds, jnp.where(kinds == 5, 0, n + 127))
    single = (kinds != 0) & (kinds != 4) & (kinds < 7) & (spots == only)
    return jnp.where(single, 1.0, sums)


def spread_kernel(
    inbox_ref, mx_ref, my_ref, v_hbm,
    e_hbm, rl_ref, cn_ref, ud_ref,
    *scratch,
):
    grids = scratch[:COPIES]
    vbuf, m8, base_v, base_s, mxcol, wfar_ref, wnear_ref, pick_ref, ext, rlp, udp, v_sem, e_sems, s_sem = scratch[COPIES:]
    gx, gy = lax.axis_index("gx"), lax.axis_index("gy")
    chunks = inbox_ref.shape[0] * SLOTS // 128
    vin = pltpu.make_async_copy(v_hbm, vbuf, v_sem)
    vin.start()
    lane = lax.broadcasted_iota(jnp.int32, (8, 128), 1)
    sub = lax.broadcasted_iota(jnp.int32, (8, 128), 0)

    def regroup(g):
        out = None
        for k in range(4):
            row = inbox_ref[g * 4 + k]
            x = jnp.where(
                sub < 4, jnp.broadcast_to(row[:, 0:128], (8, 128)), jnp.broadcast_to(row[:, 128:256], (8, 128))
            )
            y = x
            for j in range(4):
                turn = (SLOTS * (k - j)) % 128
                z = pltpu.roll(x, turn, 1) if turn else x
                y = jnp.where((sub & 3) == j, z, y)
            out = y if out is None else jnp.where((lane >> 5) == k, y, out)
        at = g * 128 if isinstance(g, int) else pl.multiple_of(g * 128, 128)
        m8[:, pl.ds(at, 128)] = out
        code = out[6:7].astype(jnp.int32)
        tile = (((code >> 4) & 255) * 1681) >> 16
        pair = (2 * tile + (code & 1)) * PAIRS + ((code & 15) >> 1)
        base_v[:, pl.ds(at, 128)] = pair * SPAN + 2 * ((code >> 12) + OFF - 1)

    rows = grids[0].shape[0]
    share = 8 * (-(-rows // (8 * chunks)))
    full = rows // share

    def regroup_and_clear(g, carry):
        for grid in grids:
            grid[pl.ds(pl.multiple_of(g * share, 8), share), :] = jnp.zeros((share, 128), F32)
        regroup(g)
        return carry

    lax.fori_loop(0, full, regroup_and_clear, 0)
    for grid in grids:
        if full * share < rows:
            grid[full * share : rows, :] = jnp.zeros((rows - full * share, 128), F32)
    for g in range(full, chunks):
        regroup(g)
    bcopy = pltpu.make_async_copy(base_v, base_s, s_sem)
    bcopy.start()
    bcopy.wait()

    sub2 = lax.broadcasted_iota(jnp.int32, (128, 128), 0)
    comp = jnp.where(sub2 >= 2 * GROUP, 2, jnp.where(sub2 >= GROUP, 1, 0))
    rel = jnp.where(sub2 >= 3 * GROUP, -100, sub2 - GROUP * comp)

    def tables(c):
        m = m8[:, pl.ds(pl.multiple_of(c * 128, 128), 128)]
        ws = stencil_weights(m)
        code = m[6:7].astype(jnp.int32)
        cell_y = (code >> 4) & 255
        inner = cell_y - BASES * ((cell_y * 1681) >> 16)
        d = rel - inner
        w = jnp.where(d == 0, ws[0][4:5], 0.0)
        w = jnp.where(d == 1, ws[1][4:5], w)
        w = jnp.where(d == 2, ws[2][4:5], w)
        w = jnp.where(d == 3, ws[3][4:5], w)
        f = jnp.where(comp == 0, m[0:1], jnp.where(comp == 1, m[1:2], m[2:3]))
        wx8 = jnp.concatenate([ws[i // 2][3:4] for i in range(8)], axis=0)
        sides = ((ws[0][5:6], ws[1][5:6]), (ws[2][5:6], ws[3][5:6]))
        tall = [wx8 * jnp.concatenate(list(side) * 4, axis=0) for side in sides]
        return jnp.transpose(w * f), tall

    def chunk(i, carry):
        built = [tables(i * TOGETHER + j) for j in range(TOGETHER)]
        for j, (fr, tall) in enumerate(built):
            bs = [base_s[0, (i * TOGETHER + j) * 128 + k] for k in range(128)]
            for k0 in range(0, 128, COPIES):
                group = []
                for k in range(k0, k0 + COPIES):
                    grid = grids[k % COPIES]
                    for q in range(2):
                        at = bs[k] + q * SPAN
                        group.append((grid, at, grid[pl.ds(at, 8), :] + tall[q][:, k : k + 1] * fr[k : k + 1, :]))
                for grid, at, value in group:
                    grid[pl.ds(at, 8), :] = value
        return carry

    lax.fori_loop(0, chunks // TOGETHER, chunk, 0)

    def spots(t, e, odds=(0, 1)):
        return [(2 * t + odd) * PAIRS * SPAN + ((e - odd) >> 1) * SPAN + ((e - odd) & 1) for odd in odds]

    for t in range(TILES):
        for src, odds, dst in ((0, (0,), 16), (17, (0, 1), 1), (18, (1,), 2)):
            moved = None
            for grid in grids:
                for at in spots(t, src, odds):
                    x = grid[pl.ds(at, XEXT, stride=2), :]
                    moved = x if moved is None else moved + x
            here = pl.ds(spots(t, dst)[0], XEXT, stride=2)
            grids[0][here, :] = grids[0][here, :] + moved

    nx, ny = mx_ref.shape[0], my_ref.shape[0]
    mxcol[0:OFF, :] = row_as_column(mx_ref[pl.ds(lax.rem(gx + nx - 1, nx), 1), :])[128 - OFF : 128]
    mxcol[OFF : OFF + 128, :] = row_as_column(mx_ref[pl.ds(gx, 1), :])
    mxcol[OFF + 128 : XEXT, :] = row_as_column(mx_ref[pl.ds(lax.rem(gx + 1, nx), 1), :])[0 : XEXT - OFF - 128]
    after = my_ref[pl.ds(lax.rem(2 * gy + 2, ny), 1), :]
    before = my_ref[pl.ds(lax.rem(2 * gy + ny - 1, ny), 1), :]
    lane1 = lax.broadcasted_iota(jnp.int32, (1, 128), 1)
    rim = jnp.where(lane1 < 2, after, jnp.where(lane1 == 127, before, 0.0))
    mys = [HALF * my_ref[pl.ds(2 * gy, 1), :], HALF * my_ref[pl.ds(2 * gy + 1, 1), :], HALF * rim]
    at = lax.broadcasted_iota(jnp.int32, (XEXT, 128), 0) - OFF
    wfar_ref[...] = edge_table(128, 0, at)
    wnear_ref[...] = edge_table(128, 4, at)
    kinds = lax.broadcasted_iota(jnp.int32, (8, 384), 0)
    high, low = split(edge_table(256, kinds, lax.broadcasted_iota(jnp.int32, (8, 384), 1)))
    pick_ref[...] = jnp.concatenate([high.astype(F32), low.astype(F32)], axis=0).astype(BF16)
    vin.wait()

    part = 48
    lanes = lax.broadcasted_iota(jnp.int32, (part, 128), 1)

    def moves(h):
        out = [(6, 0, 2), (0, 127, 128)] if h == 2 else []
        for t in range(TILES):
            low, high = BASES * t - 1 - 128 * h, BASES * t - 1 + GROUP - 128 * h
            if h < 2 and high > 0 and low < 128:
                out.append((t, max(low, 0), min(high, 128)))
        return out

    def plane(z, carry):
        far = [[jnp.zeros((8, 128), F32)] * 3 for _ in range(3)]
        near = [[jnp.zeros((8, 128), F32)] * 3 for _ in range(3)]
        for r0 in range(0, XEXT, part):
            tiles = []
            for t in range(TILES):
                x = None
                for grid in grids:
                    for at in spots(t, z + 1):
                        y = grid[pl.ds(at + 2 * r0, part, stride=2), :]
                        x = y if x is None else x + y
                tiles.append(x)
            mcol = mxcol[r0 : r0 + part, :]
            wf, wn = wfar_ref[r0 : r0 + part, :], wnear_ref[r0 : r0 + part, :]
            r1 = r0 + part
            i0, i1 = max(r0, OFF), min(r1, OFF + 128)
            for c in range(3):
                turned = [pltpu.roll(tiles[t], (BASES * t - 1 - GROUP * c) % 128, 1) for t in range(TILES)]
                for h in range(3):
                    e = None
                    for t, low, high in moves(h):
                        x = turned[t]
                        if low > 0 or high < 128:
                            x = jnp.where((lanes >= low) & (lanes < high), x, 0.0)
                        e = x if e is None else e + x
                    e = e * mcol * mys[h]
                    if h < 2:
                        cols = slice(h * 128, (h + 1) * 128)
                        inner = e[i0 - r0 : i1 - r0] + vbuf[c, z, i0 - OFF : i1 - OFF, cols]
                        vbuf[c, z, i0 - OFF : i1 - OFF, cols] = inner
                        pieces = [e[0 : i0 - r0]] if i0 > r0 else []
                        pieces.append(inner)
                        if i1 < r1:
                            pieces.append(e[i1 - r0 :])
                        e = jnp.concatenate(pieces, axis=0) if len(pieces) > 1 else inner
                    ext[c, h, r0:r1, :] = e
                    far[c][h] = far[c][h] + jnp.sum((e * wf).reshape(part // 8, 8, 128), axis=0)
                    near[c][h] = near[c][h] + jnp.sum((e * wn).reshape(part // 8, 8, 128), axis=0)
        for c in range(3):
            p = c * 16 + z
            at = pl.multiple_of(p * 8, 8)
            for h in range(3):
                rowset = [
                    jnp.sum(far[c][h], axis=0, keepdims=True),
                    ext[c, h, OFF + 127 : OFF + 130, :],
                    jnp.sum(near[c][h], axis=0, keepdims=True),
                    ext[c, h, OFF : OFF + 1, :],
                    ext[c, h, OFF - 1 : OFF, :],
                    jnp.zeros((1, 128), F32),
                ]
                rlp[h, pl.ds(at, 8), :] = jnp.concatenate(rowset, axis=0)
            high, low = split(jnp.concatenate([ext[c, h, OFF : OFF + 128, :] for h in range(3)], axis=1))
            nt = (((1,), (1,)), ((), ()))
            one = lax.dot_general(pick_ref[...], high, nt, preferred_element_type=F32)
            two = lax.dot_general(pick_ref[...], low, nt, preferred_element_type=F32)
            udp[pl.ds(at, 8), :] = one[0:8] + one[8:16] + two[0:8]
        pltpu.make_async_copy(vbuf.at[:, z], e_hbm.at[:, z], e_sems.at[z]).start()
        return carry

    lax.fori_loop(0, 16, plane, 0)

    corner = jnp.zeros((48, 128), F32)
    kinds = jnp.minimum(lax.broadcasted_iota(jnp.int32, (384, 128), 1), 7)
    tail = edge_table(256, kinds, lax.broadcasted_iota(jnp.int32, (384, 128), 0))
    for t in range(7):
        row = jnp.concatenate([rlp[h, pl.ds(t, 48, stride=8), :] for h in range(3)], axis=1)
        rl_ref[t] = row[:, 0:256]
        ends = jnp.dot(row, tail, preferred_element_type=F32, precision=lax.Precision.HIGHEST)
        corner = corner + (pltpu.roll(ends, 8 * t, 1) if t else ends)
        ud_ref[t] = udp[pl.ds(t, 48, stride=8), :]
    rl_ref[7] = jnp.zeros((48, 256), F32)
    ud_ref[7] = jnp.zeros((48, 128), F32)
    cn_ref[...] = corner
    for z in range(16):
        pltpu.make_async_copy(vbuf.at[:, z], e_hbm.at[:, z], e_sems.at[z]).wait()


def spread(inbox, mx, my, v):
    rows = TILES * 2 * PAIRS * SPAN
    total = inbox.shape[0] * SLOTS
    vm = pl.BlockSpec(memory_space=VMEM)
    return pl.pallas_call(
        spread_kernel,
        out_shape=(
            jax.ShapeDtypeStruct(v.shape, F32),
            jax.ShapeDtypeStruct((8, 48, 256), F32),
            jax.ShapeDtypeStruct((48, 128), F32),
            jax.ShapeDtypeStruct((8, 48, 128), F32),
        ),
        in_specs=[vm] * 3 + [pl.BlockSpec(memory_space=pl.ANY)],
        out_specs=(pl.BlockSpec(memory_space=pl.ANY), vm, vm, vm),
        scratch_shapes=[VMEM((rows, 128), F32)] * COPIES
        + [
            VMEM(v.shape, F32),
            VMEM((8, total), F32),
            VMEM((1, total), jnp.int32),
            pltpu.SMEM((1, total), jnp.int32),
            VMEM((XEXT, 128), F32),
            VMEM((XEXT, 128), F32),
            VMEM((XEXT, 128), F32),
            VMEM((16, 384), BF16),
            VMEM((3, 3, XEXT, 128), F32),
            VMEM((3, 48 * 8, 128), F32),
            VMEM((48 * 8, 128), F32),
            pltpu.SemaphoreType.DMA,
            pltpu.SemaphoreType.DMA((16,)),
            pltpu.SemaphoreType.DMA,
        ],
        compiler_params=pltpu.CompilerParams(vmem_limit_bytes=45 << 20),
        cost_estimate=cost(100 << 20),
        name="spread",
    )(inbox, mx, my, v)


def exchange_kernel(
    rl_hbm, cn_hbm, ud_hbm, xh_ref, yh_ref, rl_ref, cn_ref, ud_ref,
    ra, ca, rb, cb, umsg, hmsg, pu, ph, qd, qh, own_sems, send_sems, recv_sems,
):
    pairs = ((cn_hbm, cn_ref), (ud_hbm, ud_ref), (rl_hbm, rl_ref))
    loads = [pltpu.make_async_copy(src, dst, own_sems.at[i]) for i, (src, dst) in enumerate(pairs)]
    for load in loads:
        load.start()
    gx, gy = lax.axis_index("gx"), lax.axis_index("gy")
    nx, ny = lax.axis_size("gx"), lax.axis_size("gy")
    right = (lax.rem(gx + 1, nx), gy)
    left = (lax.rem(gx + nx - 1, nx), gy)
    up = (gx, lax.rem(gy + 1, ny))
    down = (gx, lax.rem(gy + ny - 1, ny))
    barrier = pltpu.get_barrier_semaphore()
    for device in (right, left, up, down):
        pl.semaphore_signal(barrier, inc=1, device_id=device, device_id_type=MESH)
    pl.semaphore_wait(barrier, 4)

    def send(i, src, dst, device):
        copy = pltpu.make_async_remote_copy(
            src_ref=src, dst_ref=dst, send_sem=send_sems.at[i], recv_sem=recv_sems.at[i],
            device_id=device, device_id_type=MESH,
        )
        copy.start()
        return copy

    first = [
        send(0, cn_hbm, ca, right),
        send(1, cn_hbm, cb, left),
        send(2, rl_hbm.at[0:4], ra, right),
        send(3, rl_hbm.at[4:7], rb, left),
    ]
    planes = cn_ref.shape[0]
    lane = lax.broadcasted_iota(jnp.int32, (planes, 128), 1)
    for load in loads:
        load.wait()
    first[0].wait()
    first[1].wait()
    own, a, b = cn_ref[...], ca[...], cb[...]
    turn = lambda x, by: pltpu.roll(x, by % 128, 1)
    hold = jnp.where(lane < 8, a + turn(own, -48), a + turn(own, -40))
    hold = jnp.where(
        lane < 16, hold, turn(b, -16) + jnp.where(lane < 24, own + ROOT * turn(own, -8), turn(own, 8))
    )
    hmsg[...] = jnp.where(lane < 32, hold, 0.0)
    for s in range(7):
        umsg[s] = (
            ud_ref[s]
            + jnp.where(lane == 0, a[:, 16 + s : 17 + s], 0.0)
            + jnp.where(lane == 1, a[:, 24 + s : 25 + s], 0.0)
            + jnp.where(lane == 127, b[:, 48 + s : 49 + s], 0.0)
        )
    second = [
        send(4, hmsg, ph, up),
        send(5, hmsg, qh, down),
        send(6, umsg.at[0:4], pu, up),
        send(7, umsg.at[4:7], qd, down),
    ]
    first[2].wait()
    first[3].wait()
    second[0].wait()
    second[1].wait()
    lane = lax.broadcasted_iota(jnp.int32, (planes, 256), 1)
    p, q = ph[...], qh[...]

    def rims(h):
        return (
            jnp.where(lane == 0, p[:, 8 * h + 2 : 8 * h + 3], 0.0)
            + jnp.where(lane == 1, p[:, 8 * h + 3 : 8 * h + 4], 0.0)
            + jnp.where(lane == 255, q[:, 8 * h + 6 : 8 * h + 7], 0.0)
        )

    def put(t, value):
        for h in range(2):
            xh_ref[h, pl.ds(t, planes, stride=8), :] = value[:, h * 128 : (h + 1) * 128]

    put(0, ra[0] + rl_ref[6] + rims(0))
    put(1, ra[1] + rl_ref[6] + rims(1))
    put(2, rb[0] + rl_ref[2] + ROOT * rl_ref[3] + rims(2))
    put(3, rb[1] + rl_ref[2] + rims(3))
    put(4, ra[2])
    put(5, ra[3])
    put(6, rb[2])
    put(7, jnp.zeros((planes, 256), F32))
    second[2].wait()
    second[3].wait()
    yh_ref[pl.ds(0, planes, stride=8), :] = pu[0] + umsg[6]
    yh_ref[pl.ds(1, planes, stride=8), :] = pu[1] + umsg[6]
    yh_ref[pl.ds(2, planes, stride=8), :] = qd[0] + umsg[2] + ROOT * umsg[3]
    yh_ref[pl.ds(3, planes, stride=8), :] = qd[1] + umsg[2]
    yh_ref[pl.ds(4, planes, stride=8), :] = pu[2]
    yh_ref[pl.ds(5, planes, stride=8), :] = pu[3]
    yh_ref[pl.ds(6, planes, stride=8), :] = qd[2]
    yh_ref[pl.ds(7, planes, stride=8), :] = jnp.zeros((planes, 128), F32)


def exchange(rl, cn, ud):
    n = cn.shape[0]
    vm = pl.BlockSpec(memory_space=VMEM)
    return pl.pallas_call(
        exchange_kernel,
        out_shape=(jax.ShapeDtypeStruct((2, 8 * n, 128), F32), jax.ShapeDtypeStruct((8 * n, 128), F32)),
        in_specs=[pl.BlockSpec(memory_space=pl.ANY)] * 3,
        out_specs=(vm, vm),
        scratch_shapes=[
            VMEM((8, n, 256), F32),
            VMEM((n, 128), F32),
            VMEM((8, n, 128), F32),
            VMEM((4, n, 256), F32),
            VMEM((n, 128), F32),
            VMEM((3, n, 256), F32),
            VMEM((n, 128), F32),
            VMEM((7, n, 128), F32),
            VMEM((n, 128), F32),
            VMEM((4, n, 128), F32),
            VMEM((n, 128), F32),
            VMEM((3, n, 128), F32),
            VMEM((n, 128), F32),
            pltpu.SemaphoreType.DMA((3,)),
            pltpu.SemaphoreType.DMA((8,)),
            pltpu.SemaphoreType.DMA((8,)),
        ],
        compiler_params=pltpu.CompilerParams(vmem_limit_bytes=8 << 20, collective_id=0, has_side_effects=True),
        cost_estimate=cost(30 << 20),
        name="exchange",
    )(rl, cn, ud)


def derive_kernel(e_ref, xh_ref, yh_ref, mx_ref, my_ref, kx_ref, ky_ref, kl_ref, rim_ref, dx_ref, dy_ref, mxcol, myrow):
    @pl.when(pl.program_id(0) == 0)
    def _():
        gx, gy = lax.axis_index("gx"), lax.axis_index("gy")
        mxcol[...] = row_as_column(mx_ref[pl.ds(gx, 1), :])
        myrow[:, 0:128] = jnp.broadcast_to(my_ref[pl.ds(2 * gy, 1), :], (8, 128))
        myrow[:, 128:256] = jnp.broadcast_to(my_ref[pl.ds(2 * gy + 1, 1), :], (8, 128))

    each = e_ref.shape[0]
    zero = jnp.zeros((1, 256), F32)
    col = mxcol[...]
    yall = jnp.concatenate([yh_ref[i * 8 : i * 8 + 8, :] for i in range(each)], axis=1)
    high = yall.astype(BF16).astype(F32)
    stack = jnp.concatenate([high, yall - high, high, jnp.zeros_like(high)], axis=0).astype(BF16)
    extra = lax.dot_general(stack, rim_ref[...], (((0,), (0,)), ((), ())), preferred_element_type=F32)
    highs, lows = [], []
    for i in range(each):
        xall = jnp.concatenate([xh_ref[0, i * 8 : i * 8 + 8, :], xh_ref[1, i * 8 : i * 8 + 8, :]], axis=1)
        top = jnp.concatenate([xall[4:6]] + [zero] * 6, axis=0)
        low = jnp.concatenate([zero] * 7 + [xall[6:7]], axis=0)
        e = e_ref[i]
        f = jnp.concatenate([e[0:8] + top, e[8:120], e[120:128] + low], axis=0)
        f = f + extra[i * 128 : (i + 1) * 128, 256:512]
        halo = jnp.concatenate([xall[0:4]] + [zero] * 12, axis=0)
        fh, fl = split(f)
        hh, hl = split(halo)
        highs.append(fh)
        lows.append(fl)
        one = dot(kx_ref[...], jnp.concatenate([fh, hh], axis=0))
        dx = one[0:128] + one[128:256] + dot(kx_ref[0:128], jnp.concatenate([fl, hl], axis=0))
        dx_ref[i, :, 0:128] = dx[:, 0:128] * col
        dx_ref[i, :, 128:256] = dx[:, 128:256] * col
    two = dot(jnp.concatenate(highs + lows, axis=0), ky_ref[...])
    n = each * 128
    dy = two[0:n] + two[n : 2 * n] + dot(jnp.concatenate(highs, axis=0), kl_ref[...]) + extra[:, 0:256]
    dy_ref[...] = (dy * myrow[0:1, :]).reshape(dy_ref.shape)


def derive(e, xh, yh, mx, my):
    n, rows, cols = e.shape
    each = EACH
    kx = np.zeros((rows, 144))
    kx[:, 0:rows] = line_matrix(rows)
    kx[:, rows : rows + 4] = halo_columns(rows)
    kx = np.concatenate(halves(kx), axis=0)
    kh, kl = halves(line_matrix(cols).T)
    rim = np.zeros((8, 512))
    rim[0:4, 0:256] = halo_columns(cols).T
    rim[4, 256] = 1.0
    rim[5, 257] = 1.0
    rim[6, 511] = 1.0
    rh, rlow = halves(rim)
    rim = np.concatenate([rh, rh, rlow, np.zeros((8, 512), BF16)], axis=0)
    whole = lambda x: pl.BlockSpec(x.shape, lambda i: (0,) * x.ndim)
    block = pl.BlockSpec((each, rows, cols), lambda i: (i, 0, 0))
    consts = (kx, kh, kl, rim)
    xspec = pl.BlockSpec((2, each * 8, 128), lambda i: (0, i, 0))
    yspec = pl.BlockSpec((each * 8, 128), lambda i: (i, 0))
    return pl.pallas_call(
        derive_kernel,
        grid=(n // each,),
        out_shape=(jax.ShapeDtypeStruct(e.shape, F32),) * 2,
        in_specs=[block, xspec, yspec] + [whole(x) for x in (mx, my) + consts],
        out_specs=(block, block),
        scratch_shapes=[VMEM((128, 128), F32), VMEM((8, 256), F32)],
        compiler_params=pltpu.CompilerParams(vmem_limit_bytes=30 << 20),
        cost_estimate=cost(30 << 20),
        name="derive",
    )(e, xh, yh, mx, my, *consts)


def local(
    velocity, metric_x, metric_y, marker_force, marker_frac, marker_cell_x, marker_cell_y, marker_cell_z, send_counts
):
    comps, planes, rows, cols = velocity.shape
    fold = lambda x: x.reshape(-1, 128)
    cells = [fold(x) for x in (marker_cell_x, marker_cell_y, marker_cell_z)]
    outbox = pack(send_counts, marker_force, marker_frac, *cells)
    inbox = shuffle(outbox).reshape(-1, 1, 256)
    mx, my = fold(metric_x), fold(metric_y)
    e, rl, cn, ud = spread(inbox, mx, my, velocity)
    xh, yh = exchange(rl, cn, ud)
    dx, dy = derive(e.reshape(comps * planes, rows, cols), xh, yh, mx, my)
    return dx.reshape(velocity.shape), dy.reshape(velocity.shape)


def solution(mesh):
    both = ("gx", "gy")
    placed = (
        P(None, None, "gx", "gy"), P(), P(), P(None, both), P(None, both), P(both), P(both), P(both), P(both, None),
    )
    return jax.shard_map(
        local,
        mesh=mesh,
        in_specs=placed,
        out_specs=(P(None, None, "gx", "gy"), P(None, None, "gx", "gy")),
        check_vma=False,
    )
```

```python
import functools
import math

import jax
import jax.numpy as jnp
import numpy as np
from jax import lax
from jax.experimental import pallas as pl
from jax.experimental.pallas import tpu as pltpu
from jax.sharding import PartitionSpec as P

SLOTS = 32
HALF = 0.5
GROUP = 42
BASES = 39
OFF = 8
XEXT = 144
PAIRS = 9
SPAN = 2 * XEXT
EACH = 12
METRIC = 8
UNROLL = 4
TOGETHER = 4
TILES = 7
COPIES = 2
ROOT = (math.sqrt(5.0) - 3.0) / 2.0
MESH = pl.DeviceIdType.MESH
VMEM = pltpu.VMEM
F32 = jnp.float32
BF16 = jnp.bfloat16


SCALE = 1.0 / (1.0 + 2.0 * ROOT / 3.0)
LEAD = SCALE * (7.0 / 9.0 * (1.0 / ROOT - ROOT) + 1.0 / 36.0 * (1.0 / ROOT**2 - ROOT**2))
NEAR = SCALE / 36.0 * (ROOT - 1.0 / ROOT)


def line_matrix(n):
    gap = np.arange(n)[None, :] - np.arange(n)[:, None]
    out = np.sign(gap) * LEAD * ROOT ** np.abs(gap).astype(np.float64)
    return out + np.where(np.abs(gap) == 1, np.sign(gap) * NEAR, 0.0)


def halo_columns(n):
    out = np.zeros((n, 4))
    steps = np.arange(n)
    out[:, 0] = -LEAD * ROOT ** (steps + 1.0)
    out[0, 1] = -NEAR
    out[:, 2] = LEAD * ROOT ** (n - steps * 1.0)
    out[n - 1, 3] = NEAR
    return out


def halves(values):
    values = np.asarray(values, np.float32)
    high = values.astype(BF16)
    low = (values - high.astype(np.float32)).astype(BF16)
    return high, low


def split(x):
    high = x.astype(BF16)
    return high, (x - high.astype(F32)).astype(BF16)


def dot(a, b):
    return jnp.dot(a, b, preferred_element_type=F32)


def cost(size):
    return pl.CostEstimate(flops=0, bytes_accessed=size, transcendentals=0)


def pack_kernel(counts_ref, force_ref, frac_ref, cx_ref, cy_ref, cz_ref, out_ref, wide):
    size = force_ref.shape[1]
    wide[0:3, 0:size] = force_ref[...]
    wide[3:6, 0:size] = frac_ref[...]
    code = ((cx_ref[...] * 256 + cy_ref[...]) * 16 + cz_ref[...]).astype(F32)
    for i in range(size // 128):
        wide[6:7, i * 128 : (i + 1) * 128] = code[i : i + 1]
    wide[7:8, 0:size] = jnp.zeros((1, size), F32)
    wide[:, size:] = jnp.zeros((8, wide.shape[1] - size), F32)
    lane = lax.broadcasted_iota(jnp.int32, (8, 128), 1)
    sub = lax.broadcasted_iota(jnp.int32, (8, 128), 0)
    part = sub & 3
    unused = jnp.where((sub == 6) & (lane < SLOTS), lane * (4 << 12), 0).astype(F32)

    def one(d, start):
        count = counts_ref[0, d]
        first = pl.multiple_of((start >> 7) << 7, 128)
        shift = start & 127
        back = (128 - shift) & 127
        a = pltpu.roll(wide[:, pl.ds(first, 128)], back, 1)
        b = pltpu.roll(wide[:, pl.ds(first + 128, 128)], back, 1)
        w = jnp.where(lane + shift < 128, a, b)
        w = jnp.where(lane < count, w, unused)
        m = w
        for j in range(1, 4):
            m = jnp.where(part == j, pltpu.roll(w, SLOTS * j, 1), m)
        top = jnp.sum(jnp.where(sub < 4, m, 0.0), axis=0, keepdims=True)
        low = jnp.sum(jnp.where(sub < 4, 0.0, m), axis=0, keepdims=True)
        return start + count, jnp.concatenate([top, low], axis=1)

    def several(g, start):
        for j in range(UNROLL):
            for k in range(8):
                start, out_ref[k, g * UNROLL + j] = one((g * UNROLL + j) * 8 + k, start)
        return start

    lax.fori_loop(0, out_ref.shape[1] // UNROLL, several, jnp.int32(0))


def pack(counts, *fields):
    vm = pl.BlockSpec(memory_space=VMEM)
    return pl.pallas_call(
        pack_kernel,
        out_shape=jax.ShapeDtypeStruct((8, counts.shape[1] // 8, 1, 256), F32),
        in_specs=[pl.BlockSpec(memory_space=pltpu.SMEM)] + [vm] * 5,
        out_specs=vm,
        scratch_shapes=[VMEM((8, fields[0].shape[1] + 256), F32)],
        cost_estimate=cost(12 << 20),
        name="pack",
    )(counts, *fields)


def shuffle_kernel(out_ref, mx_ref, my_ref, in_ref, mid, own_sems, send_y, recv_y, send_x, recv_x):
    gx, gy = lax.axis_index("gx"), lax.axis_index("gy")
    nx, ny = lax.axis_size("gx"), lax.axis_size("gy")
    own = pltpu.make_async_copy(out_ref.at[gy], mid.at[gy], own_sems.at[0])
    own.start()
    metrics = [
        pltpu.make_async_copy(src, in_ref.at[nx + i], own_sems.at[2 + i]) for i, src in enumerate((mx_ref, my_ref))
    ]
    for copy in metrics:
        copy.start()
    barrier = pltpu.get_barrier_semaphore()
    for k in range(1, ny):
        pl.semaphore_signal(barrier, inc=1, device_id=(gx, lax.rem(gy + k, ny)), device_id_type=MESH)
    for k in range(1, nx):
        pl.semaphore_signal(barrier, inc=1, device_id=(lax.rem(gx + k, nx), gy), device_id_type=MESH)
    pl.semaphore_wait(barrier, nx + ny - 2)
    copies = []
    for k in range(1, ny):
        peer = lax.rem(gy + k, ny)
        copy = pltpu.make_async_remote_copy(
            src_ref=out_ref.at[peer], dst_ref=mid.at[gy], send_sem=send_y.at[k], recv_sem=recv_y.at[k],
            device_id=(gx, peer), device_id_type=MESH,
        )
        copy.start()
        copies.append(copy)
    own.wait()
    for copy in copies:
        copy.wait()
    own = pltpu.make_async_copy(mid.at[:, gx], in_ref.at[gx], own_sems.at[1])
    own.start()
    copies = []
    for k in range(1, nx):
        peer = lax.rem(gx + k, nx)
        copy = pltpu.make_async_remote_copy(
            src_ref=mid.at[:, peer], dst_ref=in_ref.at[gx], send_sem=send_x.at[k], recv_sem=recv_x.at[k],
            device_id=(peer, gy), device_id_type=MESH,
        )
        copy.start()
        copies.append(copy)
    own.wait()
    for copy in copies + metrics:
        copy.wait()


def shuffle(outbox, mx, my):
    ny, nx = outbox.shape[0:2]
    anywhere = pl.BlockSpec(memory_space=pl.ANY)
    dma = pltpu.SemaphoreType.DMA
    return pl.pallas_call(
        shuffle_kernel,
        out_shape=jax.ShapeDtypeStruct((nx + 2, ny, 1, 256), F32),
        in_specs=[anywhere] * 3,
        out_specs=anywhere,
        scratch_shapes=[VMEM((ny, nx, 1, 256), F32), dma((4,)), dma((ny,)), dma((ny,)), dma((nx,)), dma((nx,))],
        compiler_params=pltpu.CompilerParams(collective_id=1, has_side_effects=True),
        cost_estimate=cost(36 << 20),
        name="shuffle",
    )(outbox, mx, my)


def row_as_column(row):
    return jnp.transpose(jnp.broadcast_to(row, (128, 128)))


def stencil_weights(t):
    root = jnp.sqrt(jnp.maximum(1.0 + 4.0 * t - 4.0 * t * t, 0.0))
    return (
        (3.0 - 2.0 * t - root) / 8.0,
        (3.0 - 2.0 * t + root) / 8.0,
        (1.0 + 2.0 * t + root) / 8.0,
        (1.0 + 2.0 * t - root) / 8.0,
    )


def powers(steps):
    size = jnp.exp(steps.astype(F32) * math.log(-ROOT))
    return jnp.where((steps & 1) == 1, -size, size)


def edge_table(n, kinds, spots):
    inside = (spots >= 0) & (spots < n)
    steps = jnp.where(kinds == 0, n - 1 - spots, spots)
    sums = jnp.where(inside & ((kinds == 0) | (kinds == 4)), powers(jnp.where(inside, steps, 0)), 0.0)
    only = jnp.where(kinds < 4, n - 2 + kinds, jnp.where(kinds == 5, 0, n + 127))
    single = (kinds != 0) & (kinds != 4) & (kinds < 7) & (spots == only)
    return jnp.where(single, 1.0, sums)


def spread_kernel(
    inbox_ref, v_hbm,
    e_hbm, rl_ref, cn_ref, ud_ref,
    *scratch,
):
    grids = scratch[:COPIES]
    vbuf, m8, base_v, base_s, mxcol, wfar_ref, wnear_ref, pick_ref, ext, rlp, udp, v_sem, e_sems, s_sem = scratch[COPIES:]
    gx, gy = lax.axis_index("gx"), lax.axis_index("gy")
    messages = inbox_ref.shape[0] - 2 * METRIC
    chunks = messages * SLOTS // 128
    vin = pltpu.make_async_copy(v_hbm, vbuf, v_sem)
    vin.start()
    lane = lax.broadcasted_iota(jnp.int32, (8, 128), 1)
    sub = lax.broadcasted_iota(jnp.int32, (8, 128), 0)

    def regroup(g):
        out = None
        for k in range(4):
            row = inbox_ref[g * 4 + k]
            x = jnp.where(
                sub < 4, jnp.broadcast_to(row[:, 0:128], (8, 128)), jnp.broadcast_to(row[:, 128:256], (8, 128))
            )
            y = x
            for j in range(4):
                turn = (SLOTS * (k - j)) % 128
                z = pltpu.roll(x, turn, 1) if turn else x
                y = jnp.where((sub & 3) == j, z, y)
            out = y if out is None else jnp.where((lane >> 5) == k, y, out)
        at = g * 128 if isinstance(g, int) else pl.multiple_of(g * 128, 128)
        m8[:, pl.ds(at, 128)] = out
        code = out[6:7].astype(jnp.int32)
        tile = (((code >> 4) & 255) * 1681) >> 16
        pair = (2 * tile + (code & 1)) * PAIRS + ((code & 15) >> 1)
        base_v[:, pl.ds(at, 128)] = pair * SPAN + 2 * ((code >> 12) + OFF - 1)

    rows = grids[0].shape[0]
    share = 8 * (-(-rows // (8 * chunks)))
    full = rows // share

    def regroup_and_clear(g, carry):
        for grid in grids:
            grid[pl.ds(pl.multiple_of(g * share, 8), share), :] = jnp.zeros((share, 128), F32)
        regroup(g)
        return carry

    lax.fori_loop(0, full, regroup_and_clear, 0)
    for grid in grids:
        if full * share < rows:
            grid[full * share : rows, :] = jnp.zeros((rows - full * share, 128), F32)
    for g in range(full, chunks):
        regroup(g)
    bcopy = pltpu.make_async_copy(base_v, base_s, s_sem)
    bcopy.start()
    bcopy.wait()

    sub2 = lax.broadcasted_iota(jnp.int32, (128, 128), 0)
    comp = jnp.where(sub2 >= 2 * GROUP, 2, jnp.where(sub2 >= GROUP, 1, 0))
    rel = jnp.where(sub2 >= 3 * GROUP, -100, sub2 - GROUP * comp)

    def tables(c):
        m = m8[:, pl.ds(pl.multiple_of(c * 128, 128), 128)]
        ws = stencil_weights(m)
        code = m[6:7].astype(jnp.int32)
        cell_y = (code >> 4) & 255
        inner = cell_y - BASES * ((cell_y * 1681) >> 16)
        d = rel - inner
        w = jnp.where(d == 0, ws[0][4:5], 0.0)
        w = jnp.where(d == 1, ws[1][4:5], w)
        w = jnp.where(d == 2, ws[2][4:5], w)
        w = jnp.where(d == 3, ws[3][4:5], w)
        f = jnp.where(comp == 0, m[0:1], jnp.where(comp == 1, m[1:2], m[2:3]))
        wx8 = jnp.concatenate([ws[i // 2][3:4] for i in range(8)], axis=0)
        sides = ((ws[0][5:6], ws[1][5:6]), (ws[2][5:6], ws[3][5:6]))
        tall = [wx8 * jnp.concatenate(list(side) * 4, axis=0) for side in sides]
        return jnp.transpose(w * f), tall

    def chunk(i, carry):
        built = [tables(i * TOGETHER + j) for j in range(TOGETHER)]
        for j, (fr, tall) in enumerate(built):
            bs = [base_s[0, (i * TOGETHER + j) * 128 + k] for k in range(128)]
            for k0 in range(0, 128, COPIES):
                group = []
                for k in range(k0, k0 + COPIES):
                    grid = grids[k % COPIES]
                    for q in range(2):
                        at = bs[k] + q * SPAN
                        group.append((grid, at, grid[pl.ds(at, 8), :] + tall[q][:, k : k + 1] * fr[k : k + 1, :]))
                for grid, at, value in group:
                    grid[pl.ds(at, 8), :] = value
        return carry

    lax.fori_loop(0, chunks // TOGETHER, chunk, 0)

    def spots(t, e, odds=(0, 1)):
        return [(2 * t + odd) * PAIRS * SPAN + ((e - odd) >> 1) * SPAN + ((e - odd) & 1) for odd in odds]

    for t in range(TILES):
        for src, odds, dst in ((0, (0,), 16), (17, (0, 1), 1), (18, (1,), 2)):
            moved = None
            for grid in grids:
                for at in spots(t, src, odds):
                    x = grid[pl.ds(at, XEXT, stride=2), :]
                    moved = x if moved is None else moved + x
            here = pl.ds(spots(t, dst)[0], XEXT, stride=2)
            grids[0][here, :] = grids[0][here, :] + moved

    def along_x(i):
        i = lax.rem(i, 2 * METRIC)
        pair = inbox_ref[messages + (i >> 1)]
        return row_as_column(jnp.where((i & 1) == 1, pair[:, 128:256], pair[:, 0:128]))

    def along_y(i):
        return inbox_ref[messages + METRIC + lax.rem(i, METRIC)]

    mxcol[0:OFF, :] = along_x(gx + 2 * METRIC - 1)[128 - OFF : 128]
    mxcol[OFF : OFF + 128, :] = along_x(gx)
    mxcol[OFF + 128 : XEXT, :] = along_x(gx + 1)[0 : XEXT - OFF - 128]
    after = along_y(gy + 1)[:, 0:128]
    before = along_y(gy + METRIC - 1)[:, 128:256]
    here = along_y(gy)
    lane1 = lax.broadcasted_iota(jnp.int32, (1, 128), 1)
    rim = jnp.where(lane1 < 2, after, jnp.where(lane1 == 127, before, 0.0))
    mys = [HALF * here[:, 0:128], HALF * here[:, 128:256], HALF * rim]
    at = lax.broadcasted_iota(jnp.int32, (XEXT, 128), 0) - OFF
    wfar_ref[...] = edge_table(128, 0, at)
    wnear_ref[...] = edge_table(128, 4, at)
    kinds = lax.broadcasted_iota(jnp.int32, (8, 384), 0)
    high, low = split(edge_table(256, kinds, lax.broadcasted_iota(jnp.int32, (8, 384), 1)))
    pick_ref[...] = jnp.concatenate([high.astype(F32), low.astype(F32)], axis=0).astype(BF16)
    vin.wait()

    part = 48
    lanes = lax.broadcasted_iota(jnp.int32, (part, 128), 1)

    def moves(h):
        out = [(6, 0, 2), (0, 127, 128)] if h == 2 else []
        for t in range(TILES):
            low, high = BASES * t - 1 - 128 * h, BASES * t - 1 + GROUP - 128 * h
            if h < 2 and high > 0 and low < 128:
                out.append((t, max(low, 0), min(high, 128)))
        return out

    def plane(z, carry):
        far = [[jnp.zeros((8, 128), F32)] * 3 for _ in range(3)]
        near = [[jnp.zeros((8, 128), F32)] * 3 for _ in range(3)]
        for r0 in range(0, XEXT, part):
            tiles = []
            for t in range(TILES):
                x = None
                for grid in grids:
                    for at in spots(t, z + 1):
                        y = grid[pl.ds(at + 2 * r0, part, stride=2), :]
                        x = y if x is None else x + y
                tiles.append(x)
            mcol = mxcol[r0 : r0 + part, :]
            wf, wn = wfar_ref[r0 : r0 + part, :], wnear_ref[r0 : r0 + part, :]
            r1 = r0 + part
            i0, i1 = max(r0, OFF), min(r1, OFF + 128)
            for c in range(3):
                turned = [pltpu.roll(tiles[t], (BASES * t - 1 - GROUP * c) % 128, 1) for t in range(TILES)]
                for h in range(3):
                    e = None
                    for t, low, high in moves(h):
                        x = turned[t]
                        if low > 0 or high < 128:
                            x = jnp.where((lanes >= low) & (lanes < high), x, 0.0)
                        e = x if e is None else e + x
                    e = e * mcol * mys[h]
                    if h < 2:
                        cols = slice(h * 128, (h + 1) * 128)
                        inner = e[i0 - r0 : i1 - r0] + vbuf[c, z, i0 - OFF : i1 - OFF, cols]
                        vbuf[c, z, i0 - OFF : i1 - OFF, cols] = inner
                        pieces = [e[0 : i0 - r0]] if i0 > r0 else []
                        pieces.append(inner)
                        if i1 < r1:
                            pieces.append(e[i1 - r0 :])
                        e = jnp.concatenate(pieces, axis=0) if len(pieces) > 1 else inner
                    ext[c, h, r0:r1, :] = e
                    far[c][h] = far[c][h] + jnp.sum((e * wf).reshape(part // 8, 8, 128), axis=0)
                    near[c][h] = near[c][h] + jnp.sum((e * wn).reshape(part // 8, 8, 128), axis=0)
        for c in range(3):
            p = c * 16 + z
            at = pl.multiple_of(p * 8, 8)
            for h in range(3):
                rowset = [
                    jnp.sum(far[c][h], axis=0, keepdims=True),
                    ext[c, h, OFF + 127 : OFF + 130, :],
                    jnp.sum(near[c][h], axis=0, keepdims=True),
                    ext[c, h, OFF : OFF + 1, :],
                    ext[c, h, OFF - 1 : OFF, :],
                    jnp.zeros((1, 128), F32),
                ]
                rlp[h, pl.ds(at, 8), :] = jnp.concatenate(rowset, axis=0)
            high, low = split(jnp.concatenate([ext[c, h, OFF : OFF + 128, :] for h in range(3)], axis=1))
            nt = (((1,), (1,)), ((), ()))
            one = lax.dot_general(pick_ref[...], high, nt, preferred_element_type=F32)
            two = lax.dot_general(pick_ref[...], low, nt, preferred_element_type=F32)
            udp[pl.ds(at, 8), :] = one[0:8] + one[8:16] + two[0:8]
        pltpu.make_async_copy(vbuf.at[:, z], e_hbm.at[:, z], e_sems.at[z]).start()
        return carry

    lax.fori_loop(0, 16, plane, 0)

    corner = jnp.zeros((48, 128), F32)
    kinds = jnp.minimum(lax.broadcasted_iota(jnp.int32, (384, 128), 1), 7)
    tail = edge_table(256, kinds, lax.broadcasted_iota(jnp.int32, (384, 128), 0))
    lines = []
    for t in range(7):
        row = jnp.concatenate([rlp[h, pl.ds(t, 48, stride=8), :] for h in range(3)], axis=1)
        rl_ref[t] = row[:, 0:256]
        ud_ref[t] = udp[pl.ds(t, 48, stride=8), :]
        lines.append(row)
    lines = jnp.concatenate(lines, axis=0)
    ends = jnp.dot(lines, tail, preferred_element_type=F32, precision=lax.Precision.HIGHEST)
    for t in range(7):
        end = ends[t * 48 : (t + 1) * 48]
        corner = corner + (pltpu.roll(end, 8 * t, 1) if t else end)
    rl_ref[7] = jnp.zeros((48, 256), F32)
    ud_ref[7] = jnp.zeros((48, 128), F32)
    cn_ref[...] = corner
    for z in range(16):
        pltpu.make_async_copy(vbuf.at[:, z], e_hbm.at[:, z], e_sems.at[z]).wait()


def spread(inbox, v):
    rows = TILES * 2 * PAIRS * SPAN + 8
    total = (inbox.shape[0] - 2 * METRIC) * SLOTS
    vm = pl.BlockSpec(memory_space=VMEM)
    return pl.pallas_call(
        spread_kernel,
        out_shape=(
            jax.ShapeDtypeStruct(v.shape, F32),
            jax.ShapeDtypeStruct((8, 48, 256), F32),
            jax.ShapeDtypeStruct((48, 128), F32),
            jax.ShapeDtypeStruct((8, 48, 128), F32),
        ),
        in_specs=[vm] + [pl.BlockSpec(memory_space=pl.ANY)],
        out_specs=(pl.BlockSpec(memory_space=pl.ANY), vm, vm, vm),
        scratch_shapes=[VMEM((rows, 128), F32)] * COPIES
        + [
            VMEM(v.shape, F32),
            VMEM((8, total), F32),
            VMEM((1, total), jnp.int32),
            pltpu.SMEM((1, total), jnp.int32),
            VMEM((XEXT, 128), F32),
            VMEM((XEXT, 128), F32),
            VMEM((XEXT, 128), F32),
            VMEM((16, 384), BF16),
            VMEM((3, 3, XEXT, 128), F32),
            VMEM((3, 48 * 8, 128), F32),
            VMEM((48 * 8, 128), F32),
            pltpu.SemaphoreType.DMA,
            pltpu.SemaphoreType.DMA((16,)),
            pltpu.SemaphoreType.DMA,
        ],
        compiler_params=pltpu.CompilerParams(vmem_limit_bytes=45 << 20),
        cost_estimate=cost(100 << 20),
        name="spread",
    )(inbox, v)


def exchange_kernel(
    rl_hbm, cn_hbm, ud_hbm, xh_ref, yh_ref, rl_ref, cn_ref, ud_ref,
    ra, ca, rb, cb, umsg, hmsg, pu, ph, qd, qh, own_sems, send_sems, recv_sems,
):
    pairs = ((cn_hbm, cn_ref), (ud_hbm, ud_ref), (rl_hbm, rl_ref))
    loads = [pltpu.make_async_copy(src, dst, own_sems.at[i]) for i, (src, dst) in enumerate(pairs)]
    for load in loads:
        load.start()
    gx, gy = lax.axis_index("gx"), lax.axis_index("gy")
    nx, ny = lax.axis_size("gx"), lax.axis_size("gy")
    right = (lax.rem(gx + 1, nx), gy)
    left = (lax.rem(gx + nx - 1, nx), gy)
    up = (gx, lax.rem(gy + 1, ny))
    down = (gx, lax.rem(gy + ny - 1, ny))
    barrier = pltpu.get_barrier_semaphore()
    for device in (right, left, up, down):
        pl.semaphore_signal(barrier, inc=1, device_id=device, device_id_type=MESH)
    pl.semaphore_wait(barrier, 4)

    def send(i, src, dst, device):
        copy = pltpu.make_async_remote_copy(
            src_ref=src, dst_ref=dst, send_sem=send_sems.at[i], recv_sem=recv_sems.at[i],
            device_id=device, device_id_type=MESH,
        )
        copy.start()
        return copy

    first = [
        send(0, cn_hbm, ca, right),
        send(1, cn_hbm, cb, left),
        send(2, rl_hbm.at[0:4], ra, right),
        send(3, rl_hbm.at[4:7], rb, left),
    ]
    planes = cn_ref.shape[0]
    lane = lax.broadcasted_iota(jnp.int32, (planes, 128), 1)
    for load in loads:
        load.wait()
    first[0].wait()
    first[1].wait()
    own, a, b = cn_ref[...], ca[...], cb[...]
    turn = lambda x, by: pltpu.roll(x, by % 128, 1)
    hold = jnp.where(lane < 8, a + turn(own, -48), a + turn(own, -40))
    hold = jnp.where(
        lane < 16, hold, turn(b, -16) + jnp.where(lane < 24, own + ROOT * turn(own, -8), turn(own, 8))
    )
    hmsg[...] = jnp.where(lane < 32, hold, 0.0)
    for s in range(7):
        umsg[s] = (
            ud_ref[s]
            + jnp.where(lane == 0, a[:, 16 + s : 17 + s], 0.0)
            + jnp.where(lane == 1, a[:, 24 + s : 25 + s], 0.0)
            + jnp.where(lane == 127, b[:, 48 + s : 49 + s], 0.0)
        )
    second = [
        send(4, hmsg, ph, up),
        send(5, hmsg, qh, down),
        send(6, umsg.at[0:4], pu, up),
        send(7, umsg.at[4:7], qd, down),
    ]
    first[2].wait()
    first[3].wait()
    second[0].wait()
    second[1].wait()
    lane = lax.broadcasted_iota(jnp.int32, (planes, 256), 1)
    p, q = ph[...], qh[...]

    def rims(h):
        return (
            jnp.where(lane == 0, p[:, 8 * h + 2 : 8 * h + 3], 0.0)
            + jnp.where(lane == 1, p[:, 8 * h + 3 : 8 * h + 4], 0.0)
            + jnp.where(lane == 255, q[:, 8 * h + 6 : 8 * h + 7], 0.0)
        )

    def put(t, value):
        for h in range(2):
            xh_ref[h, pl.ds(t, planes, stride=8), :] = value[:, h * 128 : (h + 1) * 128]

    put(0, ra[0] + rl_ref[6] + rims(0))
    put(1, ra[1] + rl_ref[6] + rims(1))
    put(2, rb[0] + rl_ref[2] + ROOT * rl_ref[3] + rims(2))
    put(3, rb[1] + rl_ref[2] + rims(3))
    put(4, ra[2])
    put(5, ra[3])
    put(6, rb[2])
    put(7, jnp.zeros((planes, 256), F32))
    second[2].wait()
    second[3].wait()
    yh_ref[pl.ds(0, planes, stride=8), :] = pu[0] + umsg[6]
    yh_ref[pl.ds(1, planes, stride=8), :] = pu[1] + umsg[6]
    yh_ref[pl.ds(2, planes, stride=8), :] = qd[0] + umsg[2] + ROOT * umsg[3]
    yh_ref[pl.ds(3, planes, stride=8), :] = qd[1] + umsg[2]
    yh_ref[pl.ds(4, planes, stride=8), :] = pu[2]
    yh_ref[pl.ds(5, planes, stride=8), :] = pu[3]
    yh_ref[pl.ds(6, planes, stride=8), :] = qd[2]
    yh_ref[pl.ds(7, planes, stride=8), :] = jnp.zeros((planes, 128), F32)


def exchange(rl, cn, ud):
    n = cn.shape[0]
    vm = pl.BlockSpec(memory_space=VMEM)
    return pl.pallas_call(
        exchange_kernel,
        out_shape=(jax.ShapeDtypeStruct((2, 8 * n, 128), F32), jax.ShapeDtypeStruct((8 * n, 128), F32)),
        in_specs=[pl.BlockSpec(memory_space=pl.ANY)] * 3,
        out_specs=(vm, vm),
        scratch_shapes=[
            VMEM((8, n, 256), F32),
            VMEM((n, 128), F32),
            VMEM((8, n, 128), F32),
            VMEM((4, n, 256), F32),
            VMEM((n, 128), F32),
            VMEM((3, n, 256), F32),
            VMEM((n, 128), F32),
            VMEM((7, n, 128), F32),
            VMEM((n, 128), F32),
            VMEM((4, n, 128), F32),
            VMEM((n, 128), F32),
            VMEM((3, n, 128), F32),
            VMEM((n, 128), F32),
            pltpu.SemaphoreType.DMA((3,)),
            pltpu.SemaphoreType.DMA((8,)),
            pltpu.SemaphoreType.DMA((8,)),
        ],
        compiler_params=pltpu.CompilerParams(vmem_limit_bytes=8 << 20, collective_id=0, has_side_effects=True),
        cost_estimate=cost(30 << 20),
        name="exchange",
    )(rl, cn, ud)


def derive_kernel(e_ref, xh_ref, yh_ref, mx_ref, my_ref, kx_ref, ky_ref, kl_ref, rim_ref, dx_ref, dy_ref, mxcol, myrow):
    @pl.when(pl.program_id(0) == 0)
    def _():
        gx, gy = lax.axis_index("gx"), lax.axis_index("gy")
        mxcol[...] = row_as_column(mx_ref[pl.ds(gx, 1), :])
        myrow[:, 0:128] = jnp.broadcast_to(my_ref[pl.ds(2 * gy, 1), :], (8, 128))
        myrow[:, 128:256] = jnp.broadcast_to(my_ref[pl.ds(2 * gy + 1, 1), :], (8, 128))

    each = e_ref.shape[0]
    zero = jnp.zeros((1, 256), F32)
    col = mxcol[...]
    yall = jnp.concatenate([yh_ref[i * 8 : i * 8 + 8, :] for i in range(each)], axis=1)
    high = yall.astype(BF16).astype(F32)
    stack = jnp.concatenate([high, yall - high, high, jnp.zeros_like(high)], axis=0).astype(BF16)
    extra = lax.dot_general(stack, rim_ref[...], (((0,), (0,)), ((), ())), preferred_element_type=F32)
    highs, lows = [], []
    for i in range(each):
        xall = jnp.concatenate([xh_ref[0, i * 8 : i * 8 + 8, :], xh_ref[1, i * 8 : i * 8 + 8, :]], axis=1)
        top = jnp.concatenate([xall[4:6]] + [zero] * 6, axis=0)
        low = jnp.concatenate([zero] * 7 + [xall[6:7]], axis=0)
        e = e_ref[i]
        f = jnp.concatenate([e[0:8] + top, e[8:120], e[120:128] + low], axis=0)
        f = f + extra[i * 128 : (i + 1) * 128, 256:512]
        halo = jnp.concatenate([xall[0:4]] + [zero] * 12, axis=0)
        fh, fl = split(f)
        hh, hl = split(halo)
        highs.append(fh)
        lows.append(fl)
        one = dot(kx_ref[...], jnp.concatenate([fh, hh], axis=0))
        dx = one[0:128] + one[128:256] + dot(kx_ref[0:128], jnp.concatenate([fl, hl], axis=0))
        dx_ref[i, :, 0:128] = dx[:, 0:128] * col
        dx_ref[i, :, 128:256] = dx[:, 128:256] * col
    two = dot(jnp.concatenate(highs + lows, axis=0), ky_ref[...])
    n = each * 128
    dy = two[0:n] + two[n : 2 * n] + dot(jnp.concatenate(highs, axis=0), kl_ref[...]) + extra[:, 0:256]
    dy_ref[...] = (dy * myrow[0:1, :]).reshape(dy_ref.shape)


def derive(e, xh, yh, mx, my):
    n, rows, cols = e.shape
    each = EACH
    kx = np.zeros((rows, 144))
    kx[:, 0:rows] = line_matrix(rows)
    kx[:, rows : rows + 4] = halo_columns(rows)
    kx = np.concatenate(halves(kx), axis=0)
    kh, kl = halves(line_matrix(cols).T)
    rim = np.zeros((8, 512))
    rim[0:4, 0:256] = halo_columns(cols).T
    rim[4, 256] = 1.0
    rim[5, 257] = 1.0
    rim[6, 511] = 1.0
    rh, rlow = halves(rim)
    rim = np.concatenate([rh, rh, rlow, np.zeros((8, 512), BF16)], axis=0)
    whole = lambda x: pl.BlockSpec(x.shape, lambda i: (0,) * x.ndim)
    block = pl.BlockSpec((each, rows, cols), lambda i: (i, 0, 0))
    consts = (kx, kh, kl, rim)
    xspec = pl.BlockSpec((2, each * 8, 128), lambda i: (0, i, 0))
    yspec = pl.BlockSpec((each * 8, 128), lambda i: (i, 0))
    return pl.pallas_call(
        derive_kernel,
        grid=(n // each,),
        out_shape=(jax.ShapeDtypeStruct(e.shape, F32),) * 2,
        in_specs=[block, xspec, yspec] + [whole(x) for x in (mx, my) + consts],
        out_specs=(block, block),
        scratch_shapes=[VMEM((128, 128), F32), VMEM((8, 256), F32)],
        compiler_params=pltpu.CompilerParams(vmem_limit_bytes=30 << 20),
        cost_estimate=cost(30 << 20),
        name="derive",
    )(e, xh, yh, mx, my, *consts)


def local(
    velocity, metric_x, metric_y, marker_force, marker_frac, marker_cell_x, marker_cell_y, marker_cell_z, send_counts
):
    comps, planes, rows, cols = velocity.shape
    fold = lambda x: x.reshape(-1, 128)
    cells = [fold(x) for x in (marker_cell_x, marker_cell_y, marker_cell_z)]
    outbox = pack(send_counts, marker_force, marker_frac, *cells)
    slab = lambda x: x.reshape(METRIC, 1, 256)
    inbox = shuffle(outbox, slab(metric_x), slab(metric_y)).reshape(-1, 1, 256)
    mx, my = fold(metric_x), fold(metric_y)
    e, rl, cn, ud = spread(inbox, velocity)
    xh, yh = exchange(rl, cn, ud)
    dx, dy = derive(e.reshape(comps * planes, rows, cols), xh, yh, mx, my)
    return dx.reshape(velocity.shape), dy.reshape(velocity.shape)


def solution(mesh):
    both = ("gx", "gy")
    placed = (
        P(None, None, "gx", "gy"), P(), P(), P(None, both), P(None, both), P(both), P(both), P(both), P(both, None),
    )
    return jax.shard_map(
        local,
        mesh=mesh,
        in_specs=placed,
        out_specs=(P(None, None, "gx", "gy"), P(None, None, "gx", "gy")),
        check_vma=False,
    )
```

```python
import functools
import math

import jax
import jax.numpy as jnp
import numpy as np
from jax import lax
from jax.experimental import pallas as pl
from jax.experimental.pallas import tpu as pltpu
from jax.sharding import PartitionSpec as P

SLOTS = 32
HALF = 0.5
GROUP = 42
BASES = 39
OFF = 8
XEXT = 144
PAIRS = 9
SPAN = 2 * XEXT
EACH = 12
METRIC = 8
UNROLL = 4
TOGETHER = 4
TILES = 7
COPIES = 2
ROOT = (math.sqrt(5.0) - 3.0) / 2.0
MESH = pl.DeviceIdType.MESH
VMEM = pltpu.VMEM
F32 = jnp.float32
BF16 = jnp.bfloat16


SCALE = 1.0 / (1.0 + 2.0 * ROOT / 3.0)
LEAD = SCALE * (7.0 / 9.0 * (1.0 / ROOT - ROOT) + 1.0 / 36.0 * (1.0 / ROOT**2 - ROOT**2))
NEAR = SCALE / 36.0 * (ROOT - 1.0 / ROOT)


def line_matrix(n):
    gap = np.arange(n)[None, :] - np.arange(n)[:, None]
    out = np.sign(gap) * LEAD * ROOT ** np.abs(gap).astype(np.float64)
    return out + np.where(np.abs(gap) == 1, np.sign(gap) * NEAR, 0.0)


def halo_columns(n):
    out = np.zeros((n, 4))
    steps = np.arange(n)
    out[:, 0] = -LEAD * ROOT ** (steps + 1.0)
    out[0, 1] = -NEAR
    out[:, 2] = LEAD * ROOT ** (n - steps * 1.0)
    out[n - 1, 3] = NEAR
    return out


def halves(values):
    values = np.asarray(values, np.float32)
    high = values.astype(BF16)
    low = (values - high.astype(np.float32)).astype(BF16)
    return high, low


def split(x):
    high = x.astype(BF16)
    return high, (x - high.astype(F32)).astype(BF16)


def dot(a, b):
    return jnp.dot(a, b, preferred_element_type=F32)


def cost(size):
    return pl.CostEstimate(flops=0, bytes_accessed=size, transcendentals=0)


def pack_kernel(counts_ref, force_ref, frac_ref, cx_ref, cy_ref, cz_ref, out_ref, wide):
    size = force_ref.shape[1]
    wide[0:3, 0:size] = force_ref[...]
    wide[3:6, 0:size] = frac_ref[...]
    code = ((cx_ref[...] * 256 + cy_ref[...]) * 16 + cz_ref[...]).astype(F32)
    for i in range(size // 128):
        wide[6:7, i * 128 : (i + 1) * 128] = code[i : i + 1]
    wide[7:8, 0:size] = jnp.zeros((1, size), F32)
    wide[:, size:] = jnp.zeros((8, wide.shape[1] - size), F32)
    lane = lax.broadcasted_iota(jnp.int32, (8, 128), 1)
    sub = lax.broadcasted_iota(jnp.int32, (8, 128), 0)
    part = sub & 3
    unused = jnp.where((sub == 6) & (lane < SLOTS), lane * (4 << 12), 0).astype(F32)

    def one(d, start):
        count = counts_ref[0, d]
        first = pl.multiple_of((start >> 7) << 7, 128)
        shift = start & 127
        back = (128 - shift) & 127
        a = pltpu.roll(wide[:, pl.ds(first, 128)], back, 1)
        b = pltpu.roll(wide[:, pl.ds(first + 128, 128)], back, 1)
        w = jnp.where(lane + shift < 128, a, b)
        w = jnp.where(lane < count, w, unused)
        m = w
        for j in range(1, 4):
            m = jnp.where(part == j, pltpu.roll(w, SLOTS * j, 1), m)
        top = jnp.sum(jnp.where(sub < 4, m, 0.0), axis=0, keepdims=True)
        low = jnp.sum(jnp.where(sub < 4, 0.0, m), axis=0, keepdims=True)
        return start + count, jnp.concatenate([top, low], axis=1)

    def several(g, start):
        for j in range(UNROLL):
            for k in range(8):
                start, out_ref[k, g * UNROLL + j] = one((g * UNROLL + j) * 8 + k, start)
        return start

    lax.fori_loop(0, out_ref.shape[1] // UNROLL, several, jnp.int32(0))


def pack(counts, *fields):
    vm = pl.BlockSpec(memory_space=VMEM)
    return pl.pallas_call(
        pack_kernel,
        out_shape=jax.ShapeDtypeStruct((8, counts.shape[1] // 8, 1, 256), F32),
        in_specs=[pl.BlockSpec(memory_space=pltpu.SMEM)] + [vm] * 5,
        out_specs=vm,
        scratch_shapes=[VMEM((8, fields[0].shape[1] + 256), F32)],
        cost_estimate=cost(12 << 20),
        name="pack",
    )(counts, *fields)


def shuffle_kernel(out_ref, mx_ref, my_ref, in_ref, mid, own_sems, send_y, recv_y, send_x, recv_x):
    gx, gy = lax.axis_index("gx"), lax.axis_index("gy")
    nx, ny = lax.axis_size("gx"), lax.axis_size("gy")
    own = pltpu.make_async_copy(out_ref.at[gy], mid.at[gy], own_sems.at[0])
    own.start()
    metrics = [
        pltpu.make_async_copy(src, in_ref.at[nx + i], own_sems.at[2 + i]) for i, src in enumerate((mx_ref, my_ref))
    ]
    for copy in metrics:
        copy.start()
    barrier = pltpu.get_barrier_semaphore()
    for k in range(1, ny):
        pl.semaphore_signal(barrier, inc=1, device_id=(gx, lax.rem(gy + k, ny)), device_id_type=MESH)
    for k in range(1, nx):
        pl.semaphore_signal(barrier, inc=1, device_id=(lax.rem(gx + k, nx), gy), device_id_type=MESH)
    pl.semaphore_wait(barrier, nx + ny - 2)
    copies = []
    for k in range(1, ny):
        peer = lax.rem(gy + k, ny)
        copy = pltpu.make_async_remote_copy(
            src_ref=out_ref.at[peer], dst_ref=mid.at[gy], send_sem=send_y.at[k], recv_sem=recv_y.at[k],
            device_id=(gx, peer), device_id_type=MESH,
        )
        copy.start()
        copies.append(copy)
    own.wait()
    for copy in copies:
        copy.wait()
    own = pltpu.make_async_copy(mid.at[:, gx], in_ref.at[gx], own_sems.at[1])
    own.start()
    copies = []
    for k in range(1, nx):
        peer = lax.rem(gx + k, nx)
        copy = pltpu.make_async_remote_copy(
            src_ref=mid.at[:, peer], dst_ref=in_ref.at[gx], send_sem=send_x.at[k], recv_sem=recv_x.at[k],
            device_id=(peer, gy), device_id_type=MESH,
        )
        copy.start()
        copies.append(copy)
    own.wait()
    for copy in copies + metrics:
        copy.wait()


def shuffle(outbox, mx, my):
    ny, nx = outbox.shape[0:2]
    anywhere = pl.BlockSpec(memory_space=pl.ANY)
    dma = pltpu.SemaphoreType.DMA
    return pl.pallas_call(
        shuffle_kernel,
        out_shape=jax.ShapeDtypeStruct((nx + 2, ny, 1, 256), F32),
        in_specs=[anywhere] * 3,
        out_specs=anywhere,
        scratch_shapes=[VMEM((ny, nx, 1, 256), F32), dma((4,)), dma((ny,)), dma((ny,)), dma((nx,)), dma((nx,))],
        compiler_params=pltpu.CompilerParams(collective_id=1, has_side_effects=True),
        cost_estimate=cost(36 << 20),
        name="shuffle",
    )(outbox, mx, my)


def row_as_column(row):
    return jnp.transpose(jnp.broadcast_to(row, (128, 128)))


def stencil_weights(t):
    root = jnp.sqrt(jnp.maximum(1.0 + 4.0 * t - 4.0 * t * t, 0.0))
    return (
        (3.0 - 2.0 * t - root) / 8.0,
        (3.0 - 2.0 * t + root) / 8.0,
        (1.0 + 2.0 * t + root) / 8.0,
        (1.0 + 2.0 * t - root) / 8.0,
    )


def powers(steps):
    size = jnp.exp(steps.astype(F32) * math.log(-ROOT))
    return jnp.where((steps & 1) == 1, -size, size)


def edge_table(n, kinds, spots):
    inside = (spots >= 0) & (spots < n)
    steps = jnp.where(kinds == 0, n - 1 - spots, spots)
    sums = jnp.where(inside & ((kinds == 0) | (kinds == 4)), powers(jnp.where(inside, steps, 0)), 0.0)
    only = jnp.where(kinds < 4, n - 2 + kinds, jnp.where(kinds == 5, 0, n + 127))
    single = (kinds != 0) & (kinds != 4) & (kinds < 7) & (spots == only)
    return jnp.where(single, 1.0, sums)


def spread_kernel(
    inbox_ref, v_hbm,
    e_hbm, rl_ref, cn_ref, ud_ref,
    *scratch,
):
    grids = scratch[:COPIES]
    vbuf, m8, base_v, base_s, mxcol, wfar_ref, wnear_ref, pick_ref, ext, rlp, udp, v_sem, e_sems, s_sem = scratch[COPIES:]
    gx, gy = lax.axis_index("gx"), lax.axis_index("gy")
    messages = inbox_ref.shape[0] - 2 * METRIC
    chunks = messages * SLOTS // 128
    vin = pltpu.make_async_copy(v_hbm, vbuf, v_sem)
    vin.start()
    lane = lax.broadcasted_iota(jnp.int32, (8, 128), 1)
    sub = lax.broadcasted_iota(jnp.int32, (8, 128), 0)

    def regroup(g):
        out = None
        for k in range(4):
            row = inbox_ref[g * 4 + k]
            x = jnp.where(
                sub < 4, jnp.broadcast_to(row[:, 0:128], (8, 128)), jnp.broadcast_to(row[:, 128:256], (8, 128))
            )
            y = x
            for j in range(4):
                turn = (SLOTS * (k - j)) % 128
                z = pltpu.roll(x, turn, 1) if turn else x
                y = jnp.where((sub & 3) == j, z, y)
            out = y if out is None else jnp.where((lane >> 5) == k, y, out)
        at = g * 128 if isinstance(g, int) else pl.multiple_of(g * 128, 128)
        m8[:, pl.ds(at, 128)] = out
        code = out[6:7].astype(jnp.int32)
        tile = (((code >> 4) & 255) * 1681) >> 16
        pair = (2 * tile + (code & 1)) * PAIRS + ((code & 15) >> 1)
        base_v[:, pl.ds(at, 128)] = pair * SPAN + 2 * ((code >> 12) + OFF - 1)

    rows = grids[0].shape[0]
    share = 8 * (-(-rows // (8 * chunks)))
    full = rows // share

    def regroup_and_clear(g, carry):
        for grid in grids:
            grid[pl.ds(pl.multiple_of(g * share, 8), share), :] = jnp.zeros((share, 128), F32)
        regroup(g)
        return carry

    lax.fori_loop(0, full, regroup_and_clear, 0)
    for grid in grids:
        if full * share < rows:
            grid[full * share : rows, :] = jnp.zeros((rows - full * share, 128), F32)
    for g in range(full, chunks):
        regroup(g)
    bcopy = pltpu.make_async_copy(base_v, base_s, s_sem)
    bcopy.start()
    bcopy.wait()

    sub2 = lax.broadcasted_iota(jnp.int32, (128, 128), 0)
    comp = jnp.where(sub2 >= 2 * GROUP, 2, jnp.where(sub2 >= GROUP, 1, 0))
    rel = jnp.where(sub2 >= 3 * GROUP, -100, sub2 - GROUP * comp)

    def tables(c):
        m = m8[:, pl.ds(pl.multiple_of(c * 128, 128), 128)]
        ws = stencil_weights(m)
        code = m[6:7].astype(jnp.int32)
        cell_y = (code >> 4) & 255
        inner = cell_y - BASES * ((cell_y * 1681) >> 16)
        d = rel - inner
        w = jnp.where(d == 0, ws[0][4:5], 0.0)
        w = jnp.where(d == 1, ws[1][4:5], w)
        w = jnp.where(d == 2, ws[2][4:5], w)
        w = jnp.where(d == 3, ws[3][4:5], w)
        f = jnp.where(comp == 0, m[0:1], jnp.where(comp == 1, m[1:2], m[2:3]))
        wx8 = jnp.concatenate([ws[i // 2][3:4] for i in range(8)], axis=0)
        sides = ((ws[0][5:6], ws[1][5:6]), (ws[2][5:6], ws[3][5:6]))
        tall = [wx8 * jnp.concatenate(list(side) * 4, axis=0) for side in sides]
        return jnp.transpose(w * f), tall

    def chunk(i, carry):
        built = [tables(i * TOGETHER + j) for j in range(TOGETHER)]
        for j, (fr, tall) in enumerate(built):
            bs = [base_s[0, (i * TOGETHER + j) * 128 + k] for k in range(128)]
            for k0 in range(0, 128, COPIES):
                group = []
                for k in range(k0, k0 + COPIES):
                    grid = grids[k % COPIES]
                    for q in range(2):
                        at = bs[k] + q * SPAN
                        group.append((grid, at, grid[pl.ds(at, 8), :] + tall[q][:, k : k + 1] * fr[k : k + 1, :]))
                for grid, at, value in group:
                    grid[pl.ds(at, 8), :] = value
        return carry

    lax.fori_loop(0, chunks // TOGETHER, chunk, 0)

    def spots(t, e, odds=(0, 1)):
        return [(2 * t + odd) * PAIRS * SPAN + ((e - odd) >> 1) * SPAN + ((e - odd) & 1) for odd in odds]

    for t in range(TILES):
        for src, odds, dst in ((0, (0,), 16), (17, (0, 1), 1), (18, (1,), 2)):
            moved = None
            for grid in grids:
                for at in spots(t, src, odds):
                    x = grid[pl.ds(at, XEXT, stride=2), :]
                    moved = x if moved is None else moved + x
            here = pl.ds(spots(t, dst)[0], XEXT, stride=2)
            grids[0][here, :] = grids[0][here, :] + moved

    def along_x(i):
        i = lax.rem(i, 2 * METRIC)
        pair = inbox_ref[messages + (i >> 1)]
        return row_as_column(jnp.where((i & 1) == 1, pair[:, 128:256], pair[:, 0:128]))

    def along_y(i):
        return inbox_ref[messages + METRIC + lax.rem(i, METRIC)]

    mxcol[0:OFF, :] = along_x(gx + 2 * METRIC - 1)[128 - OFF : 128]
    mxcol[OFF : OFF + 128, :] = along_x(gx)
    mxcol[OFF + 128 : XEXT, :] = along_x(gx + 1)[0 : XEXT - OFF - 128]
    after = along_y(gy + 1)[:, 0:128]
    before = along_y(gy + METRIC - 1)[:, 128:256]
    here = along_y(gy)
    lane1 = lax.broadcasted_iota(jnp.int32, (1, 128), 1)
    rim = jnp.where(lane1 < 2, after, jnp.where(lane1 == 127, before, 0.0))
    mys = [HALF * here[:, 0:128], HALF * here[:, 128:256], HALF * rim]
    at = lax.broadcasted_iota(jnp.int32, (XEXT, 128), 0) - OFF
    wfar_ref[...] = edge_table(128, 0, at)
    wnear_ref[...] = edge_table(128, 4, at)
    kinds = lax.broadcasted_iota(jnp.int32, (8, 384), 0)
    high, low = split(edge_table(256, kinds, lax.broadcasted_iota(jnp.int32, (8, 384), 1)))
    pick_ref[...] = jnp.concatenate([high.astype(F32), low.astype(F32)], axis=0).astype(BF16)
    vin.wait()

    part = 48
    lanes = lax.broadcasted_iota(jnp.int32, (part, 128), 1)

    def moves(h):
        out = [(6, 0, 2), (0, 127, 128)] if h == 2 else []
        for t in range(TILES):
            low, high = BASES * t - 1 - 128 * h, BASES * t - 1 + GROUP - 128 * h
            if h < 2 and high > 0 and low < 128:
                out.append((t, max(low, 0), min(high, 128)))
        return out

    def plane(z, carry):
        far = [[jnp.zeros((8, 128), F32)] * 3 for _ in range(3)]
        near = [[jnp.zeros((8, 128), F32)] * 3 for _ in range(3)]
        for r0 in range(0, XEXT, part):
            tiles = []
            for t in range(TILES):
                x = None
                for grid in grids:
                    for at in spots(t, z + 1):
                        y = grid[pl.ds(at + 2 * r0, part, stride=2), :]
                        x = y if x is None else x + y
                tiles.append(x)
            mcol = mxcol[r0 : r0 + part, :]
            wf, wn = wfar_ref[r0 : r0 + part, :], wnear_ref[r0 : r0 + part, :]
            r1 = r0 + part
            i0, i1 = max(r0, OFF), min(r1, OFF + 128)
            for c in range(3):
                turned = [pltpu.roll(tiles[t], (BASES * t - 1 - GROUP * c) % 128, 1) for t in range(TILES)]
                for h in range(3):
                    e = None
                    for t, low, high in moves(h):
                        x = turned[t]
                        if low > 0 or high < 128:
                            x = jnp.where((lanes >= low) & (lanes < high), x, 0.0)
                        e = x if e is None else e + x
                    e = e * mcol * mys[h]
                    if h < 2:
                        cols = slice(h * 128, (h + 1) * 128)
                        inner = e[i0 - r0 : i1 - r0] + vbuf[c, z, i0 - OFF : i1 - OFF, cols]
                        vbuf[c, z, i0 - OFF : i1 - OFF, cols] = inner
                        pieces = [e[0 : i0 - r0]] if i0 > r0 else []
                        pieces.append(inner)
                        if i1 < r1:
                            pieces.append(e[i1 - r0 :])
                        e = jnp.concatenate(pieces, axis=0) if len(pieces) > 1 else inner
                    ext[c, h, r0:r1, :] = e
                    far[c][h] = far[c][h] + jnp.sum((e * wf).reshape(part // 8, 8, 128), axis=0)
                    near[c][h] = near[c][h] + jnp.sum((e * wn).reshape(part // 8, 8, 128), axis=0)
        for c in range(3):
            p = c * 16 + z
            at = pl.multiple_of(p * 8, 8)
            for h in range(3):
                rowset = [
                    jnp.sum(far[c][h], axis=0, keepdims=True),
                    ext[c, h, OFF + 127 : OFF + 130, :],
                    jnp.sum(near[c][h], axis=0, keepdims=True),
                    ext[c, h, OFF : OFF + 1, :],
                    ext[c, h, OFF - 1 : OFF, :],
                    jnp.zeros((1, 128), F32),
                ]
                rlp[h, pl.ds(at, 8), :] = jnp.concatenate(rowset, axis=0)
            high, low = split(jnp.concatenate([ext[c, h, OFF : OFF + 128, :] for h in range(3)], axis=1))
            nt = (((1,), (1,)), ((), ()))
            one = lax.dot_general(pick_ref[...], high, nt, preferred_element_type=F32)
            two = lax.dot_general(pick_ref[...], low, nt, preferred_element_type=F32)
            udp[pl.ds(at, 8), :] = one[0:8] + one[8:16] + two[0:8]
        pltpu.make_async_copy(vbuf.at[:, z], e_hbm.at[:, z], e_sems.at[z]).start()
        return carry

    def some_planes(i, carry):
        for j in range(4):
            carry = plane(4 * i + j, carry)
        return carry

    lax.fori_loop(0, 4, some_planes, 0)

    corner = jnp.zeros((48, 128), F32)
    kinds = jnp.minimum(lax.broadcasted_iota(jnp.int32, (384, 128), 1), 7)
    tail = edge_table(256, kinds, lax.broadcasted_iota(jnp.int32, (384, 128), 0))
    lines = []
    for t in range(7):
        row = jnp.concatenate([rlp[h, pl.ds(t, 48, stride=8), :] for h in range(3)], axis=1)
        rl_ref[t] = row[:, 0:256]
        ud_ref[t] = udp[pl.ds(t, 48, stride=8), :]
        lines.append(row)
    lines = jnp.concatenate(lines, axis=0)
    ends = jnp.dot(lines, tail, preferred_element_type=F32, precision=lax.Precision.HIGHEST)
    for t in range(7):
        end = ends[t * 48 : (t + 1) * 48]
        corner = corner + (pltpu.roll(end, 8 * t, 1) if t else end)
    rl_ref[7] = jnp.zeros((48, 256), F32)
    ud_ref[7] = jnp.zeros((48, 128), F32)
    cn_ref[...] = corner
    for z in range(16):
        pltpu.make_async_copy(vbuf.at[:, z], e_hbm.at[:, z], e_sems.at[z]).wait()


def spread(inbox, v):
    rows = TILES * 2 * PAIRS * SPAN + 8
    total = (inbox.shape[0] - 2 * METRIC) * SLOTS
    vm = pl.BlockSpec(memory_space=VMEM)
    return pl.pallas_call(
        spread_kernel,
        out_shape=(
            jax.ShapeDtypeStruct(v.shape, F32),
            jax.ShapeDtypeStruct((8, 48, 256), F32),
            jax.ShapeDtypeStruct((48, 128), F32),
            jax.ShapeDtypeStruct((8, 48, 128), F32),
        ),
        in_specs=[vm] + [pl.BlockSpec(memory_space=pl.ANY)],
        out_specs=(pl.BlockSpec(memory_space=pl.ANY), vm, vm, vm),
        scratch_shapes=[VMEM((rows, 128), F32)] * COPIES
        + [
            VMEM(v.shape, F32),
            VMEM((8, total), F32),
            VMEM((1, total), jnp.int32),
            pltpu.SMEM((1, total), jnp.int32),
            VMEM((XEXT, 128), F32),
            VMEM((XEXT, 128), F32),
            VMEM((XEXT, 128), F32),
            VMEM((16, 384), BF16),
            VMEM((3, 3, XEXT, 128), F32),
            VMEM((3, 48 * 8, 128), F32),
            VMEM((48 * 8, 128), F32),
            pltpu.SemaphoreType.DMA,
            pltpu.SemaphoreType.DMA((16,)),
            pltpu.SemaphoreType.DMA,
        ],
        compiler_params=pltpu.CompilerParams(vmem_limit_bytes=47616 << 10),
        cost_estimate=cost(100 << 20),
        name="spread",
    )(inbox, v)


def exchange_kernel(
    rl_hbm, cn_hbm, ud_hbm, xh_ref, yh_ref, rl_ref, cn_ref, ud_ref,
    ra, ca, rb, cb, umsg, hmsg, pu, ph, qd, qh, own_sems, send_sems, recv_sems,
):
    pairs = ((cn_hbm, cn_ref), (ud_hbm, ud_ref), (rl_hbm, rl_ref))
    loads = [pltpu.make_async_copy(src, dst, own_sems.at[i]) for i, (src, dst) in enumerate(pairs)]
    for load in loads:
        load.start()
    gx, gy = lax.axis_index("gx"), lax.axis_index("gy")
    nx, ny = lax.axis_size("gx"), lax.axis_size("gy")
    right = (lax.rem(gx + 1, nx), gy)
    left = (lax.rem(gx + nx - 1, nx), gy)
    up = (gx, lax.rem(gy + 1, ny))
    down = (gx, lax.rem(gy + ny - 1, ny))
    barrier = pltpu.get_barrier_semaphore()
    for device in (right, left, up, down):
        pl.semaphore_signal(barrier, inc=1, device_id=device, device_id_type=MESH)
    pl.semaphore_wait(barrier, 4)

    def send(i, src, dst, device):
        copy = pltpu.make_async_remote_copy(
            src_ref=src, dst_ref=dst, send_sem=send_sems.at[i], recv_sem=recv_sems.at[i],
            device_id=device, device_id_type=MESH,
        )
        copy.start()
        return copy

    first = [
        send(0, cn_hbm, ca, right),
        send(1, cn_hbm, cb, left),
        send(2, rl_hbm.at[0:4], ra, right),
        send(3, rl_hbm.at[4:7], rb, left),
    ]
    planes = cn_ref.shape[0]
    lane = lax.broadcasted_iota(jnp.int32, (planes, 128), 1)
    for load in loads:
        load.wait()
    first[0].wait()
    first[1].wait()
    own, a, b = cn_ref[...], ca[...], cb[...]
    turn = lambda x, by: pltpu.roll(x, by % 128, 1)
    hold = jnp.where(lane < 8, a + turn(own, -48), a + turn(own, -40))
    hold = jnp.where(
        lane < 16, hold, turn(b, -16) + jnp.where(lane < 24, own + ROOT * turn(own, -8), turn(own, 8))
    )
    hmsg[...] = jnp.where(lane < 32, hold, 0.0)
    for s in range(7):
        umsg[s] = (
            ud_ref[s]
            + jnp.where(lane == 0, a[:, 16 + s : 17 + s], 0.0)
            + jnp.where(lane == 1, a[:, 24 + s : 25 + s], 0.0)
            + jnp.where(lane == 127, b[:, 48 + s : 49 + s], 0.0)
        )
    second = [
        send(4, hmsg, ph, up),
        send(5, hmsg, qh, down),
        send(6, umsg.at[0:4], pu, up),
        send(7, umsg.at[4:7], qd, down),
    ]
    first[2].wait()
    first[3].wait()
    second[0].wait()
    second[1].wait()
    lane = lax.broadcasted_iota(jnp.int32, (planes, 256), 1)
    p, q = ph[...], qh[...]

    def rims(h):
        return (
            jnp.where(lane == 0, p[:, 8 * h + 2 : 8 * h + 3], 0.0)
            + jnp.where(lane == 1, p[:, 8 * h + 3 : 8 * h + 4], 0.0)
            + jnp.where(lane == 255, q[:, 8 * h + 6 : 8 * h + 7], 0.0)
        )

    def put(t, value):
        for h in range(2):
            xh_ref[h, pl.ds(t, planes, stride=8), :] = value[:, h * 128 : (h + 1) * 128]

    put(0, ra[0] + rl_ref[6] + rims(0))
    put(1, ra[1] + rl_ref[6] + rims(1))
    put(2, rb[0] + rl_ref[2] + ROOT * rl_ref[3] + rims(2))
    put(3, rb[1] + rl_ref[2] + rims(3))
    put(4, ra[2])
    put(5, ra[3])
    put(6, rb[2])
    put(7, jnp.zeros((planes, 256), F32))
    second[2].wait()
    second[3].wait()
    yh_ref[pl.ds(0, planes, stride=8), :] = pu[0] + umsg[6]
    yh_ref[pl.ds(1, planes, stride=8), :] = pu[1] + umsg[6]
    yh_ref[pl.ds(2, planes, stride=8), :] = qd[0] + umsg[2] + ROOT * umsg[3]
    yh_ref[pl.ds(3, planes, stride=8), :] = qd[1] + umsg[2]
    yh_ref[pl.ds(4, planes, stride=8), :] = pu[2]
    yh_ref[pl.ds(5, planes, stride=8), :] = pu[3]
    yh_ref[pl.ds(6, planes, stride=8), :] = qd[2]
    yh_ref[pl.ds(7, planes, stride=8), :] = jnp.zeros((planes, 128), F32)


def exchange(rl, cn, ud):
    n = cn.shape[0]
    vm = pl.BlockSpec(memory_space=VMEM)
    return pl.pallas_call(
        exchange_kernel,
        out_shape=(jax.ShapeDtypeStruct((2, 8 * n, 128), F32), jax.ShapeDtypeStruct((8 * n, 128), F32)),
        in_specs=[pl.BlockSpec(memory_space=pl.ANY)] * 3,
        out_specs=(vm, vm),
        scratch_shapes=[
            VMEM((8, n, 256), F32),
            VMEM((n, 128), F32),
            VMEM((8, n, 128), F32),
            VMEM((4, n, 256), F32),
            VMEM((n, 128), F32),
            VMEM((3, n, 256), F32),
            VMEM((n, 128), F32),
            VMEM((7, n, 128), F32),
            VMEM((n, 128), F32),
            VMEM((4, n, 128), F32),
            VMEM((n, 128), F32),
            VMEM((3, n, 128), F32),
            VMEM((n, 128), F32),
            pltpu.SemaphoreType.DMA((3,)),
            pltpu.SemaphoreType.DMA((8,)),
            pltpu.SemaphoreType.DMA((8,)),
        ],
        compiler_params=pltpu.CompilerParams(vmem_limit_bytes=8 << 20, collective_id=0, has_side_effects=True),
        cost_estimate=cost(30 << 20),
        name="exchange",
    )(rl, cn, ud)


def derive_kernel(e_ref, xh_ref, yh_ref, mx_ref, my_ref, kx_ref, ky_ref, kl_ref, rim_ref, dx_ref, dy_ref, mxcol, myrow):
    @pl.when(pl.program_id(0) == 0)
    def _():
        gx, gy = lax.axis_index("gx"), lax.axis_index("gy")
        mxcol[...] = row_as_column(mx_ref[pl.ds(gx, 1), :])
        myrow[:, 0:128] = jnp.broadcast_to(my_ref[pl.ds(2 * gy, 1), :], (8, 128))
        myrow[:, 128:256] = jnp.broadcast_to(my_ref[pl.ds(2 * gy + 1, 1), :], (8, 128))

    each = e_ref.shape[0]
    zero = jnp.zeros((1, 256), F32)
    col = mxcol[...]
    yall = jnp.concatenate([yh_ref[i * 8 : i * 8 + 8, :] for i in range(each)], axis=1)
    high = yall.astype(BF16).astype(F32)
    stack = jnp.concatenate([high, yall - high, high, jnp.zeros_like(high)], axis=0).astype(BF16)
    extra = lax.dot_general(stack, rim_ref[...], (((0,), (0,)), ((), ())), preferred_element_type=F32)
    highs, lows = [], []
    for i in range(each):
        xall = jnp.concatenate([xh_ref[0, i * 8 : i * 8 + 8, :], xh_ref[1, i * 8 : i * 8 + 8, :]], axis=1)
        top = jnp.concatenate([xall[4:6]] + [zero] * 6, axis=0)
        low = jnp.concatenate([zero] * 7 + [xall[6:7]], axis=0)
        e = e_ref[i]
        f = jnp.concatenate([e[0:8] + top, e[8:120], e[120:128] + low], axis=0)
        f = f + extra[i * 128 : (i + 1) * 128, 256:512]
        halo = jnp.concatenate([xall[0:4]] + [zero] * 12, axis=0)
        fh, fl = split(f)
        hh, hl = split(halo)
        highs.append(fh)
        lows.append(fl)
        one = dot(kx_ref[...], jnp.concatenate([fh, hh], axis=0))
        dx = one[0:128] + one[128:256] + dot(kx_ref[0:128], jnp.concatenate([fl, hl], axis=0))
        dx_ref[i, :, 0:128] = dx[:, 0:128] * col
        dx_ref[i, :, 128:256] = dx[:, 128:256] * col
    two = dot(jnp.concatenate(highs + lows, axis=0), ky_ref[...])
    n = each * 128
    dy = two[0:n] + two[n : 2 * n] + dot(jnp.concatenate(highs, axis=0), kl_ref[...]) + extra[:, 0:256]
    dy_ref[...] = (dy * myrow[0:1, :]).reshape(dy_ref.shape)


def derive(e, xh, yh, mx, my):
    n, rows, cols = e.shape
    each = EACH
    kx = np.zeros((rows, 144))
    kx[:, 0:rows] = line_matrix(rows)
    kx[:, rows : rows + 4] = halo_columns(rows)
    kx = np.concatenate(halves(kx), axis=0)
    kh, kl = halves(line_matrix(cols).T)
    rim = np.zeros((8, 512))
    rim[0:4, 0:256] = halo_columns(cols).T
    rim[4, 256] = 1.0
    rim[5, 257] = 1.0
    rim[6, 511] = 1.0
    rh, rlow = halves(rim)
    rim = np.concatenate([rh, rh, rlow, np.zeros((8, 512), BF16)], axis=0)
    whole = lambda x: pl.BlockSpec(x.shape, lambda i: (0,) * x.ndim)
    block = pl.BlockSpec((each, rows, cols), lambda i: (i, 0, 0))
    consts = (kx, kh, kl, rim)
    xspec = pl.BlockSpec((2, each * 8, 128), lambda i: (0, i, 0))
    yspec = pl.BlockSpec((each * 8, 128), lambda i: (i, 0))
    return pl.pallas_call(
        derive_kernel,
        grid=(n // each,),
        out_shape=(jax.ShapeDtypeStruct(e.shape, F32),) * 2,
        in_specs=[block, xspec, yspec] + [whole(x) for x in (mx, my) + consts],
        out_specs=(block, block),
        scratch_shapes=[VMEM((128, 128), F32), VMEM((8, 256), F32)],
        compiler_params=pltpu.CompilerParams(vmem_limit_bytes=30 << 20),
        cost_estimate=cost(30 << 20),
        name="derive",
    )(e, xh, yh, mx, my, *consts)


def local(
    velocity, metric_x, metric_y, marker_force, marker_frac, marker_cell_x, marker_cell_y, marker_cell_z, send_counts
):
    comps, planes, rows, cols = velocity.shape
    fold = lambda x: x.reshape(-1, 128)
    cells = [fold(x) for x in (marker_cell_x, marker_cell_y, marker_cell_z)]
    outbox = pack(send_counts, marker_force, marker_frac, *cells)
    slab = lambda x: x.reshape(METRIC, 1, 256)
    inbox = shuffle(outbox, slab(metric_x), slab(metric_y)).reshape(-1, 1, 256)
    mx, my = fold(metric_x), fold(metric_y)
    e, rl, cn, ud = spread(inbox, velocity)
    xh, yh = exchange(rl, cn, ud)
    dx, dy = derive(e.reshape(comps * planes, rows, cols), xh, yh, mx, my)
    return dx.reshape(velocity.shape), dy.reshape(velocity.shape)


def solution(mesh):
    both = ("gx", "gy")
    placed = (
        P(None, None, "gx", "gy"), P(), P(), P(None, both), P(None, both), P(both), P(both), P(both), P(both, None),
    )
    return jax.shard_map(
        local,
        mesh=mesh,
        in_specs=placed,
        out_specs=(P(None, None, "gx", "gy"), P(None, None, "gx", "gy")),
        check_vma=False,
    )
```
